256 devices in a mesh: row: 16 (over z, core), col: 16 (over y, x).
Axes of the slice: x: 4, y: 4, z: 8, core: 2. Of those that a mesh axis runs over, the one named last changes fastest.
Arguments:
- matrix: float32 [8192, 8192], P('row', 'col'), as said below
Outputs:
- reduced: float32 [8192, 8192], P('row', 'col')
Inputs may be any that keep to these rules, and one draw needn't show every extreme that they name: matrix is symmetric.
All inputs are finite; a program needn't handle non-finite values.
Results may differ from the reference program's by a relative error of at most 0.00014.
Values sent between devices are 32-bit elements; how exact they have to be, the bound alone decides.
A program may use at most 64 MiB of HBM per device.

```python
import jax
import jax.numpy as jnp
from jax import lax

ORDER = 8192
BLOCK = 256
PANELS = 2


def draw_matrix(key, part):
    base = jax.random.normal(key, (ORDER, ORDER), jnp.float32)
    symmetric = (base + base.T) * 0.7071
    return symmetric


def setup_inputs(seed: int = 0) -> dict:
    keys = jax.random.split(jax.random.key(seed), 2)
    return {
        "matrix": draw_matrix(jax.random.fold_in(keys[1], 71), 0),
    }


HIGH = lax.Precision.HIGHEST

def mult(left, right):
    return jnp.dot(left.astype(jnp.float32), right.astype(jnp.float32), precision=HIGH, preferred_element_type=jnp.float32)

def inverse_transposed(shifted):
    factor = jnp.linalg.cholesky(mult(shifted, shifted.T))
    half = jax.scipy.linalg.solve_triangular(factor, shifted, lower=True)
    return jax.scipy.linalg.solve_triangular(factor, half, lower=True, trans='T')

def reflect(current, index):
    lead = (index + 1) * BLOCK
    rows = jnp.arange(ORDER, dtype=jnp.int32)
    panel = jnp.where((rows >= lead)[:, None], current[:, index * BLOCK:(index + 1) * BLOCK], jnp.float32(0.0))
    gram = mult(panel.T, panel)
    lower = jnp.linalg.cholesky(gram)
    basis = jax.scipy.linalg.solve_triangular(lower, panel.T, lower=True).T
    top = basis[lead:lead + BLOCK]
    kernel = inverse_transposed(jnp.eye(BLOCK, dtype=jnp.float32) + top)
    unit = ((rows - lead)[:, None] == jnp.arange(BLOCK, dtype=jnp.int32)[None, :]).astype(jnp.float32)
    vectors = basis + unit
    product = mult(current, vectors)
    inner = mult(vectors.T, product)
    coupled = mult(kernel.T, mult(inner, kernel))
    update = mult(product, kernel) - 0.5 * mult(vectors, coupled)
    return current - mult(update, vectors.T) - mult(vectors, update.T)

def reference(matrix):
    current = matrix
    for index in range(PANELS):
        current = reflect(current, index)
    return current
```

```python
import functools

import jax
import jax.numpy as jnp
from jax import lax
from jax.experimental import pallas as pl
from jax.experimental.pallas import tpu as pltpu
from jax.sharding import PartitionSpec as P

BLOCK = 256
PANELS = 2
N = 16
NZ = 8
HIGH = lax.Precision.HIGHEST
F32 = jnp.float32
MESH = pl.DeviceIdType.MESH
VMEM = pl.BlockSpec(memory_space=pltpu.VMEM)


def dot(left, right, over=(1, 0)):
    return lax.dot_general(
        left,
        right,
        (((over[0],), (over[1],)), ((), ())),
        precision=HIGH,
        preferred_element_type=F32,
    )


def sweep(aug, jj, inverse):
    base = pl.multiple_of(8 * jj, 8)
    sub = lax.broadcasted_iota(jnp.int32, (8, 128), 0)
    sub2 = lax.broadcasted_iota(jnp.int32, (8, 256), 0)

    def lane(block, s):
        index = jnp.full((8, 128), base + s, jnp.int32)
        return jnp.take_along_axis(block, index, axis=1)

    group = aug[pl.ds(base, 8), :]
    cols = [lane(group[:, :128], s) for s in range(8)]
    kept = group
    for s in range(8):
        pivot = jnp.broadcast_to(cols[s][s : s + 1], (8, 128))
        inv = 1.0 / pivot
        inv2 = jnp.concatenate([inv, inv], axis=1)
        row = jnp.broadcast_to(group[s : s + 1], (8, 256))
        if not inverse:
            scale = lax.rsqrt(pivot)
            kept = jnp.where(sub2 == s, row * jnp.concatenate([scale, scale], axis=1), kept)
        new = row * inv2
        f = cols[s]
        f2 = jnp.concatenate([f, f], axis=1)
        group = jnp.where(sub2 == s, new, group - f2 * new)
        for t in range(s + 1, 8):
            crow = jnp.broadcast_to(cols[t][s : s + 1], (8, 128)) * inv
            cols[t] = jnp.where(sub == s, crow, cols[t] - f * crow)
    aug[pl.ds(base, 8), :] = group if inverse else kept
    rows = [jnp.broadcast_to(group[s : s + 1], (8, 256)) for s in range(8)]
    for g in range(16):
        block = aug[8 * g : 8 * g + 8, :]
        keep = (g != jj) if inverse else (g > jj)
        new = block
        for s in range(8):
            c = lane(block[:, :128], s)
            new = new - jnp.concatenate([c, c], axis=1) * rows[s]
        aug[8 * g : 8 * g + 8, :] = jnp.where(keep, new, block)


def factor_kernel(t_ref, lt_ref, k_ref, aug):
    eye = (
        lax.broadcasted_iota(jnp.int32, (128, 128), 0)
        == lax.broadcasted_iota(jnp.int32, (128, 128), 1)
    ).astype(F32)
    upper = lax.broadcasted_iota(jnp.int32, (128, 128), 0) <= lax.broadcasted_iota(
        jnp.int32, (128, 128), 1
    )

    def run(block, inverse):
        aug[:, :128] = block
        aug[:, 128:] = eye
        lax.fori_loop(0, 16, lambda jj, _: (sweep(aug, jj, inverse), 0)[1], 0)

    gram = t_ref[0]
    run(gram[:128, :128], False)
    lt00 = jnp.where(upper, aug[:, :128], 0.0)
    lt01 = dot(aug[:, 128:], gram[:128, 128:])
    run(gram[128:, 128:] - dot(lt01, lt01, (0, 0)), False)
    lt_ref[:128, :128] = lt00
    lt_ref[:128, 128:] = lt01
    lt_ref[128:, :128] = jnp.zeros((128, 128), F32)
    lt_ref[128:, 128:] = jnp.where(upper, aug[:, :128], 0.0)
    n = gram + dot(t_ref[1], lt_ref[...], (0, 0))
    run(n[:128, :128], True)
    d0 = aug[:, 128:]
    n01 = dot(d0, n[:128, 128:])
    q = dot(n[128:, :128], d0)
    run(n[128:, 128:] - dot(n[128:, :128], n01), True)
    e = aug[:, 128:]
    k10 = -dot(e, q)
    k_ref[:128, :128] = d0 - dot(n01, k10)
    k_ref[:128, 128:] = -dot(n01, e)
    k_ref[128:, :128] = k10
    k_ref[128:, 128:] = e


def factor(t):
    shape = jax.ShapeDtypeStruct((256, 256), F32)
    return pl.pallas_call(
        factor_kernel,
        out_shape=(shape, shape),
        in_specs=[VMEM],
        out_specs=(VMEM, VMEM),
        scratch_shapes=[pltpu.VMEM((128, 256), F32)],
    )(t)


def remote(src, dst, send, recv, row, col):
    return pltpu.make_async_remote_copy(
        src_ref=src,
        dst_ref=dst,
        send_sem=send,
        recv_sem=recv,
        device_id=(row, col),
        device_id_type=MESH,
    )


def place():
    r, c = lax.axis_index("row"), lax.axis_index("col")
    return r, c, r // 2, lax.rem(r, 2)


def greet(r, c):
    barrier = pltpu.get_barrier_semaphore()
    for k in range(1, N):
        pl.semaphore_signal(barrier, inc=1, device_id=(r, lax.rem(c + k, N)), device_id_type=MESH)
        pl.semaphore_signal(barrier, inc=1, device_id=(lax.rem(r + k, N), c), device_id_type=MESH)
    pl.semaphore_wait(barrier, 2 * (N - 1))


def piece(ref, index, size):
    return ref.at[pl.ds(pl.multiple_of(index * size, size), size)]


SLOT_SEMS = [
    pltpu.SemaphoreType.DMA((2,)),
    pltpu.SemaphoreType.DMA((NZ,)),
    pltpu.SemaphoreType.DMA((NZ,)),
    pltpu.SemaphoreType.DMA((N,)),
    pltpu.SemaphoreType.DMA((N,)),
    pltpu.SemaphoreType.DMA((2,)),
]


def slot_sum(local, pair, ring, out, sems):
    r, c, z, core = place()
    psem, zs, zr, ps, pr, fsem = sems
    mate = r + 1 - 2 * core
    swap = remote(local.at[:, 1 - core], pair, psem.at[0], psem.at[1], mate, c)
    swap.start()
    swap.wait()
    ring[z] = local[:, core] + pair[...]
    across = []
    for k in range(1, NZ):
        zz = lax.rem(z + k, NZ)
        across.append(
            remote(ring.at[z], ring.at[z], zs.at[k], zr.at[z], 2 * zz + core, c)
        )
    for copy in across:
        copy.start()
    for k in range(1, NZ):
        zz = lax.rem(z + k, NZ)
        remote(ring.at[zz], ring.at[zz], zs.at[k], zr.at[zz], r, c).wait_recv()
    total = ring[0]
    for k in range(1, NZ):
        total = total + ring[k]
    out[:, c, core] = total
    around = []
    for k in range(1, N):
        i = lax.rem(c + k, N)
        around.append(
            remote(out.at[:, c, core], out.at[:, c, core], ps.at[k], pr.at[c], r, i)
        )
    for copy in around:
        copy.start()
    for k in range(1, N):
        i = lax.rem(c + k, N)
        remote(out.at[:, i, core], out.at[:, i, core], ps.at[k], pr.at[i], r, c).wait_recv()
    final = remote(out.at[:, :, core], out.at[:, :, core], fsem.at[0], fsem.at[1], mate, c)
    final.start()
    final.wait_send()
    other = 1 - core
    remote(out.at[:, :, other], out.at[:, :, other], fsem.at[0], fsem.at[1], mate, c).wait_recv()
    for copy in across + around:
        copy.wait_send()


def spread_kernel(
    first, lead, a_ref, pr_ref, pct_ref, t_ref, gram, local, pair, ring, s1, r1, s2, s3, r3, s4, s5, *slots
):
    r, c, z, core = place()
    height = a_ref.shape[0]
    root_r, root_c = c == 0, r == 0

    @pl.when(root_r)
    def _():
        rows = r * height + lax.broadcasted_iota(jnp.int32, pr_ref.shape, 0)
        pr_ref[...] = jnp.where(rows >= lead, a_ref[:, first : first + BLOCK], 0.0)

    @pl.when(root_c)
    def _():
        cols = c * height + lax.broadcasted_iota(jnp.int32, pct_ref.shape, 1)
        pct_ref[...] = jnp.where(cols >= lead, a_ref[first : first + BLOCK, :], 0.0)

    greet(r, c)

    def pr_to(p, i, sem):
        return remote(piece(pr_ref, p, 32), piece(pr_ref, p, 32), sem, r1.at[p], r, i)

    def pct_to(p, row, sem):
        return remote(piece(pct_ref, p, 32), piece(pct_ref, p, 32), sem, r3.at[p], row, c)

    root_r_copies = [pr_to(i, i, s1.at[i]) for i in range(1, N)]
    root_r_copies += [pr_to(0, i, s2.at[i]) for i in range(1, N)]
    root_c_copies = [pct_to(p, 2 * p, s3.at[p]) for p in range(1, NZ)]
    root_c_copies += [pct_to(0, 2 * p, s4.at[p]) for p in range(1, NZ)]
    root_c_copies += [pct_to(p, 1, s5.at[p]) for p in range(NZ)]
    ahead_r = []
    for k in range(1, N):
        i = lax.rem(c + k, N)
        ahead_r.append((i, pr_to(c, i, s1.at[k])))
    ahead_c = []
    down_c = [pct_to(z, r + 1, s5.at[0])]
    for k in range(1, NZ):
        zz = lax.rem(z + k, NZ)
        ahead_c.append((zz, pct_to(z, 2 * zz, s3.at[k])))
        down_c.append(pct_to(zz, r + 1, s5.at[k]))

    def got(ref, index, sems):
        remote(piece(ref, index, 32), piece(ref, index, 32), s1.at[0], sems.at[index], r, c).wait_recv()

    @pl.when(root_r)
    def _():
        for copy in root_r_copies:
            copy.start()

    @pl.when(root_c)
    def _():
        for copy in root_c_copies:
            copy.start()

    relay_c = (core == 0) & (z != 0)

    @pl.when(c != 0)
    def _():
        got(pr_ref, c, r1)
        for i, copy in ahead_r:

            @pl.when(i != 0)
            def _():
                copy.start()

    @pl.when(relay_c)
    def _():
        got(pct_ref, z, r3)
        for zz, copy in ahead_c:

            @pl.when(zz != 0)
            def _():
                copy.start()

        down_c[0].start()
        for k in range(1, NZ):
            got(pct_ref, lax.rem(z + k, NZ), r3)
            down_c[k].start()

    @pl.when(core == 1)
    def _():
        for p in range(NZ):
            got(pct_ref, p, r3)

    @pl.when(c != 0)
    def _():
        for k in range(1, N):
            got(pr_ref, lax.rem(c + k, N), r1)

    gram[...] = dot(pr_ref[...], pr_ref[...], (0, 0))
    local[0] = gram[pl.ds(pl.multiple_of(16 * c, 16), 16), :].reshape(2, 8, 256)
    off = lead % height
    top = pr_ref[pl.ds(pl.multiple_of(off + 16 * c, 16), 16), :]
    local[1] = jnp.where(r == lead // height, top, 0.0).reshape(2, 8, 256)
    slot_sum(local, pair, ring, t_ref, slots)

    @pl.when(root_r)
    def _():
        for copy in root_r_copies:
            copy.wait_send()

    @pl.when(root_c)
    def _():
        for copy in root_c_copies:
            copy.wait_send()

    @pl.when(c != 0)
    def _():
        for i, copy in ahead_r:

            @pl.when(i != 0)
            def _():
                copy.wait_send()

    @pl.when(relay_c)
    def _():
        for zz, copy in ahead_c:

            @pl.when(zz != 0)
            def _():
                copy.wait_send()

        for copy in down_c:
            copy.wait_send()


def spread(current, index):
    dma = pltpu.SemaphoreType.DMA
    return pl.pallas_call(
        functools.partial(spread_kernel, index * BLOCK, (index + 1) * BLOCK),
        out_shape=(
            jax.ShapeDtypeStruct((512, 256), F32),
            jax.ShapeDtypeStruct((256, 512), F32),
            jax.ShapeDtypeStruct((2, N, 2, 8, 256), F32),
        ),
        in_specs=[VMEM],
        out_specs=(VMEM,) * 3,
        scratch_shapes=[
            pltpu.VMEM((256, 256), F32),
            pltpu.VMEM((2, 2, 8, 256), F32),
            pltpu.VMEM((2, 8, 256), F32),
            pltpu.VMEM((NZ, 2, 8, 256), F32),
            dma((N,)),
            dma((N,)),
            dma((N,)),
            dma((NZ,)),
            dma((NZ,)),
            dma((NZ,)),
            dma((NZ,)),
        ]
        + SLOT_SEMS,
        compiler_params=pltpu.CompilerParams(collective_id=2 * index, has_side_effects=True),
        name=f"spread{index}",
    )(current)


def gather_kernel(
    wr_ref, wct_ref, m_ref, xr_ref, xct_ref, mt_ref,
    rs_r, rs_m, half, hsum, zbuf, local, pair, ring,
    s1, r1, s2, r2, hs, s3, r3, s4, r4, s5, r5, s6, r6, *slots,
):
    r, c, z, core = place()
    mate = r + 1 - 2 * core
    greet(r, c)
    swap = remote(piece(wct_ref, 1 - core, 128), half, hs.at[0], hs.at[1], mate, c)
    swap.start()
    sends = [swap]
    for k in range(1, N):
        i = lax.rem(c + k, N)
        sends.append(remote(piece(wr_ref, i, 32), rs_r.at[c], s1.at[k], r1.at[c], r, i))
        sends[-1].start()
        sends.append(remote(piece(m_ref, i, 16), rs_m.at[c], s2.at[k], r2.at[c], r, i))
        sends[-1].start()
    rs_r[c] = wr_ref[pl.ds(pl.multiple_of(32 * c, 32), 32), :]
    rs_m[c] = m_ref[pl.ds(pl.multiple_of(16 * c, 16), 16), :]
    swap.wait_recv()
    mine = wct_ref[pl.ds(pl.multiple_of(core * 128, 128), 128), :] + half[...]
    hsum[...] = mine.reshape(NZ, 16, 512)
    zbuf[z] = hsum[z]
    for k in range(1, NZ):
        zz = lax.rem(z + k, NZ)
        sends.append(remote(hsum.at[zz], zbuf.at[z], s3.at[k], r3.at[z], 2 * zz + core, c))
        sends[-1].start()

    def got(ref, sem):
        remote(ref, ref, hs.at[0], sem, r, c).wait_recv()

    for k in range(1, N):
        i = lax.rem(c + k, N)
        got(rs_r.at[i], r1.at[i])
        got(rs_m.at[i], r2.at[i])
    total = rs_r[0]
    total_m = rs_m[0]
    for k in range(1, N):
        total = total + rs_r[k]
        total_m = total_m + rs_m[k]
    xr_ref[pl.ds(pl.multiple_of(32 * c, 32), 32), :] = total
    for k in range(1, N):
        i = lax.rem(c + k, N)
        own = piece(xr_ref, c, 32)
        sends.append(remote(own, own, s4.at[k], r4.at[c], r, i))
        sends[-1].start()
    local[0] = total_m.reshape(2, 8, 256)
    for k in range(1, NZ):
        zz = lax.rem(z + k, NZ)
        got(zbuf.at[zz], r3.at[zz])
    total = zbuf[0]
    for k in range(1, NZ):
        total = total + zbuf[k]
    mine = core * NZ + z
    xct_ref[pl.ds(pl.multiple_of(16 * mine, 16), 16), :] = total
    own = piece(xct_ref, mine, 16)
    for k in range(1, NZ):
        zz = lax.rem(z + k, NZ)
        sends.append(remote(own, own, s5.at[k], r5.at[z], 2 * zz + core, c))
        sends[-1].start()
    sends.append(remote(own, own, s6.at[0], r6.at[z], mate, c))
    sends[-1].start()
    slot_sum(local, pair, ring, mt_ref, slots)
    for k in range(1, NZ):
        zz = lax.rem(z + k, NZ)
        part = piece(xct_ref, core * NZ + zz, 16)
        got(part, r5.at[zz])
        sends.append(remote(part, part, s6.at[k], r6.at[zz], mate, c))
        sends[-1].start()
    for k in range(1, N):
        i = lax.rem(c + k, N)
        got(piece(xr_ref, i, 32), r4.at[i])
    for k in range(NZ):
        got(piece(xct_ref, (1 - core) * NZ + k, 16), r6.at[k])
    for copy in sends:
        copy.wait_send()


def gather(wr, wct, m, index):
    dma = pltpu.SemaphoreType.DMA
    return pl.pallas_call(
        gather_kernel,
        out_shape=(
            jax.ShapeDtypeStruct((512, 256), F32),
            jax.ShapeDtypeStruct((256, 512), F32),
            jax.ShapeDtypeStruct((1, N, 2, 8, 256), F32),
        ),
        in_specs=[VMEM] * 3,
        out_specs=(VMEM,) * 3,
        scratch_shapes=[
            pltpu.VMEM((N, 32, 256), F32),
            pltpu.VMEM((N, 16, 256), F32),
            pltpu.VMEM((128, 512), F32),
            pltpu.VMEM((NZ, 16, 512), F32),
            pltpu.VMEM((NZ, 16, 512), F32),
            pltpu.VMEM((1, 2, 8, 256), F32),
            pltpu.VMEM((1, 8, 256), F32),
            pltpu.VMEM((NZ, 1, 8, 256), F32),
            dma((N,)), dma((N,)), dma((N,)), dma((N,)),
            dma((2,)),
            dma((NZ,)), dma((NZ,)), dma((N,)), dma((N,)),
            dma((NZ,)), dma((NZ,)), dma((NZ,)), dma((NZ,)),
        ]
        + SLOT_SEMS,
        compiler_params=pltpu.CompilerParams(collective_id=2 * index + 1, has_side_effects=True),
        name=f"gather{index}",
    )(wr, wct, m)


def reflect(current, index, row_index, column):
    height = current.shape[0]
    lead = (index + 1) * BLOCK
    owner, off = lead // height, lead % height
    pr, pct, t = spread(current, index)
    lt, k = factor(t.reshape(2, 256, 256))
    low = jnp.pad(lt, ((off, height - off - BLOCK), (0, 0)))
    zr = pr + jnp.where(row_index == owner, low, 0.0)
    zct = pct + jnp.where(column == owner, low.T, 0.0)
    wr = dot(current, zct, (1, 1))
    wct = dot(zr, current, (0, 0))
    m = dot(zr, wr, (0, 0))
    xr, xct, b = gather(wr, wct, m, index)
    half = 0.5 * dot(k, dot(b.reshape(256, 256), k), (0, 0))
    ur = dot(xr, k) - dot(zr, half)
    uct = dot(k, xct, (0, 0)) - dot(half, zct, (0, 0))
    return current - dot(ur, zct) - dot(zr, uct)


def per_device(matrix):
    row_index = lax.axis_index("row")
    column = lax.axis_index("col")
    current = matrix
    for index in range(PANELS):
        current = reflect(current, index, row_index, column)
    return current


def solution(mesh):
    return jax.shard_map(
        per_device, mesh=mesh, in_specs=(P("row", "col"),), out_specs=P("row", "col"), check_vma=False
    )
```

```python
import jax
import jax.numpy as jnp
from jax import lax
from jax.experimental import pallas as pl
from jax.experimental.pallas import tpu as pltpu
from jax.sharding import PartitionSpec as P

BLOCK = 256
PANELS = 2
N = 16
NZ = 8
HIGH = lax.Precision.HIGHEST
F32 = jnp.float32
MESH = pl.DeviceIdType.MESH
VMEM = pl.BlockSpec(memory_space=pltpu.VMEM)


def dot(left, right, over=(1, 0)):
    return lax.dot_general(
        left,
        right,
        (((over[0],), (over[1],)), ((), ())),
        precision=HIGH,
        preferred_element_type=F32,
    )


def sweep(aug, jj, inverse):
    base = pl.multiple_of(8 * jj, 8)
    sub = lax.broadcasted_iota(jnp.int32, (8, 128), 0)
    sub2 = lax.broadcasted_iota(jnp.int32, (8, 256), 0)

    def lane(block, s):
        index = jnp.full((8, 128), base + s, jnp.int32)
        return jnp.take_along_axis(block, index, axis=1)

    group = aug[pl.ds(base, 8), :]
    cols = [lane(group[:, :128], s) for s in range(8)]
    kept = group
    for s in range(8):
        pivot = jnp.broadcast_to(cols[s][s : s + 1], (8, 128))
        inv = 1.0 / pivot
        inv2 = jnp.concatenate([inv, inv], axis=1)
        row = jnp.broadcast_to(group[s : s + 1], (8, 256))
        if not inverse:
            scale = lax.rsqrt(pivot)
            kept = jnp.where(sub2 == s, row * jnp.concatenate([scale, scale], axis=1), kept)
        new = row * inv2
        f = cols[s]
        f2 = jnp.concatenate([f, f], axis=1)
        group = jnp.where(sub2 == s, new, group - f2 * new)
        for t in range(s + 1, 8):
            crow = jnp.broadcast_to(cols[t][s : s + 1], (8, 128)) * inv
            cols[t] = jnp.where(sub == s, crow, cols[t] - f * crow)
    aug[pl.ds(base, 8), :] = group if inverse else kept
    rows = [jnp.broadcast_to(group[s : s + 1], (8, 256)) for s in range(8)]
    for g in range(16):
        block = aug[8 * g : 8 * g + 8, :]
        keep = (g != jj) if inverse else (g > jj)
        new = block
        for s in range(8):
            c = lane(block[:, :128], s)
            new = new - jnp.concatenate([c, c], axis=1) * rows[s]
        aug[8 * g : 8 * g + 8, :] = jnp.where(keep, new, block)


def remote(src, dst, send, recv, row, col):
    return pltpu.make_async_remote_copy(
        src_ref=src,
        dst_ref=dst,
        send_sem=send,
        recv_sem=recv,
        device_id=(row, col),
        device_id_type=MESH,
    )


def greet(r, c):
    barrier = pltpu.get_barrier_semaphore()
    for k in range(1, N):
        pl.semaphore_signal(barrier, inc=1, device_id=(r, lax.rem(c + k, N)), device_id_type=MESH)
        pl.semaphore_signal(barrier, inc=1, device_id=(lax.rem(r + k, N), c), device_id_type=MESH)
    pl.semaphore_wait(barrier, 2 * (N - 1))


def at(index, size):
    return pl.ds(pl.multiple_of(index * size, size), size)


def kernel(
    a_ref, out_ref,
    cur, pr, pct, gram, gin, tall, lt_ref, k_ref, n_ref, aug, zr, zct,
    wr, wct, m, inr, inm, half, hsum, zin, xr, xct, mloc, mpair, mring, ball,
    ss, g_r, t_r, p_r, q_r, r_r, m_r, h_r, z_r, x_r, y_r, w_r, s_r, u_r, v_r, f_r,
):
    r, c = lax.axis_index("row"), lax.axis_index("col")
    z, core = r // 2, lax.rem(r, 2)
    mate = r + 1 - 2 * core
    height = a_ref.shape[0]
    eye = (
        lax.broadcasted_iota(jnp.int32, (128, 128), 0)
        == lax.broadcasted_iota(jnp.int32, (128, 128), 1)
    ).astype(F32)
    upper = lax.broadcasted_iota(jnp.int32, (128, 128), 0) <= lax.broadcasted_iota(
        jnp.int32, (128, 128), 1
    )
    plane = [lax.rem(c + k, N) for k in range(1, N)]
    line = [lax.rem(r + k, N) for k in range(1, N)]
    ring = [lax.rem(z + k, NZ) for k in range(1, NZ)]

    def load(block):
        aug[:, :128] = block
        aug[:, 128:] = eye

    def sweeps(lo, hi, inverse):
        lax.fori_loop(lo, hi, lambda jj, _: (sweep(aug, jj, inverse), 0)[1], 0)

    def got(ref, sem):
        remote(ref, ref, ss.at[0], sem, r, c).wait_recv()

    cur[...] = a_ref[...]

    for p in range(PANELS):
        first, lead = p * BLOCK, (p + 1) * BLOCK
        owner, off = lead // height, lead % height
        count = iter(range(1, 400))

        def send(src, dst, sem, row, col):
            return remote(src, dst, ss.at[next(count)], sem, row, col)

        @pl.when(r == 0)
        def _():
            cols = c * height + lax.broadcasted_iota(jnp.int32, (BLOCK, height), 1)
            pct[p] = jnp.where(cols >= lead, cur[first : first + BLOCK, :], 0.0)
            gram[...] = dot(pct[p], pct[p], (1, 1))
            gin[p, c] = gram[at(c, 16), :]

        @pl.when(c == 0)
        def _():
            rows = r * height + lax.broadcasted_iota(jnp.int32, (height, BLOCK), 0)
            pr[p] = jnp.where(rows >= lead, cur[:, first : first + BLOCK], 0.0)

        if p == 0:
            greet(r, c)

        def slot(a, i):
            return tall.at[p, a, i]

        def pr_to(q, i):
            return send(pr.at[p, at(q, 32)], pr.at[p, at(q, 32)], p_r.at[p, q], r, i)

        def pct_to(q, row):
            return send(pct.at[p, at(q, 32)], pct.at[p, at(q, 32)], q_r.at[p, q], row, c)

        g_out = [send(gram.at[at(i, 16)], gin.at[p, c], g_r.at[p, c], r, i) for i in plane]
        top_out = [
            send(pct.at[p, at(i, 16), pl.ds(off, BLOCK)], slot(1, i), t_r.at[p, 1, i], r, i)
            for i in plane
        ]
        down = [send(slot(a, c), slot(a, c), t_r.at[p, a, c], i, c) for a in (0, 1) for i in line]
        share = [
            [send(slot(a, c), slot(a, c), t_r.at[p, a, c], r, i) for i in plane] for a in (0, 1)
        ]
        root_r = [pr_to(i, i) for i in range(1, N)] + [pr_to(0, i) for i in range(1, N)]
        root_c = [pct_to(q, 2 * q) for q in range(1, NZ)] + [pct_to(0, 2 * q) for q in range(1, NZ)]
        root_c += [pct_to(q, 1) for q in range(NZ)]
        ahead_r = [(i, pr_to(c, i)) for i in plane]
        ahead_c = [(q, pct_to(z, 2 * q)) for q in ring]
        low_c = [pct_to(z, r + 1)] + [pct_to(q, r + 1) for q in ring]
        relay = (core == 0) & (z != 0)

        @pl.when(r == 0)
        def _():
            for copy in g_out:
                copy.start()

        @pl.when((r == 0) & (c == owner))
        def _():
            for copy in top_out:
                copy.start()
            tall[p, 1, c] = pct[p, at(c, 16), off : off + BLOCK]

        @pl.when(c == 0)
        def _():
            for copy in root_r:
                copy.start()

        @pl.when(r == 0)
        def _():
            for copy in root_c:
                copy.start()

        @pl.when(c != 0)
        def _():
            got(pr.at[p, at(c, 32)], p_r.at[p, c])
            for i, copy in ahead_r:

                @pl.when(i != 0)
                def _():
                    copy.start()

        @pl.when(r == 0)
        def _():
            for i in plane:
                got(gin.at[p, i], g_r.at[p, i])
            total = gin[p, 0]
            for i in range(1, N):
                total = total + gin[p, i]
            tall[p, 0, c] = total
            for copy in down[: N - 1]:
                copy.start()

            @pl.when(c != owner)
            def _():
                got(slot(1, c), t_r.at[p, 1, c])

            for copy in down[N - 1 :]:
                copy.start()

        @pl.when(relay)
        def _():
            got(pct.at[p, at(z, 32)], q_r.at[p, z])
            for q, copy in ahead_c:

                @pl.when(q != 0)
                def _():
                    copy.start()

            low_c[0].start()

        @pl.when(r != 0)
        def _():
            got(slot(0, c), t_r.at[p, 0, c])

        for copy in share[0]:
            copy.start()

        @pl.when(r != 0)
        def _():
            got(slot(1, c), t_r.at[p, 1, c])

        for copy in share[1]:
            copy.start()

        @pl.when(relay)
        def _():
            for k in range(1, NZ):
                got(pct.at[p, at(ring[k - 1], 32)], q_r.at[p, ring[k - 1]])
                low_c[k].start()

        for i in plane:
            got(slot(0, i), t_r.at[p, 0, i])

        g = tall[p, 0].reshape(BLOCK, BLOCK)
        load(g[:128, :128])
        sweeps(0, 16, False)
        lt00 = jnp.where(upper, aug[:, :128], 0.0)
        lt01 = dot(aug[:, 128:], g[:128, 128:])
        load(g[128:, 128:] - dot(lt01, lt01, (0, 0)))
        sweeps(0, 16, False)
        lt_ref[:128, :128] = lt00
        lt_ref[:128, 128:] = lt01
        lt_ref[128:, :128] = jnp.zeros((128, 128), F32)
        lt_ref[128:, 128:] = jnp.where(upper, aug[:, :128], 0.0)

        @pl.when(core == 1)
        def _():
            for q in range(NZ):
                got(pct.at[p, at(q, 32)], q_r.at[p, q])

        @pl.when(c != 0)
        def _():
            for i in plane:
                got(pr.at[p, at(i, 32)], p_r.at[p, i])

        for i in plane:
            got(slot(1, i), t_r.at[p, 1, i])

        zr[...] = pr[p]
        zct[...] = pct[p]

        @pl.when(r == owner)
        def _():
            zr[off : off + BLOCK, :] = zr[off : off + BLOCK, :] + lt_ref[...]

        @pl.when(c == owner)
        def _():
            zct[:, off : off + BLOCK] = zct[:, off : off + BLOCK] + lt_ref[...].T

        wct[...] = dot(zr[...], cur[...], (0, 0))
        swap = send(wct.at[at(1 - core, 128)], half.at[p], h_r.at[p], mate, c)
        swap.start()
        sends = [swap]

        def go(copy):
            copy.start()
            sends.append(copy)

        wr[...] = dot(cur[...], zct[...], (1, 1))
        for i in plane:
            go(send(wr.at[at(i, 32)], inr.at[p, c], r_r.at[p, c], r, i))
        m[...] = dot(zr[...], wr[...], (0, 0))
        for i in plane:
            go(send(m.at[at(i, 16)], inm.at[p, c], m_r.at[p, c], r, i))
        inr[p, c] = wr[at(c, 32), :]
        inm[p, c] = m[at(c, 16), :]
        swap.wait_recv()
        mine = wct[at(core, 128), :] + half[p]
        hsum[...] = mine.reshape(NZ, 16, 512)
        zin[p, z] = hsum[z]
        for q in ring:
            go(send(hsum.at[q], zin.at[p, z], z_r.at[p, z], 2 * q + core, c))

        n_ref[...] = g + dot(tall[p, 1].reshape(BLOCK, BLOCK), lt_ref[...])
        load(n_ref[:128, :128])
        sweeps(0, 8, True)

        for i in plane:
            got(inr.at[p, i], r_r.at[p, i])
        total = inr[p, 0]
        for i in range(1, N):
            total = total + inr[p, i]
        xr[p, at(c, 32), :] = total
        for i in plane:
            own = xr.at[p, at(c, 32)]
            go(send(own, own, x_r.at[p, c], r, i))
        for i in plane:
            got(inm.at[p, i], m_r.at[p, i])
        total = inm[p, 0]
        for i in range(1, N):
            total = total + inm[p, i]
        mloc[...] = total.reshape(2, 8, BLOCK)
        go(send(mloc.at[1 - core], mpair.at[p], s_r.at[p], mate, c))
        for q in ring:
            got(zin.at[p, q], z_r.at[p, q])
        total = zin[p, 0]
        for q in range(1, NZ):
            total = total + zin[p, q]
        spot = core * NZ + z
        xct[p, at(spot, 16), :] = total
        own = xct.at[p, at(spot, 16)]
        for q in ring:
            go(send(own, own, y_r.at[p, z], 2 * q + core, c))
        go(send(own, own, w_r.at[p, z], mate, c))
        got(mpair.at[p], s_r.at[p])
        mring[p, z] = mloc[core] + mpair[p]
        for q in ring:
            go(send(mring.at[p, z], mring.at[p, z], u_r.at[p, z], 2 * q + core, c))

        sweeps(8, 16, True)
        d0 = aug[:, 128:]
        n01 = dot(d0, n_ref[:128, 128:])
        n10d = dot(n_ref[128:, :128], d0)
        load(n_ref[128:, 128:] - dot(n_ref[128:, :128], n01))

        for q in ring:
            got(mring.at[p, q], u_r.at[p, q])
        total = mring[p, 0]
        for q in range(1, NZ):
            total = total + mring[p, q]
        ball[p, c, core] = total
        own = ball.at[p, c, core]
        for i in plane:
            go(send(own, own, v_r.at[p, c], r, i))
        for q in ring:
            part = xct.at[p, at(core * NZ + q, 16)]
            got(part, y_r.at[p, q])
            go(send(part, part, w_r.at[p, q], mate, c))

        sweeps(0, 8, True)
        for i in plane:
            got(ball.at[p, i, core], v_r.at[p, i])
        final = ball.at[p, :, core]
        go(send(final, final, f_r.at[p], mate, c))
        sweeps(8, 16, True)
        e = aug[:, 128:]
        k10 = -dot(e, n10d)
        k_ref[:128, :128] = d0 - dot(n01, k10)
        k_ref[:128, 128:] = -dot(n01, e)
        k_ref[128:, :128] = k10
        k_ref[128:, 128:] = e

        for i in plane:
            got(xr.at[p, at(i, 32)], x_r.at[p, i])
        for q in range(NZ):
            got(xct.at[p, at((1 - core) * NZ + q, 16)], w_r.at[p, q])
        got(ball.at[p, :, 1 - core], f_r.at[p])

        inner = ball[p].reshape(BLOCK, BLOCK)
        coupled = 0.5 * dot(k_ref[...], dot(inner, k_ref[...]), (0, 0))
        ur = dot(xr[p], k_ref[...]) - dot(zr[...], coupled)
        uct = dot(k_ref[...], xct[p], (0, 0)) - dot(coupled, zct[...], (0, 0))
        dest = out_ref if p == PANELS - 1 else cur
        dest[...] = cur[...] - dot(ur, zct[...]) - dot(zr[...], uct)

        for copy in share[0] + share[1] + sends:
            copy.wait_send()

        @pl.when(r == 0)
        def _():
            for copy in g_out + down + root_c:
                copy.wait_send()

        @pl.when((r == 0) & (c == owner))
        def _():
            for copy in top_out:
                copy.wait_send()

        @pl.when(c == 0)
        def _():
            for copy in root_r:
                copy.wait_send()

        @pl.when(c != 0)
        def _():
            for i, copy in ahead_r:

                @pl.when(i != 0)
                def _():
                    copy.wait_send()

        @pl.when(relay)
        def _():
            for q, copy in ahead_c:

                @pl.when(q != 0)
                def _():
                    copy.wait_send()

            for copy in low_c:
                copy.wait_send()


def per_device(matrix):
    dma = pltpu.SemaphoreType.DMA

    def buf(*shape):
        return pltpu.VMEM(shape, F32)

    return pl.pallas_call(
        kernel,
        out_shape=jax.ShapeDtypeStruct(matrix.shape, F32),
        in_specs=[VMEM],
        out_specs=VMEM,
        scratch_shapes=[
            buf(512, 512),
            buf(2, 512, 256),
            buf(2, 256, 512),
            buf(256, 256),
            buf(2, N, 16, 256),
            buf(2, 2, N, 16, 256),
            buf(256, 256),
            buf(256, 256),
            buf(256, 256),
            buf(128, 256),
            buf(512, 256),
            buf(256, 512),
            buf(512, 256),
            buf(256, 512),
            buf(256, 256),
            buf(2, N, 32, 256),
            buf(2, N, 16, 256),
            buf(2, 128, 512),
            buf(NZ, 16, 512),
            buf(2, NZ, 16, 512),
            buf(2, 512, 256),
            buf(2, 256, 512),
            buf(2, 8, 256),
            buf(2, 8, 256),
            buf(2, NZ, 8, 256),
            buf(2, N, 2, 8, 256),
            dma((400,)),
            dma((2, N)),
            dma((2, 2, N)),
            dma((2, N)),
            dma((2, NZ)),
            dma((2, N)),
            dma((2, N)),
            dma((2,)),
            dma((2, NZ)),
            dma((2, N)),
            dma((2, NZ)),
            dma((2, NZ)),
            dma((2,)),
            dma((2, NZ)),
            dma((2, N)),
            dma((2,)),
        ],
        compiler_params=pltpu.CompilerParams(collective_id=0, has_side_effects=True),
        name="reduce_panels",
    )(matrix)


def solution(mesh):
    return jax.shard_map(
        per_device, mesh=mesh, in_specs=(P("row", "col"),), out_specs=P("row", "col"), check_vma=False
    )
```

```python
import jax
import jax.numpy as jnp
from jax import lax
from jax.experimental import pallas as pl
from jax.experimental.pallas import tpu as pltpu
from jax.sharding import PartitionSpec as P

BLOCK = 256
PANELS = 2
N = 16
NZ = 8
HIGH = lax.Precision.HIGHEST
F32 = jnp.float32
MESH = pl.DeviceIdType.MESH
VMEM = pl.BlockSpec(memory_space=pltpu.VMEM)


def dot(left, right, over=(1, 0)):
    return lax.dot_general(
        left,
        right,
        (((over[0],), (over[1],)), ((), ())),
        precision=HIGH,
        preferred_element_type=F32,
    )


def sweep(aug, jj, inverse):
    base = pl.multiple_of(8 * jj, 8)
    sub = lax.broadcasted_iota(jnp.int32, (8, 128), 0)
    sub2 = lax.broadcasted_iota(jnp.int32, (8, 256), 0)

    def lane(block, s):
        index = jnp.full((8, 128), base + s, jnp.int32)
        return jnp.take_along_axis(block, index, axis=1)

    group = aug[pl.ds(base, 8), :]
    cols = [lane(group[:, :128], s) for s in range(8)]
    kept = group
    for s in range(8):
        pivot = jnp.broadcast_to(cols[s][s : s + 1], (8, 128))
        inv = 1.0 / pivot
        inv2 = jnp.concatenate([inv, inv], axis=1)
        row = jnp.broadcast_to(group[s : s + 1], (8, 256))
        if not inverse:
            scale = lax.rsqrt(pivot)
            kept = jnp.where(sub2 == s, row * jnp.concatenate([scale, scale], axis=1), kept)
        new = row * inv2
        f = cols[s]
        f2 = jnp.concatenate([f, f], axis=1)
        group = jnp.where(sub2 == s, new, group - f2 * new)
        for t in range(s + 1, 8):
            crow = jnp.broadcast_to(cols[t][s : s + 1], (8, 128)) * inv
            cols[t] = jnp.where(sub == s, crow, cols[t] - f * crow)
    aug[pl.ds(base, 8), :] = group if inverse else kept
    rows = [jnp.broadcast_to(group[s : s + 1], (8, 256)) for s in range(8)]
    for g in range(16):
        block = aug[8 * g : 8 * g + 8, :]
        keep = (g != jj) if inverse else (g > jj)
        new = block
        for s in range(8):
            c = lane(block[:, :128], s)
            new = new - jnp.concatenate([c, c], axis=1) * rows[s]
        aug[8 * g : 8 * g + 8, :] = jnp.where(keep, new, block)


def remote(src, dst, send, recv, row, col):
    return pltpu.make_async_remote_copy(
        src_ref=src,
        dst_ref=dst,
        send_sem=send,
        recv_sem=recv,
        device_id=(row, col),
        device_id_type=MESH,
    )


def greet(r, c):
    barrier = pltpu.get_barrier_semaphore()
    for k in range(1, N):
        pl.semaphore_signal(barrier, inc=1, device_id=(r, lax.rem(c + k, N)), device_id_type=MESH)
        pl.semaphore_signal(barrier, inc=1, device_id=(lax.rem(r + k, N), c), device_id_type=MESH)
    pl.semaphore_wait(barrier, 2 * (N - 1))


def at(index, size):
    return pl.ds(pl.multiple_of(index * size, size), size)


def kernel(
    a_ref, out_ref,
    cur, pr, pct, pc, aer, aec, aepr, aepc, gram, gin, tsrc, tall, lt_ref, k_ref, n_ref, aug, zr, zc,
    wr, wc, m, inr, inm, iny, half, hsum, zin, xr, xc, mloc, mpair, mring, ball,
    ss, g_r, b_r, t_r, tm_r, p_r, q_r, ar_r, ac_r, r_r, m_r, yt_r, h_r, z_r, x_r, y_r, w_r, s_r, u_r, v_r, f_r,
):
    r, c = lax.axis_index("row"), lax.axis_index("col")
    z, core = r // 2, lax.rem(r, 2)
    other = 1 - core
    mate = r + 1 - 2 * core
    height = a_ref.shape[0]
    eye = (
        lax.broadcasted_iota(jnp.int32, (128, 128), 0)
        == lax.broadcasted_iota(jnp.int32, (128, 128), 1)
    ).astype(F32)
    upper = lax.broadcasted_iota(jnp.int32, (128, 128), 0) <= lax.broadcasted_iota(
        jnp.int32, (128, 128), 1
    )
    plane = [lax.rem(c + k, N) for k in range(1, N)]
    line = [lax.rem(r + k, N) for k in range(1, N)]
    ring = [lax.rem(z + k, NZ) for k in range(1, NZ)]

    def load(block):
        aug[:, :128] = block
        aug[:, 128:] = eye

    def sweeps(lo, hi, inverse):
        lax.fori_loop(lo, hi, lambda jj, _: (sweep(aug, jj, inverse), 0)[1], 0)

    def got(ref, sem):
        remote(ref, ref, ss.at[0], sem, r, c).wait_recv()

    def when(cond, run):
        pl.when(cond)(run)

    cur[...] = a_ref[...]

    for p in range(PANELS):
        first, lead = p * BLOCK, (p + 1) * BLOCK
        owner, off = lead // height, lead % height
        count = iter(range(1, 480))

        def send(src, dst, sem, row, col):
            return remote(src, dst, ss.at[next(count)], sem, row, col)

        def start(copies):
            for copy in copies:
                copy.start()

        @pl.when(r == 0)
        def _():
            cols = c * height + lax.broadcasted_iota(jnp.int32, (BLOCK, height), 1)
            pct[...] = jnp.where(cols >= lead, cur[first : first + BLOCK, :], 0.0)
            gram[...] = dot(pct[...], pct[...], (1, 1))
            gin[p, c] = gram[at(c, 16), :]

        def slot(a, i, h):
            return tall.at[p, a, i, h]

        def pr_to(q, i):
            return send(pr.at[p, at(q, 32)], pr.at[p, at(q, 32)], p_r.at[p, q], r, i)

        def pc_to(q, row):
            return send(pc.at[p, at(q, 64)], pc.at[p, at(q, 64)], q_r.at[p, q], row, c)

        g_out = [send(gram.at[at(i, 16)], gin.at[p, c], g_r.at[p, c], r, i) for i in plane]
        top_out = [
            send(
                pr.at[p, pl.ds(pl.multiple_of(off + 16 * i + 8 * h, 8), 8)],
                tsrc.at[p, 1, h], b_r.at[p, 1, h], r, i,
            )
            for i in plane for h in (0, 1)
        ]
        ee_out = [
            send(
                aer.at[pl.ds(pl.multiple_of(off + 16 * i + 8 * h, 8), 8)],
                tsrc.at[p, 2, h], b_r.at[p, 2, h], r, i,
            )
            for i in plane for h in (0, 1)
        ]
        down = [
            [
                send(tsrc.at[p, a, lax.rem(i, 2)], slot(a, c, lax.rem(i, 2)), t_r.at[p, a, c, lax.rem(i, 2)], i, c)
                for i in line
            ]
            for a in range(3)
        ]
        share = [
            [send(slot(a, c, core), slot(a, c, core), t_r.at[p, a, c, core], r, i) for i in plane]
            for a in range(3)
        ]
        cross = [
            send(tall.at[p, a, :, core], tall.at[p, a, :, core], tm_r.at[p, a], mate, c)
            for a in range(3)
        ]
        root_r = [pr_to(i, i) for i in range(1, N)] + [pr_to(0, i) for i in range(1, N)]
        root_c = [pc_to(q, 2 * q) for q in range(1, NZ)] + [pc_to(0, 2 * q) for q in range(1, NZ)]
        root_c += [pc_to(q, 1) for q in range(NZ)]
        ae_r = [send(aer.at[at(i, 32)], aepr.at[p], ar_r.at[p], r, i) for i in plane]
        ae_c = [
            send(aec.at[at(lax.rem(i, 2) * NZ + i // 2, 32)], aepc.at[p], ac_r.at[p], i, c)
            for i in line
        ]
        ahead_r = [(i, pr_to(c, i)) for i in plane]
        ahead_c = [(q, pc_to(z, 2 * q)) for q in ring]
        low_c = [pc_to(z, r + 1)] + [pc_to(q, r + 1) for q in ring]
        relay = (core == 0) & (z != 0)

        @pl.when(c == 0)
        def _():
            rows = r * height + lax.broadcasted_iota(jnp.int32, (height, BLOCK), 0)
            pr[p] = jnp.where(rows >= lead, cur[:, first : first + BLOCK], 0.0)

        @pl.when(c == owner)
        def _():
            aer[...] = cur[:, off : off + BLOCK]
            aepr[p] = aer[at(c, 32), :]

        @pl.when(r == owner)
        def _():
            aec[...] = cur[off : off + BLOCK, :].T
            aepc[p] = aec[at(core * NZ + z, 32), :]

        if p == 0:
            greet(r, c)

        when(r == 0, lambda: start(g_out))

        @pl.when((r == owner) & (c == 0))
        def _():
            start(top_out)
            for h in (0, 1):
                tsrc[p, 1, h] = pr[p, pl.ds(pl.multiple_of(off + 16 * c + 8 * h, 8), 8), :]

        when(c == 0, lambda: start(root_r))

        @pl.when(r == 0)
        def _():
            pc[p] = pct[...].T
            start(root_c)

        @pl.when((r == owner) & (c == owner))
        def _():
            start(ee_out)
            for h in (0, 1):
                tsrc[p, 2, h] = aer[pl.ds(pl.multiple_of(off + 16 * c + 8 * h, 8), 8), :]

        @pl.when(r == 0)
        def _():
            for i in plane:
                got(gin.at[p, i], g_r.at[p, i])
            total = gin[p, 0]
            for i in range(1, N):
                total = total + gin[p, i]
            tsrc[p, 0] = total.reshape(2, 8, BLOCK)
            tall[p, 0, c, core] = tsrc[p, 0, core]
            start(down[0])

        @pl.when(c != 0)
        def _():
            got(pr.at[p, at(c, 32)], p_r.at[p, c])
            for i, copy in ahead_r:
                when(i != 0, copy.start)

        @pl.when(relay)
        def _():
            got(pc.at[p, at(z, 64)], q_r.at[p, z])
            for q, copy in ahead_c:
                when(q != 0, copy.start)
            low_c[0].start()

        when(r != 0, lambda: got(slot(0, c, core), t_r.at[p, 0, c, core]))
        start(share[0])

        @pl.when(r == owner)
        def _():
            for a, holder in ((1, 0), (2, owner)):

                @pl.when(c != holder)
                def _():
                    for h in (0, 1):
                        got(tsrc.at[p, a, h], b_r.at[p, a, h])

                tall[p, a, c, core] = tsrc[p, a, core]
                start(down[a])

        when(c == owner, lambda: start(ae_r))
        when(r == owner, lambda: start(ae_c))

        for i in plane:
            got(slot(0, i, core), t_r.at[p, 0, i, core])
        cross[0].start()

        for a in (1, 2):
            when(r != owner, lambda a=a: got(slot(a, c, core), t_r.at[p, a, c, core]))
            start(share[a])

        got(tall.at[p, 0, :, other], tm_r.at[p, 0])

        g = tall[p, 0].reshape(BLOCK, BLOCK)
        load(g[:128, :128])
        sweeps(0, 16, False)
        lt00 = jnp.where(upper, aug[:, :128], 0.0)
        lt01 = dot(aug[:, 128:], g[:128, 128:])
        load(g[128:, 128:] - dot(lt01, lt01, (0, 0)))
        lt_ref[:128, :128] = lt00
        lt_ref[:128, 128:] = lt01
        lt_ref[128:, :128] = jnp.zeros((128, 128), F32)

        @pl.when(relay)
        def _():
            for k in range(1, NZ):
                got(pc.at[p, at(ring[k - 1], 64)], q_r.at[p, ring[k - 1]])
                low_c[k].start()

        @pl.when(c != 0)
        def _():
            for i in plane:
                got(pr.at[p, at(i, 32)], p_r.at[p, i])

        sends = []

        def go(copy):
            copy.start()
            sends.append(copy)

        wc[...] = dot(cur[...], pr[p], (0, 0))
        swap = send(wc.at[at(other, 256)], half.at[p], h_r.at[p], mate, c)
        go(swap)

        @pl.when(core == 1)
        def _():
            for q in range(NZ):
                got(pc.at[p, at(q, 64)], q_r.at[p, q])

        wr[...] = dot(cur[...], pc[p])
        for i in plane:
            go(send(wr.at[at(i, 32)], inr.at[p, c], r_r.at[p, c], r, i))
        inr[p, c] = wr[at(c, 32), :]
        m[...] = dot(pr[p], wr[...], (0, 0))
        for i in plane:
            go(send(m.at[at(i, 16)], inm.at[p, c], m_r.at[p, c], r, i))
        inm[p, c] = m[at(c, 16), :]

        def top_rows(i):
            return pl.ds(pl.multiple_of(off + 16 * i, 16), 16)

        y_out = [send(wr.at[top_rows(i)], iny.at[p, c], yt_r.at[p, c], r, i) for i in plane]

        @pl.when(r == owner)
        def _():
            start(y_out)
            iny[p, c] = wr[top_rows(c), :]

        swap.wait_recv()
        hsum[...] = (wc[at(core, 256), :] + half[p]).reshape(NZ, 32, BLOCK)
        zin[p, z] = hsum[z]
        for q in ring:
            go(send(hsum.at[q], zin.at[p, z], z_r.at[p, z], 2 * q + core, c))

        sweeps(0, 16, False)
        lt_ref[128:, 128:] = jnp.where(upper, aug[:, :128], 0.0)
        lt = lt_ref[...]

        for i in plane:
            got(inr.at[p, i], r_r.at[p, i])
        total = inr[p, 0]
        for i in range(1, N):
            total = total + inr[p, i]
        when(c != owner, lambda: got(aepr.at[p], ar_r.at[p]))
        xr[p, at(c, 32), :] = total + dot(aepr[p], lt)
        for i in plane:
            own = xr.at[p, at(c, 32)]
            go(send(own, own, x_r.at[p, c], r, i))
        for q in ring:
            got(zin.at[p, q], z_r.at[p, q])
        total = zin[p, 0]
        for q in range(1, NZ):
            total = total + zin[p, q]
        when(r != owner, lambda: got(aepc.at[p], ac_r.at[p]))
        spot = core * NZ + z
        xc[p, at(spot, 32), :] = total + dot(aepc[p], lt)
        own = xc.at[p, at(spot, 32)]
        for q in ring:
            go(send(own, own, y_r.at[p, z], 2 * q + core, c))
        go(send(own, own, w_r.at[p, z], mate, c))
        for i in plane:
            got(inm.at[p, i], m_r.at[p, i])
        total = inm[p, 0]
        for i in range(1, N):
            total = total + inm[p, i]
        mloc[0] = total.reshape(2, 8, BLOCK)

        @pl.when(r == owner)
        def _():
            for i in plane:
                got(iny.at[p, i], yt_r.at[p, i])
            total = iny[p, 0]
            for i in range(1, N):
                total = total + iny[p, i]
            mloc[1] = total.reshape(2, 8, BLOCK)

        @pl.when(r != owner)
        def _():
            mloc[1] = jnp.zeros((2, 8, BLOCK), F32)

        go(send(mloc.at[:, other], mpair.at[p], s_r.at[p], mate, c))

        for i in plane:
            got(slot(1, i, core), t_r.at[p, 1, i, core])
        cross[1].start()
        for i in plane:
            got(slot(2, i, core), t_r.at[p, 2, i, core])
        cross[2].start()
        got(mpair.at[p], s_r.at[p])
        mring[p, z] = mloc[:, core] + mpair[p]
        for q in ring:
            go(send(mring.at[p, z], mring.at[p, z], u_r.at[p, z], 2 * q + core, c))
        got(tall.at[p, 1, :, other], tm_r.at[p, 1])
        got(tall.at[p, 2, :, other], tm_r.at[p, 2])

        n_ref[...] = tall[p, 0].reshape(BLOCK, BLOCK) + dot(tall[p, 1].reshape(BLOCK, BLOCK), lt, (0, 0))
        load(n_ref[:128, :128])
        sweeps(0, 16, True)

        for q in ring:
            got(mring.at[p, q], u_r.at[p, q])
        total = mring[p, 0]
        for q in range(1, NZ):
            total = total + mring[p, q]
        ball[p, :, c, core] = total
        own = ball.at[p, :, c, core]
        for i in plane:
            go(send(own, own, v_r.at[p, c], r, i))
        for q in ring:
            part = xc.at[p, at(core * NZ + q, 32)]
            got(part, y_r.at[p, q])
            go(send(part, part, w_r.at[p, q], mate, c))

        d0 = aug[:, 128:]
        n01 = dot(d0, n_ref[:128, 128:])
        n10d = dot(n_ref[128:, :128], d0)
        load(n_ref[128:, 128:] - dot(n_ref[128:, :128], n01))
        sweeps(0, 8, True)
        for i in plane:
            got(ball.at[p, :, i, core], v_r.at[p, i])
        final = ball.at[p, :, :, core]
        go(send(final, final, f_r.at[p], mate, c))
        sweeps(8, 16, True)
        e = aug[:, 128:]
        k10 = -dot(e, n10d)
        k_ref[:128, :128] = d0 - dot(n01, k10)
        k_ref[:128, 128:] = -dot(n01, e)
        k_ref[128:, :128] = k10
        k_ref[128:, 128:] = e

        zr[...] = pr[p]
        zc[...] = pc[p]

        @pl.when(r == owner)
        def _():
            zr[off : off + BLOCK, :] = zr[off : off + BLOCK, :] + lt_ref[...]

        @pl.when(c == owner)
        def _():
            zc[off : off + BLOCK, :] = zc[off : off + BLOCK, :] + lt_ref[...]

        for i in plane:
            got(xr.at[p, at(i, 32)], x_r.at[p, i])
        for q in range(NZ):
            got(xc.at[p, at(other * NZ + q, 32)], w_r.at[p, q])
        got(ball.at[p, :, :, other], f_r.at[p])

        ytop = ball[p, 1].reshape(BLOCK, BLOCK)
        xtop = ytop + dot(tall[p, 2].reshape(BLOCK, BLOCK), lt)
        inner = ball[p, 0].reshape(BLOCK, BLOCK) + dot(ytop, lt, (0, 0)) + dot(lt, xtop, (0, 0))
        coupled = 0.5 * dot(k_ref[...], dot(inner, k_ref[...]), (0, 0))
        ur = dot(xr[p], k_ref[...]) - dot(zr[...], coupled)
        uc = dot(xc[p], k_ref[...]) - dot(zc[...], coupled)
        dest = out_ref if p == PANELS - 1 else cur
        dest[...] = cur[...] - dot(ur, zc[...], (1, 1)) - dot(zr[...], uc, (1, 1))

        def left(copies):
            for copy in copies:
                copy.wait_send()

        left(share[0] + share[1] + share[2] + cross + sends)
        when(r == 0, lambda: left(g_out + down[0] + root_c))
        when(r == owner, lambda: left(down[1] + down[2] + ae_c + y_out))
        when((r == owner) & (c == 0), lambda: left(top_out))
        when((r == owner) & (c == owner), lambda: left(ee_out))
        when(c == 0, lambda: left(root_r))
        when(c == owner, lambda: left(ae_r))

        @pl.when(c != 0)
        def _():
            for i, copy in ahead_r:
                when(i != 0, copy.wait_send)

        @pl.when(relay)
        def _():
            for q, copy in ahead_c:
                when(q != 0, copy.wait_send)
            left(low_c)


def per_device(matrix):
    dma = pltpu.SemaphoreType.DMA

    def buf(*shape):
        return pltpu.VMEM(shape, F32)

    return pl.pallas_call(
        kernel,
        out_shape=jax.ShapeDtypeStruct(matrix.shape, F32),
        in_specs=[VMEM],
        out_specs=VMEM,
        scratch_shapes=[
            buf(512, 512),
            buf(2, 512, 256),
            buf(256, 512),
            buf(2, 512, 256),
            buf(512, 256),
            buf(512, 256),
            buf(2, 32, 256),
            buf(2, 32, 256),
            buf(256, 256),
            buf(2, N, 16, 256),
            buf(2, 3, 2, 8, 256),
            buf(2, 3, N, 2, 8, 256),
            buf(256, 256),
            buf(256, 256),
            buf(256, 256),
            buf(128, 256),
            buf(512, 256),
            buf(512, 256),
            buf(512, 256),
            buf(512, 256),
            buf(256, 256),
            buf(2, N, 32, 256),
            buf(2, N, 16, 256),
            buf(2, N, 16, 256),
            buf(2, 256, 256),
            buf(NZ, 32, 256),
            buf(2, NZ, 32, 256),
            buf(2, 512, 256),
            buf(2, 512, 256),
            buf(2, 2, 8, 256),
            buf(2, 2, 8, 256),
            buf(2, NZ, 2, 8, 256),
            buf(2, 2, N, 2, 8, 256),
            dma((480,)),
            dma((2, N)),
            dma((2, 3, 2)),
            dma((2, 3, N, 2)),
            dma((2, 3)),
            dma((2, N)),
            dma((2, NZ)),
            dma((2,)),
            dma((2,)),
            dma((2, N)),
            dma((2, N)),
            dma((2, N)),
            dma((2,)),
            dma((2, NZ)),
            dma((2, N)),
            dma((2, NZ)),
            dma((2, NZ)),
            dma((2,)),
            dma((2, NZ)),
            dma((2, N)),
            dma((2,)),
        ],
        compiler_params=pltpu.CompilerParams(collective_id=0, has_side_effects=True),
        name="reduce_panels",
    )(matrix)


def solution(mesh):
    return jax.shard_map(
        per_device, mesh=mesh, in_specs=(P("row", "col"),), out_specs=P("row", "col"), check_vma=False
    )
```

```python
import jax
import jax.numpy as jnp
from jax import lax
from jax.experimental import pallas as pl
from jax.experimental.pallas import tpu as pltpu
from jax.sharding import PartitionSpec as P

BLOCK = 256
PANELS = 2
N = 16
NZ = 8
HIGH = lax.Precision.HIGHEST
F32 = jnp.float32
MESH = pl.DeviceIdType.MESH
VMEM = pl.BlockSpec(memory_space=pltpu.VMEM)


def dot(left, right, over=(1, 0)):
    return lax.dot_general(
        left,
        right,
        (((over[0],), (over[1],)), ((), ())),
        precision=HIGH,
        preferred_element_type=F32,
    )


def recip(x):
    r = pl.reciprocal(x, approx=True)
    return r * (2.0 - x * r)


def lanes(block, index):
    return jnp.take_along_axis(block, jnp.full((8, 128), index, jnp.int32), axis=1)


def times(scale, row):
    if row.shape[1] == 128:
        return scale * row
    return jnp.concatenate([scale * row[:, :128], scale * row[:, 128:]], axis=1)


def put(rows):
    sub = lax.broadcasted_iota(jnp.int32, rows[0].shape, 0)
    out = rows[0]
    for s in range(1, 8):
        out = jnp.where(sub == s, rows[s], out)
    return out


def group(aug, out, base, inverse):
    width = aug.shape[1]
    lane = lax.broadcasted_iota(jnp.int32, (8, 128), 1)
    inside = (lane >= base) & (lane < base + 8)

    def left(block, value):
        if width == 128:
            return jnp.where(inside, value, block)
        return jnp.concatenate([jnp.where(inside, value, block[:, :128]), block[:, 128:]], axis=1)

    rows = [jnp.broadcast_to(aug[pl.ds(base + s, 1), :], (8, width)) for s in range(8)]
    e = [[None] * 8 for _ in range(8)]
    for t in range(8):
        for s in range(8 if inverse else t + 1):
            e[s][t] = lanes(rows[s][:, :128], base + t)
    if inverse:
        rows = [left(rows[s], (lane == base + s).astype(F32)) for s in range(8)]
    inv = []
    for s in range(8):
        inv.append(recip(e[s][s]))
        for t in range(s + 1, 8):
            f = (e[t][s] if inverse else e[s][t]) * inv[s]
            for u in range(s + 1 if inverse else t, 8):
                e[t][u] = e[t][u] - f * e[s][u]
            rows[t] = rows[t] - times(f, rows[s])
    if not inverse:
        out[pl.ds(base, 8), :] = put([times(lax.rsqrt(e[s][s]), rows[s]) for s in range(8)])
    solved = [None] * 8
    for s in reversed(range(8)):
        acc = rows[s]
        for t in range(s + 1, 8):
            acc = acc - times(e[s][t], solved[t])
        solved[s] = times(inv[s], acc)
    own = put(solved)
    strip = pl.multiple_of(base // 32 * 32, 32)
    blocks = [aug[pl.ds(strip + 8 * k, 8), :] for k in range(4)]
    after = [left(b, 0.0) if inverse else b for b in blocks]
    for s in range(8):
        for k in range(4):
            after[k] = after[k] - times(lanes(blocks[k][:, :128], base + s), solved[s])
    for k in range(4):
        aug[pl.ds(strip + 8 * k, 8), :] = jnp.where(strip + 8 * k == base, own, after[k])


def strips(aug, out, lo, hi, inverse):
    row = lax.broadcasted_iota(jnp.int32, (128, 128), 0) // 32
    lane = lax.broadcasted_iota(jnp.int32, (128, 128), 1) // 32

    def one(k, q):
        group(aug, out, pl.multiple_of(32 * q + 8 * k, 8), inverse)
        return q

    def strip(q, carry):
        lax.fori_loop(0, 4, one, q)
        aim = (lane == q) & ((row != q) if inverse else (row > q))
        near = aug[:, :128]
        prod = dot(jnp.where(aim, near, 0.0), aug[...])
        if inverse:
            near = jnp.where(aim, 0.0, near)
        aug[:, :128] = near - prod[:, :128]
        if aug.shape[1] > 128:
            aug[:, 128:] = aug[:, 128:] - prod[:, 128:]
        return carry

    lax.fori_loop(lo, hi, strip, 0)


def remote(src, dst, send, recv, row, col):
    return pltpu.make_async_remote_copy(
        src_ref=src,
        dst_ref=dst,
        send_sem=send,
        recv_sem=recv,
        device_id=(row, col),
        device_id_type=MESH,
    )


def greet(r, c):
    barrier = pltpu.get_barrier_semaphore()
    for k in range(1, N):
        pl.semaphore_signal(barrier, inc=1, device_id=(r, lax.rem(c + k, N)), device_id_type=MESH)
        pl.semaphore_signal(barrier, inc=1, device_id=(lax.rem(r + k, N), c), device_id_type=MESH)
    pl.semaphore_wait(barrier, 2 * (N - 1))


def at(index, size):
    return pl.ds(pl.multiple_of(index * size, size), size)


def kernel(
    a_ref, out_ref,
    cur, pr, pct, pc, aer, aec, aepr, aepc, gram, gin, tsrc, tall, lt_ref, k_ref, n_ref, aug, aug2, low, zr, zc,
    wr, wc, m, inr, inm, iny, half, hsum, zin, xr, xc, mloc, mpair, mring, ball,
    ss, g_r, b_r, t_r, tm_r, p_r, q_r, ar_r, ac_r, r_r, m_r, yt_r, h_r, z_r, x_r, y_r, w_r, s_r, u_r, v_r, f_r,
):
    r, c = lax.axis_index("row"), lax.axis_index("col")
    z, core = r // 2, lax.rem(r, 2)
    other = 1 - core
    mate = r + 1 - 2 * core
    height = a_ref.shape[0]
    upper = lax.broadcasted_iota(jnp.int32, (128, 128), 0) <= lax.broadcasted_iota(
        jnp.int32, (128, 128), 1
    )
    plane = [lax.rem(c + k, N) for k in range(1, N)]
    line = [lax.rem(r + k, N) for k in range(1, N)]
    ring = [lax.rem(z + k, NZ) for k in range(1, NZ)]

    def got(ref, sem):
        remote(ref, ref, ss.at[0], sem, r, c).wait_recv()

    def when(cond, run):
        pl.when(cond)(run)

    cur[...] = a_ref[...]

    for p in range(PANELS):
        first, lead = p * BLOCK, (p + 1) * BLOCK
        owner, off = lead // height, lead % height
        count = iter(range(1, 480))

        def send(src, dst, sem, row, col):
            return remote(src, dst, ss.at[next(count)], sem, row, col)

        def start(copies):
            for copy in copies:
                copy.start()

        @pl.when(r == 0)
        def _():
            cols = c * height + lax.broadcasted_iota(jnp.int32, (BLOCK, height), 1)
            pct[...] = jnp.where(cols >= lead, cur[first : first + BLOCK, :], 0.0)
            gram[...] = dot(pct[...], pct[...], (1, 1))
            gin[p, c] = gram[at(c, 16), :]

        def slot(a, i, h):
            return tall.at[p, a, i, h]

        def pr_to(q, i):
            return send(pr.at[p, at(q, 32)], pr.at[p, at(q, 32)], p_r.at[p, q], r, i)

        def pc_to(q, row):
            return send(pc.at[p, at(q, 64)], pc.at[p, at(q, 64)], q_r.at[p, q], row, c)

        g_out = [send(gram.at[at(i, 16)], gin.at[p, c], g_r.at[p, c], r, i) for i in plane]
        top_out = [
            send(
                pr.at[p, pl.ds(pl.multiple_of(off + 16 * i + 8 * h, 8), 8)],
                tsrc.at[p, 1, h], b_r.at[p, 1, h], r, i,
            )
            for i in plane for h in (0, 1)
        ]
        ee_out = [
            send(
                aer.at[pl.ds(pl.multiple_of(off + 16 * i + 8 * h, 8), 8)],
                tsrc.at[p, 2, h], b_r.at[p, 2, h], r, i,
            )
            for i in plane for h in (0, 1)
        ]
        down = [
            [
                send(tsrc.at[p, a, lax.rem(i, 2)], slot(a, c, lax.rem(i, 2)), t_r.at[p, a, c, lax.rem(i, 2)], i, c)
                for i in line
            ]
            for a in range(3)
        ]
        share = [
            [send(slot(a, c, core), slot(a, c, core), t_r.at[p, a, c, core], r, i) for i in plane]
            for a in range(3)
        ]
        cross = [
            send(tall.at[p, a, :, core], tall.at[p, a, :, core], tm_r.at[p, a], mate, c)
            for a in range(3)
        ]
        root_r = [pr_to(i, i) for i in range(1, N)] + [pr_to(0, i) for i in range(1, N)]
        root_c = [pc_to(q, 2 * q) for q in range(1, NZ)] + [pc_to(0, 2 * q) for q in range(1, NZ)]
        root_c += [pc_to(q, 1) for q in range(NZ)]
        ae_r = [send(aer.at[at(i, 32)], aepr.at[p], ar_r.at[p], r, i) for i in plane]
        ae_c = [
            send(aec.at[at(lax.rem(i, 2) * NZ + i // 2, 32)], aepc.at[p], ac_r.at[p], i, c)
            for i in line
        ]
        ahead_r = [(i, pr_to(c, i)) for i in plane]
        ahead_c = [(q, pc_to(z, 2 * q)) for q in ring]
        low_c = [pc_to(z, r + 1)] + [pc_to(q, r + 1) for q in ring]
        relay = (core == 0) & (z != 0)

        @pl.when(c == 0)
        def _():
            rows = r * height + lax.broadcasted_iota(jnp.int32, (height, BLOCK), 0)
            pr[p] = jnp.where(rows >= lead, cur[:, first : first + BLOCK], 0.0)

        @pl.when(c == owner)
        def _():
            aer[...] = cur[:, off : off + BLOCK]
            aepr[p] = aer[at(c, 32), :]

        @pl.when(r == owner)
        def _():
            aec[...] = cur[off : off + BLOCK, :].T
            aepc[p] = aec[at(core * NZ + z, 32), :]

        if p == 0:
            greet(r, c)

        when(r == 0, lambda: start(g_out))

        @pl.when((r == owner) & (c == 0))
        def _():
            start(top_out)
            for h in (0, 1):
                tsrc[p, 1, h] = pr[p, pl.ds(pl.multiple_of(off + 16 * c + 8 * h, 8), 8), :]

        when((c == 0) & (r > 1), lambda: start(root_r))

        @pl.when((r == owner) & (c == owner))
        def _():
            start(ee_out)
            for h in (0, 1):
                tsrc[p, 2, h] = aer[pl.ds(pl.multiple_of(off + 16 * c + 8 * h, 8), 8), :]

        @pl.when(r == 0)
        def _():
            for i in plane:
                got(gin.at[p, i], g_r.at[p, i])
            total = gin[p, 0]
            for i in range(1, N):
                total = total + gin[p, i]
            tsrc[p, 0] = total.reshape(2, 8, BLOCK)
            tall[p, 0, c, core] = tsrc[p, 0, core]
            start(down[0])

        when(r != 0, lambda: got(slot(0, c, core), t_r.at[p, 0, c, core]))
        start(share[0])
        when((c == 0) & (r <= 1), lambda: start(root_r))

        @pl.when(r == 0)
        def _():
            pc[p] = pct[...].T
            start(root_c)

        @pl.when(c != 0)
        def _():
            got(pr.at[p, at(c, 32)], p_r.at[p, c])
            for i, copy in ahead_r:
                when(i != 0, copy.start)

        @pl.when(relay)
        def _():
            got(pc.at[p, at(z, 64)], q_r.at[p, z])
            for q, copy in ahead_c:
                when(q != 0, copy.start)
            low_c[0].start()


        @pl.when(r == owner)
        def _():
            for a, holder in ((1, 0), (2, owner)):

                @pl.when(c != holder)
                def _():
                    for h in (0, 1):
                        got(tsrc.at[p, a, h], b_r.at[p, a, h])

                tall[p, a, c, core] = tsrc[p, a, core]
                start(down[a])

        for i in plane:
            got(slot(0, i, core), t_r.at[p, 0, i, core])
        cross[0].start()

        for a in (1, 2):
            when(r != owner, lambda a=a: got(slot(a, c, core), t_r.at[p, a, c, core]))
            start(share[a])

        got(tall.at[p, 0, :, other], tm_r.at[p, 0])

        when(c == owner, lambda: start(ae_r))
        when(r == owner, lambda: start(ae_c))

        g = tall[p, 0].reshape(BLOCK, BLOCK)
        aug[...] = g[:128, :]
        strips(aug, lt_ref, 0, 4, False)
        lt_ref[:128, :128] = jnp.where(upper, lt_ref[:128, :128], 0.0)
        lt01 = lt_ref[:128, 128:]
        aug2[...] = g[128:, 128:] - dot(lt01, lt01, (0, 0))
        lt_ref[128:, :128] = jnp.zeros((128, 128), F32)

        @pl.when(relay)
        def _():
            for k in range(1, NZ):
                got(pc.at[p, at(ring[k - 1], 64)], q_r.at[p, ring[k - 1]])
                low_c[k].start()

        @pl.when(c != 0)
        def _():
            for i in plane:
                got(pr.at[p, at(i, 32)], p_r.at[p, i])

        sends = []

        def go(copy):
            copy.start()
            sends.append(copy)

        wc[...] = dot(cur[...], pr[p], (0, 0))
        swap = send(wc.at[at(other, 256)], half.at[p], h_r.at[p], mate, c)
        go(swap)

        @pl.when(core == 1)
        def _():
            for q in range(NZ):
                got(pc.at[p, at(q, 64)], q_r.at[p, q])

        wr[...] = dot(cur[...], pc[p])
        for i in plane:
            go(send(wr.at[at(i, 32)], inr.at[p, c], r_r.at[p, c], r, i))
        inr[p, c] = wr[at(c, 32), :]
        m[...] = dot(pr[p], wr[...], (0, 0))
        for i in plane:
            go(send(m.at[at(i, 16)], inm.at[p, c], m_r.at[p, c], r, i))
        inm[p, c] = m[at(c, 16), :]

        def top_rows(i):
            return pl.ds(pl.multiple_of(off + 16 * i, 16), 16)

        y_out = [send(wr.at[top_rows(i)], iny.at[p, c], yt_r.at[p, c], r, i) for i in plane]

        @pl.when(r == owner)
        def _():
            start(y_out)
            iny[p, c] = wr[top_rows(c), :]

        swap.wait_recv()
        hsum[...] = (wc[at(core, 256), :] + half[p]).reshape(NZ, 32, BLOCK)
        zin[p, z] = hsum[z]
        for q in ring:
            go(send(hsum.at[q], zin.at[p, z], z_r.at[p, z], 2 * q + core, c))

        strips(aug2, low, 0, 4, False)
        lt_ref[128:, 128:] = jnp.where(upper, low[...], 0.0)
        lt = lt_ref[...]

        for i in plane:
            got(inr.at[p, i], r_r.at[p, i])
        total = inr[p, 0]
        for i in range(1, N):
            total = total + inr[p, i]
        when(c != owner, lambda: got(aepr.at[p], ar_r.at[p]))
        xr[p, at(c, 32), :] = total + dot(aepr[p], lt)
        for i in plane:
            own = xr.at[p, at(c, 32)]
            go(send(own, own, x_r.at[p, c], r, i))
        for q in ring:
            got(zin.at[p, q], z_r.at[p, q])
        total = zin[p, 0]
        for q in range(1, NZ):
            total = total + zin[p, q]
        when(r != owner, lambda: got(aepc.at[p], ac_r.at[p]))
        spot = core * NZ + z
        xc[p, at(spot, 32), :] = total + dot(aepc[p], lt)
        own = xc.at[p, at(spot, 32)]
        for q in ring:
            go(send(own, own, y_r.at[p, z], 2 * q + core, c))
        go(send(own, own, w_r.at[p, z], mate, c))
        for i in plane:
            got(inm.at[p, i], m_r.at[p, i])
        total = inm[p, 0]
        for i in range(1, N):
            total = total + inm[p, i]
        mloc[0] = total.reshape(2, 8, BLOCK)

        @pl.when(r == owner)
        def _():
            for i in plane:
                got(iny.at[p, i], yt_r.at[p, i])
            total = iny[p, 0]
            for i in range(1, N):
                total = total + iny[p, i]
            mloc[1] = total.reshape(2, 8, BLOCK)

        @pl.when(r != owner)
        def _():
            mloc[1] = jnp.zeros((2, 8, BLOCK), F32)

        go(send(mloc.at[:, other], mpair.at[p], s_r.at[p], mate, c))

        for i in plane:
            got(slot(1, i, core), t_r.at[p, 1, i, core])
        cross[1].start()
        for i in plane:
            got(slot(2, i, core), t_r.at[p, 2, i, core])
        cross[2].start()
        got(mpair.at[p], s_r.at[p])
        mring[p, z] = mloc[:, core] + mpair[p]
        for q in ring:
            go(send(mring.at[p, z], mring.at[p, z], u_r.at[p, z], 2 * q + core, c))
        got(tall.at[p, 1, :, other], tm_r.at[p, 1])
        got(tall.at[p, 2, :, other], tm_r.at[p, 2])

        n_ref[...] = tall[p, 0].reshape(BLOCK, BLOCK) + dot(tall[p, 1].reshape(BLOCK, BLOCK), lt, (0, 0))
        aug[...] = n_ref[:128, :]
        strips(aug, None, 0, 4, True)

        for q in ring:
            got(mring.at[p, q], u_r.at[p, q])
        total = mring[p, 0]
        for q in range(1, NZ):
            total = total + mring[p, q]
        ball[p, :, c, core] = total
        own = ball.at[p, :, c, core]
        for i in plane:
            go(send(own, own, v_r.at[p, c], r, i))
        for q in ring:
            part = xc.at[p, at(core * NZ + q, 32)]
            got(part, y_r.at[p, q])
            go(send(part, part, w_r.at[p, q], mate, c))

        d0 = aug[:, :128]
        n01 = aug[:, 128:]
        n10d = dot(n_ref[128:, :128], d0)
        aug2[...] = n_ref[128:, 128:] - dot(n_ref[128:, :128], n01)
        strips(aug2, None, 0, 2, True)
        for i in plane:
            got(ball.at[p, :, i, core], v_r.at[p, i])
        final = ball.at[p, :, :, core]
        go(send(final, final, f_r.at[p], mate, c))
        strips(aug2, None, 2, 4, True)
        e = aug2[...]
        k10 = -dot(e, n10d)
        k_ref[:128, :128] = d0 - dot(n01, k10)
        k_ref[:128, 128:] = -dot(n01, e)
        k_ref[128:, :128] = k10
        k_ref[128:, 128:] = e

        zr[...] = pr[p]
        zc[...] = pc[p]

        @pl.when(r == owner)
        def _():
            zr[off : off + BLOCK, :] = zr[off : off + BLOCK, :] + lt_ref[...]

        @pl.when(c == owner)
        def _():
            zc[off : off + BLOCK, :] = zc[off : off + BLOCK, :] + lt_ref[...]

        for i in plane:
            got(xr.at[p, at(i, 32)], x_r.at[p, i])
        for q in range(NZ):
            got(xc.at[p, at(other * NZ + q, 32)], w_r.at[p, q])
        got(ball.at[p, :, :, other], f_r.at[p])

        ytop = ball[p, 1].reshape(BLOCK, BLOCK)
        xtop = ytop + dot(tall[p, 2].reshape(BLOCK, BLOCK), lt)
        inner = ball[p, 0].reshape(BLOCK, BLOCK) + dot(ytop, lt, (0, 0)) + dot(lt, xtop, (0, 0))
        coupled = 0.5 * dot(k_ref[...], dot(inner, k_ref[...]), (0, 0))
        ur = dot(xr[p], k_ref[...]) - dot(zr[...], coupled)
        uc = dot(xc[p], k_ref[...]) - dot(zc[...], coupled)
        dest = out_ref if p == PANELS - 1 else cur
        dest[...] = cur[...] - dot(ur, zc[...], (1, 1)) - dot(zr[...], uc, (1, 1))

        def left(copies):
            for copy in copies:
                copy.wait_send()

        left(share[0] + share[1] + share[2] + cross + sends)
        when(r == 0, lambda: left(g_out + down[0] + root_c))
        when(r == owner, lambda: left(down[1] + down[2] + ae_c + y_out))
        when((r == owner) & (c == 0), lambda: left(top_out))
        when((r == owner) & (c == owner), lambda: left(ee_out))
        when(c == 0, lambda: left(root_r))
        when(c == owner, lambda: left(ae_r))

        @pl.when(c != 0)
        def _():
            for i, copy in ahead_r:
                when(i != 0, copy.wait_send)

        @pl.when(relay)
        def _():
            for q, copy in ahead_c:
                when(q != 0, copy.wait_send)
            left(low_c)


def per_device(matrix):
    dma = pltpu.SemaphoreType.DMA

    def buf(*shape):
        return pltpu.VMEM(shape, F32)

    return pl.pallas_call(
        kernel,
        out_shape=jax.ShapeDtypeStruct(matrix.shape, F32),
        in_specs=[VMEM],
        out_specs=VMEM,
        scratch_shapes=[
            buf(512, 512),
            buf(2, 512, 256),
            buf(256, 512),
            buf(2, 512, 256),
            buf(512, 256),
            buf(512, 256),
            buf(2, 32, 256),
            buf(2, 32, 256),
            buf(256, 256),
            buf(2, N, 16, 256),
            buf(2, 3, 2, 8, 256),
            buf(2, 3, N, 2, 8, 256),
            buf(256, 256),
            buf(256, 256),
            buf(256, 256),
            buf(128, 256),
            buf(128, 128),
            buf(128, 128),
            buf(512, 256),
            buf(512, 256),
            buf(512, 256),
            buf(512, 256),
            buf(256, 256),
            buf(2, N, 32, 256),
            buf(2, N, 16, 256),
            buf(2, N, 16, 256),
            buf(2, 256, 256),
            buf(NZ, 32, 256),
            buf(2, NZ, 32, 256),
            buf(2, 512, 256),
            buf(2, 512, 256),
            buf(2, 2, 8, 256),
            buf(2, 2, 8, 256),
            buf(2, NZ, 2, 8, 256),
            buf(2, 2, N, 2, 8, 256),
            dma((480,)),
            dma((2, N)),
            dma((2, 3, 2)),
            dma((2, 3, N, 2)),
            dma((2, 3)),
            dma((2, N)),
            dma((2, NZ)),
            dma((2,)),
            dma((2,)),
            dma((2, N)),
            dma((2, N)),
            dma((2, N)),
            dma((2,)),
            dma((2, NZ)),
            dma((2, N)),
            dma((2, NZ)),
            dma((2, NZ)),
            dma((2,)),
            dma((2, NZ)),
            dma((2, N)),
            dma((2,)),
        ],
        compiler_params=pltpu.CompilerParams(collective_id=0, has_side_effects=True),
        name="reduce_panels",
    )(matrix)


def solution(mesh):
    return jax.shard_map(
        per_device, mesh=mesh, in_specs=(P("row", "col"),), out_specs=P("row", "col"), check_vma=False
    )
```

```python
import jax
import jax.numpy as jnp
from jax import lax
from jax.experimental import pallas as pl
from jax.experimental.pallas import tpu as pltpu
from jax.sharding import PartitionSpec as P

BLOCK = 256
PANELS = 2
N = 16
NZ = 8
HIGH = lax.Precision.HIGHEST
F32 = jnp.float32
MESH = pl.DeviceIdType.MESH
VMEM = pl.BlockSpec(memory_space=pltpu.VMEM)


def dot(left, right, over=(1, 0)):
    return lax.dot_general(
        left,
        right,
        (((over[0],), (over[1],)), ((), ())),
        precision=HIGH,
        preferred_element_type=F32,
    )


def recip(x):
    r = pl.reciprocal(x, approx=True)
    return r * (2.0 - x * r)


def lanes(block, index):
    return jnp.take_along_axis(block, jnp.full((8, 128), index, jnp.int32), axis=1)


def times(scale, row):
    if row.shape[1] == 128:
        return scale * row
    return jnp.concatenate([scale * row[:, :128], scale * row[:, 128:]], axis=1)


def put(rows):
    sub = lax.broadcasted_iota(jnp.int32, rows[0].shape, 0)
    out = rows[0]
    for s in range(1, 8):
        out = jnp.where(sub == s, rows[s], out)
    return out


def group(aug, out, base, inverse):
    width = aug.shape[1]
    lane = lax.broadcasted_iota(jnp.int32, (8, 128), 1)
    inside = (lane >= base) & (lane < base + 8)

    def left(block, value):
        if width == 128:
            return jnp.where(inside, value, block)
        return jnp.concatenate([jnp.where(inside, value, block[:, :128]), block[:, 128:]], axis=1)

    rows = [jnp.broadcast_to(aug[pl.ds(base + s, 1), :], (8, width)) for s in range(8)]
    e = [[None] * 8 for _ in range(8)]
    for t in range(8):
        for s in range(8 if inverse else t + 1):
            e[s][t] = lanes(rows[s][:, :128], base + t)
    if inverse:
        rows = [left(rows[s], (lane == base + s).astype(F32)) for s in range(8)]
    inv = []
    for s in range(8):
        inv.append(recip(e[s][s]))
        for t in range(s + 1, 8):
            f = (e[t][s] if inverse else e[s][t]) * inv[s]
            for u in range(s + 1 if inverse else t, 8):
                e[t][u] = e[t][u] - f * e[s][u]
            rows[t] = rows[t] - times(f, rows[s])
    if not inverse:
        out[pl.ds(base, 8), :] = put([times(lax.rsqrt(e[s][s]), rows[s]) for s in range(8)])
    solved = [None] * 8
    for s in reversed(range(8)):
        acc = rows[s]
        for t in range(s + 1, 8):
            acc = acc - times(e[s][t], solved[t])
        solved[s] = times(inv[s], acc)
    own = put(solved)
    strip = pl.multiple_of(base // 32 * 32, 32)
    blocks = [aug[pl.ds(strip + 8 * k, 8), :] for k in range(4)]
    after = [left(b, 0.0) if inverse else b for b in blocks]
    for s in range(8):
        for k in range(4):
            after[k] = after[k] - times(lanes(blocks[k][:, :128], base + s), solved[s])
    for k in range(4):
        aug[pl.ds(strip + 8 * k, 8), :] = jnp.where(strip + 8 * k == base, own, after[k])


def strips(aug, out, lo, hi, inverse):
    row = lax.broadcasted_iota(jnp.int32, (128, 128), 0) // 32
    lane = lax.broadcasted_iota(jnp.int32, (128, 128), 1) // 32

    def one(k, q):
        group(aug, out, pl.multiple_of(32 * q + 8 * k, 8), inverse)
        return q

    def strip(q, carry):
        lax.fori_loop(0, 4, one, q)
        aim = (lane == q) & ((row != q) if inverse else (row > q))
        near = aug[:, :128]
        prod = dot(jnp.where(aim, near, 0.0), aug[...])
        if inverse:
            near = jnp.where(aim, 0.0, near)
        aug[:, :128] = near - prod[:, :128]
        if aug.shape[1] > 128:
            aug[:, 128:] = aug[:, 128:] - prod[:, 128:]
        return carry

    lax.fori_loop(lo, hi, strip, 0)


def remote(src, dst, send, recv, row, col):
    return pltpu.make_async_remote_copy(
        src_ref=src,
        dst_ref=dst,
        send_sem=send,
        recv_sem=recv,
        device_id=(row, col),
        device_id_type=MESH,
    )


def greet(r, c):
    barrier = pltpu.get_barrier_semaphore()
    for k in range(1, N):
        pl.semaphore_signal(barrier, inc=1, device_id=(r, lax.rem(c + k, N)), device_id_type=MESH)
        pl.semaphore_signal(barrier, inc=1, device_id=(lax.rem(r + k, N), c), device_id_type=MESH)
    pl.semaphore_wait(barrier, 2 * (N - 1))


def at(index, size):
    return pl.ds(pl.multiple_of(index * size, size), size)


def kernel(
    a_ref, out_ref,
    cur, pr, pct, pc, aer, aec, aepr, aepc, aefr, aefc, gram, gin, tsrc, tall, lt_ref, k_ref, n_ref, aug, aug2, low,
    zr, zc, wr, wc, m, mpair, mh, ybuf, yin, inr, inm, iny, half, hsum, zin, xr, xc, mring, ball,
    ss, g_r, b_r, t_r, tm_r, p_r, q_r, ar_r, ac_r, af_r, ag_r, am_r,
    r_r, m_r, yt_r, ys_r, h_r, z_r, x_r, y_r, w_r, s_r, u_r, v_r, f_r,
):
    r, c = lax.axis_index("row"), lax.axis_index("col")
    z, core = r // 2, lax.rem(r, 2)
    other = 1 - core
    mate = r + 1 - 2 * core
    height = a_ref.shape[0]
    upper = lax.broadcasted_iota(jnp.int32, (128, 128), 0) <= lax.broadcasted_iota(
        jnp.int32, (128, 128), 1
    )
    plane = [lax.rem(c + k, N) for k in range(1, N)]
    line = [lax.rem(r + k, N) for k in range(1, N)]
    ring = [lax.rem(z + k, NZ) for k in range(1, NZ)]

    def got(ref, sem):
        remote(ref, ref, ss.at[0], sem, r, c).wait_recv()

    def when(cond, run):
        pl.when(cond)(run)

    cur[...] = a_ref[...]
    zown = 0

    for p in range(PANELS):
        first, lead = p * BLOCK, (p + 1) * BLOCK
        owner, off = lead // height, lead % height
        count = iter(range(1, 480))
        sends = []

        def send(src, dst, sem, row, col):
            return remote(src, dst, ss.at[next(count)], sem, row, col)

        def start(copies):
            for copy in copies:
                copy.start()

        def go(copy):
            copy.start()
            sends.append(copy)

        def slot(a, i, h):
            return tall.at[p, a, i, h]

        def pr_to(q, i):
            return send(pr.at[p, at(q, 32)], pr.at[p, at(q, 32)], p_r.at[q], r, i)

        def pc_to(q, row):
            return send(pc.at[p, at(q, 64)], pc.at[p, at(q, 64)], q_r.at[q], row, c)

        def aer_at(i):
            return aefr.at[at(i, 32)] if p == 0 else aepr

        def aec_at(i):
            return aefc.at[at(i, 32)] if p == 0 else aepc

        spot = core * NZ + z

        if p == 0:

            @pl.when(r == 0)
            def _():
                cols = c * height + lax.broadcasted_iota(jnp.int32, (BLOCK, height), 1)
                pct[...] = jnp.where(cols >= lead, cur[first : first + BLOCK, :], 0.0)
                gram[...] = dot(pct[...], pct[...], (1, 1))
                gin[p, c] = gram[at(c, 16), :]

            @pl.when(c == 0)
            def _():
                rows = r * height + lax.broadcasted_iota(jnp.int32, (height, BLOCK), 0)
                pr[p] = jnp.where(rows >= lead, cur[:, first : first + BLOCK], 0.0)

        else:

            @pl.when(r == 0)
            def _():
                gram[...] = dot(pc[p], pc[p], (0, 0))
                gin[p, c] = gram[at(c, 16), :]

        g_out = [send(gram.at[at(i, 16)], gin.at[p, c], g_r.at[p, c], r, i) for i in plane]
        top_out = [
            send(
                pr.at[p, pl.ds(pl.multiple_of(off + 16 * i + 8 * h, 8), 8)],
                tsrc.at[p, 1, h], b_r.at[p, 1, h], r, i,
            )
            for i in plane for h in (0, 1)
        ]
        ee_out = [
            send(
                aer.at[pl.ds(pl.multiple_of(off + 16 * i + 8 * h, 8), 8)],
                tsrc.at[p, 2, h], b_r.at[p, 2, h], r, i,
            )
            for i in plane for h in (0, 1)
        ]
        down = [
            [
                send(tsrc.at[p, a, lax.rem(i, 2)], slot(a, c, lax.rem(i, 2)), t_r.at[p, a, c, lax.rem(i, 2)], i, c)
                for i in line
            ]
            for a in range(3)
        ]
        share = [
            [send(slot(a, c, core), slot(a, c, core), t_r.at[p, a, c, core], r, i) for i in plane]
            for a in range(3)
        ]
        cross = [
            send(tall.at[p, a, :, core], tall.at[p, a, :, core], tm_r.at[p, a], mate, c)
            for a in range(3)
        ]
        ae_r = [send(aer.at[at(i, 32)], aer_at(i), ar_r.at[p], r, i) for i in plane]
        ae_c = [
            send(aec.at[at(lax.rem(i, 2) * NZ + i // 2, 32)], aec_at(lax.rem(i, 2) * NZ + i // 2), ac_r.at[p], i, c)
            for i in line
        ]
        relay = (core == 0) & (z != 0)
        if p == 0:
            root_r = [pr_to(i, i) for i in range(1, N)] + [pr_to(0, i) for i in range(1, N)]
            root_c = [pc_to(q, 2 * q) for q in range(1, NZ)] + [pc_to(0, 2 * q) for q in range(1, NZ)]
            root_c += [pc_to(q, 1) for q in range(NZ)]
            ahead_r = [(i, pr_to(c, i)) for i in plane]
            ahead_c = [(q, pc_to(z, 2 * q)) for q in ring]
            low_c = [pc_to(z, r + 1)] + [pc_to(q, r + 1) for q in ring]

        @pl.when(c == owner)
        def _():
            aer[...] = cur[:, off : off + BLOCK]
            mine = aer[at(c, 32), :]
            if p == 0:
                aefr[at(c, 32), :] = mine
            else:
                aepr[...] = mine

        @pl.when(r == owner)
        def _():
            aec[...] = cur[off : off + BLOCK, :].T
            mine = aec[at(spot, 32), :]
            if p == 0:
                aefc[at(spot, 32), :] = mine
            else:
                aepc[...] = mine

        if p == 0:
            greet(r, c)

        when(r == 0, lambda: start(g_out))

        @pl.when((r == owner) & (c == 0))
        def _():
            start(top_out)
            for h in (0, 1):
                tsrc[p, 1, h] = pr[p, pl.ds(pl.multiple_of(off + 16 * c + 8 * h, 8), 8), :]

        if p == 0:
            when((c == 0) & (r > 1), lambda: start(root_r))

        @pl.when((r == owner) & (c == owner))
        def _():
            start(ee_out)
            for h in (0, 1):
                tsrc[p, 2, h] = aer[pl.ds(pl.multiple_of(off + 16 * c + 8 * h, 8), 8), :]

        swap = send(wc.at[at(other, 256)], half.at[p], h_r.at[p], mate, c)
        mswap = send(m.at[:, other], mpair.at[p], s_r.at[p], mate, c)
        yswap = send(ybuf.at[:, other], yin.at[p], ys_r.at[p], mate, c)
        y_own = [send(ybuf.at[i, core], iny.at[p, c], yt_r.at[p, c], r, i) for i in plane]
        y_mate = [send(yin.at[p, i], iny.at[p, c], yt_r.at[p, c], r, i) for i in plane]

        def products():
            wc[...] = dot(cur[...], pr[p], (0, 0))
            go(swap)
            wr[...] = dot(cur[...], pc[p])

            @pl.when(r == owner)
            def _():
                ybuf[...] = wr[off : off + BLOCK, :].reshape(N, 2, 8, BLOCK)
                yswap.start()

            m[...] = dot(pr[p], wr[...], (0, 0)).reshape(N, 2, 8, BLOCK)
            go(mswap)

        def scatter():
            mswap.wait_recv()
            mh[...] = m[:, core] + mpair[p]
            for i in plane:
                go(send(mh.at[i], inm.at[p, c], m_r.at[p, c], r, i))
            inm[p, c] = mh[c]

            @pl.when(r == owner)
            def _():
                start(y_own)
                iny[p, c] = ybuf[c, core]

            @pl.when(mate == owner)
            def _():
                yswap.wait_recv()
                start(y_mate)
                iny[p, c] = yin[p, c]

            for i in plane:
                go(send(wr.at[at(i, 32)], inr.at[p, c], r_r.at[p, c], r, i))
            inr[p, c] = wr[at(c, 32), :]
            swap.wait_recv()
            hsum[...] = (wc[at(core, 256), :] + half[p]).reshape(NZ, 32, BLOCK)
            zin[p, z] = hsum[z]
            for q in ring:
                go(send(hsum.at[q], zin.at[p, z], z_r.at[p, z], 2 * q + core, c))

        if p > 0:
            products()

        @pl.when(r == 0)
        def _():
            for i in plane:
                got(gin.at[p, i], g_r.at[p, i])
            total = gin[p, 0]
            for i in range(1, N):
                total = total + gin[p, i]
            tsrc[p, 0] = total.reshape(2, 8, BLOCK)
            tall[p, 0, c, core] = tsrc[p, 0, core]
            start(down[0])

        when(r != 0, lambda: got(slot(0, c, core), t_r.at[p, 0, c, core]))
        start(share[0])

        if p == 0:
            when((c == 0) & (r <= 1), lambda: start(root_r))

            @pl.when(r == 0)
            def _():
                pc[p] = pct[...].T
                start(root_c)

            @pl.when(relay)
            def _():
                got(pc.at[p, at(z, 64)], q_r.at[z])
                for q, copy in ahead_c:
                    when(q != 0, copy.start)
                low_c[0].start()

        @pl.when(r == owner)
        def _():
            for a, holder in ((1, 0), (2, owner)):

                @pl.when(c != holder)
                def _():
                    for h in (0, 1):
                        got(tsrc.at[p, a, h], b_r.at[p, a, h])

                tall[p, a, c, core] = tsrc[p, a, core]
                start(down[a])

        for i in plane:
            got(slot(0, i, core), t_r.at[p, 0, i, core])
        cross[0].start()

        if p == 0:

            @pl.when(c != 0)
            def _():
                got(pr.at[p, at(c, 32)], p_r.at[c])
                for i, copy in ahead_r:
                    when(i != 0, copy.start)

        else:
            scatter()

        for a in (1, 2):
            when(r != owner, lambda a=a: got(slot(a, c, core), t_r.at[p, a, c, core]))
            start(share[a])

        when(c == owner, lambda: start(ae_r))
        when(r == owner, lambda: start(ae_c))
        got(tall.at[p, 0, :, other], tm_r.at[p, 0])

        g = tall[p, 0].reshape(BLOCK, BLOCK)
        aug[...] = g[:128, :]
        strips(aug, lt_ref, 0, 4, False)
        lt_ref[:128, :128] = jnp.where(upper, lt_ref[:128, :128], 0.0)
        lt01 = lt_ref[:128, 128:]
        aug2[...] = g[128:, 128:] - dot(lt01, lt01, (0, 0))
        lt_ref[128:, :128] = jnp.zeros((128, 128), F32)

        if p == 0:

            @pl.when(relay)
            def _():
                for k in range(1, NZ):
                    got(pc.at[p, at(ring[k - 1], 64)], q_r.at[ring[k - 1]])
                    low_c[k].start()

            @pl.when(c != 0)
            def _():
                for i in plane:
                    got(pr.at[p, at(i, 32)], p_r.at[i])

            @pl.when(core == 1)
            def _():
                for q in range(NZ):
                    got(pc.at[p, at(q, 64)], q_r.at[q])

            products()
            scatter()

        for a in (1, 2):
            for i in plane:
                got(slot(a, i, core), t_r.at[p, a, i, core])
            cross[a].start()

        strips(aug2, low, 0, 4, False)
        lt_ref[128:, 128:] = jnp.where(upper, low[...], 0.0)
        lt = lt_ref[...]

        def sums():
            for i in plane:
                got(inm.at[p, i], m_r.at[p, i])
            total = inm[p, 0]
            for i in range(1, N):
                total = total + inm[p, i]
            mring[p, z, 0] = total

            @pl.when(z == zown)
            def _():
                for i in plane:
                    got(iny.at[p, i], yt_r.at[p, i])
                total = iny[p, 0]
                for i in range(1, N):
                    total = total + iny[p, i]
                mring[p, z, 1] = total

            @pl.when(z != zown)
            def _():
                mring[p, z, 1] = jnp.zeros((8, BLOCK), F32)

            for q in ring:
                go(send(mring.at[p, z], mring.at[p, z], u_r.at[p, z], 2 * q + core, c))
            for i in plane:
                got(inr.at[p, i], r_r.at[p, i])
            total = inr[p, 0]
            for i in range(1, N):
                total = total + inr[p, i]
            mine = aer_at(c)
            when(c != owner, lambda: got(mine, ar_r.at[p]))
            xr[p, at(c, 32), :] = total + dot(mine[...], lt)
            own = xr.at[p, at(c, 32)]
            for i in plane:
                go(send(own, own, x_r.at[p, c], r, i))
            for q in ring:
                got(zin.at[p, q], z_r.at[p, q])
            total = zin[p, 0]
            for q in range(1, NZ):
                total = total + zin[p, q]
            mine = aec_at(spot)
            when(r != owner, lambda: got(mine, ac_r.at[p]))
            xc[p, at(spot, 32), :] = total + dot(mine[...], lt)
            own = xc.at[p, at(spot, 32)]
            for q in ring:
                go(send(own, own, y_r.at[p, z], 2 * q + core, c))
            go(send(own, own, w_r.at[p, z], mate, c))
            if p == 0:
                own = aefc.at[at(spot, 32)]
                for q in ring:
                    go(send(own, own, ag_r.at[z], 2 * q + core, c))
                go(send(own, own, am_r.at[z], mate, c))
                own = aefr.at[at(c, 32)]
                for i in plane:
                    go(send(own, own, af_r.at[c], r, i))

        if p > 0:
            sums()

        got(tall.at[p, 1, :, other], tm_r.at[p, 1])
        top = tall[p, 1].reshape(BLOCK, BLOCK)
        n_ref[...] = tall[p, 0].reshape(BLOCK, BLOCK) + dot(top, lt, (0, 0))
        aug[...] = n_ref[:128, :]
        strips(aug, None, 0, 4, True)

        if p == 0:
            sums()

        d0 = aug[:, :128]
        n01 = aug[:, 128:]
        n10d = dot(n_ref[128:, :128], d0)
        aug2[...] = n_ref[128:, 128:] - dot(n_ref[128:, :128], n01)
        if p == 0:
            strips(aug2, None, 0, 2, True)

        for q in ring:
            got(mring.at[p, q], u_r.at[p, q])
        total = mring[p, 0]
        for q in range(1, NZ):
            total = total + mring[p, q]
        ball[p, :, c, core] = total
        own_b = ball.at[p, :, c, core]
        for i in plane:
            go(send(own_b, own_b, v_r.at[p, c], r, i))
        for q in ring:
            part = xc.at[p, at(core * NZ + q, 32)]
            got(part, y_r.at[p, q])
            go(send(part, part, w_r.at[p, q], mate, c))

        strips(aug2, None, 2 if p == 0 else 0, 4, True)
        e = aug2[...]
        k10 = -dot(e, n10d)
        k_ref[:128, :128] = d0 - dot(n01, k10)
        k_ref[:128, 128:] = -dot(n01, e)
        k_ref[128:, :128] = k10
        k_ref[128:, 128:] = e

        if p == 0:
            for q in ring:
                part = aefc.at[at(core * NZ + q, 32)]
                got(part, ag_r.at[q])
                go(send(part, part, am_r.at[q], mate, c))

        zr[...] = pr[p]
        zc[...] = pc[p]

        @pl.when(r == owner)
        def _():
            zr[off : off + BLOCK, :] = zr[off : off + BLOCK, :] + lt_ref[...]

        @pl.when(c == owner)
        def _():
            zc[off : off + BLOCK, :] = zc[off : off + BLOCK, :] + lt_ref[...]

        got(tall.at[p, 2, :, other], tm_r.at[p, 2])
        for i in plane:
            got(ball.at[p, :, i, core], v_r.at[p, i])
        final = ball.at[p, :, :, core]
        go(send(final, final, f_r.at[p], mate, c))
        for i in plane:
            got(xr.at[p, at(i, 32)], x_r.at[p, i])
        for q in range(NZ):
            got(xc.at[p, at(other * NZ + q, 32)], w_r.at[p, q])
        got(ball.at[p, :, :, other], f_r.at[p])

        ytop = ball[p, 1].reshape(BLOCK, BLOCK)
        xtop = ytop + dot(tall[p, 2].reshape(BLOCK, BLOCK), lt)
        inner = ball[p, 0].reshape(BLOCK, BLOCK) + dot(ytop, lt, (0, 0)) + dot(lt, xtop, (0, 0))
        coupled = 0.5 * dot(k_ref[...], dot(inner, k_ref[...]), (0, 0))
        ur = dot(xr[p], k_ref[...]) - dot(zr[...], coupled)
        uc = dot(xc[p], k_ref[...]) - dot(zc[...], coupled)
        dest = out_ref if p == PANELS - 1 else cur
        dest[...] = cur[...] - dot(ur, zc[...], (1, 1)) - dot(zr[...], uc, (1, 1))
        if p == 0:
            ztop = top + lt
            utop = dot(xtop, k_ref[...]) - dot(ztop, coupled)
            rows = lax.broadcasted_iota(jnp.int32, (height, BLOCK), 0)
            for i in plane:
                got(aefr.at[at(i, 32)], af_r.at[i])
            near = aefr[...] - dot(ur, ztop, (1, 1)) - dot(zr[...], utop, (1, 1))
            pr[1] = jnp.where(r * height + rows >= lead + BLOCK, near, 0.0)
            for q in range(NZ):
                got(aefc.at[at(other * NZ + q, 32)], am_r.at[q])
            near = aefc[...] - dot(uc, ztop, (1, 1)) - dot(zc[...], utop, (1, 1))
            pc[1] = jnp.where(c * height + rows >= lead + BLOCK, near, 0.0)

        def left(copies):
            for copy in copies:
                copy.wait_send()

        left(share[0] + share[1] + share[2] + cross + sends)
        when(r == 0, lambda: left(g_out + down[0]))
        when(r == owner, lambda: left(down[1] + down[2] + ae_c + y_own + [yswap]))
        when(mate == owner, lambda: left(y_mate))
        when((r == owner) & (c == 0), lambda: left(top_out))
        when((r == owner) & (c == owner), lambda: left(ee_out))
        when(c == owner, lambda: left(ae_r))
        if p == 0:
            when(r == 0, lambda: left(root_c))
            when(c == 0, lambda: left(root_r))

            @pl.when(c != 0)
            def _():
                for i, copy in ahead_r:
                    when(i != 0, copy.wait_send)

            @pl.when(relay)
            def _():
                for q, copy in ahead_c:
                    when(q != 0, copy.wait_send)
                left(low_c)


def per_device(matrix):
    dma = pltpu.SemaphoreType.DMA

    def buf(*shape):
        return pltpu.VMEM(shape, F32)

    return pl.pallas_call(
        kernel,
        out_shape=jax.ShapeDtypeStruct(matrix.shape, F32),
        in_specs=[VMEM],
        out_specs=VMEM,
        scratch_shapes=[
            buf(512, 512),
            buf(2, 512, 256),
            buf(256, 512),
            buf(2, 512, 256),
            buf(512, 256),
            buf(512, 256),
            buf(32, 256),
            buf(32, 256),
            buf(512, 256),
            buf(512, 256),
            buf(256, 256),
            buf(2, N, 16, 256),
            buf(2, 3, 2, 8, 256),
            buf(2, 3, N, 2, 8, 256),
            buf(256, 256),
            buf(256, 256),
            buf(256, 256),
            buf(128, 256),
            buf(128, 128),
            buf(128, 128),
            buf(512, 256),
            buf(512, 256),
            buf(512, 256),
            buf(512, 256),
            buf(N, 2, 8, 256),
            buf(2, N, 8, 256),
            buf(N, 8, 256),
            buf(N, 2, 8, 256),
            buf(2, N, 8, 256),
            buf(2, N, 32, 256),
            buf(2, N, 8, 256),
            buf(2, N, 8, 256),
            buf(2, 256, 256),
            buf(NZ, 32, 256),
            buf(2, NZ, 32, 256),
            buf(2, 512, 256),
            buf(2, 512, 256),
            buf(2, NZ, 2, 8, 256),
            buf(2, 2, N, 2, 8, 256),
            dma((480,)),
            dma((2, N)),
            dma((2, 3, 2)),
            dma((2, 3, N, 2)),
            dma((2, 3)),
            dma((N,)),
            dma((NZ,)),
            dma((2,)),
            dma((2,)),
            dma((N,)),
            dma((NZ,)),
            dma((NZ,)),
            dma((2, N)),
            dma((2, N)),
            dma((2, N)),
            dma((2,)),
            dma((2,)),
            dma((2, NZ)),
            dma((2, N)),
            dma((2, NZ)),
            dma((2, NZ)),
            dma((2,)),
            dma((2, NZ)),
            dma((2, N)),
            dma((2,)),
        ],
        compiler_params=pltpu.CompilerParams(collective_id=0, has_side_effects=True),
        name="reduce_panels",
    )(matrix)


def solution(mesh):
    return jax.shard_map(
        per_device, mesh=mesh, in_specs=(P("row", "col"),), out_specs=P("row", "col"), check_vma=False
    )
```

```python
import jax
import jax.numpy as jnp
from jax import lax
from jax.experimental import pallas as pl
from jax.experimental.pallas import tpu as pltpu
from jax.sharding import PartitionSpec as P

BLOCK = 256
PANELS = 2
N = 16
NZ = 8
HIGH = lax.Precision.HIGHEST
F32 = jnp.float32
MESH = pl.DeviceIdType.MESH
VMEM = pl.BlockSpec(memory_space=pltpu.VMEM)


def dot(left, right, over=(1, 0)):
    return lax.dot_general(
        left,
        right,
        (((over[0],), (over[1],)), ((), ())),
        precision=HIGH,
        preferred_element_type=F32,
    )


def dot3(left, right, over=(1, 0)):
    def split(x):
        high = x.astype(jnp.bfloat16)
        return high, (x - high.astype(F32)).astype(jnp.bfloat16)

    def part(a, b):
        return lax.dot_general(
            a, b, (((over[0],), (over[1],)), ((), ())), preferred_element_type=F32
        )

    lh, ll = split(left)
    rh, rl = split(right)
    return part(lh, rh) + (part(lh, rl) + part(ll, rh))


def recip(x):
    r = pl.reciprocal(x, approx=True)
    return r * (2.0 - x * r)


def lanes(block, index):
    return jnp.take_along_axis(block, jnp.full((8, 128), index, jnp.int32), axis=1)


def times(scale, row):
    if row.shape[1] == 128:
        return scale * row
    return jnp.concatenate([scale * row[:, :128], scale * row[:, 128:]], axis=1)


def put(rows):
    sub = lax.broadcasted_iota(jnp.int32, rows[0].shape, 0)
    out = rows[0]
    for s in range(1, 8):
        out = jnp.where(sub == s, rows[s], out)
    return out


def group(aug, out, base, inverse):
    width = aug.shape[1]
    lane = lax.broadcasted_iota(jnp.int32, (8, 128), 1)
    inside = (lane >= base) & (lane < base + 8)

    def left(block, value):
        if width == 128:
            return jnp.where(inside, value, block)
        return jnp.concatenate([jnp.where(inside, value, block[:, :128]), block[:, 128:]], axis=1)

    rows = [jnp.broadcast_to(aug[pl.ds(base + s, 1), :], (8, width)) for s in range(8)]
    e = [[None] * 8 for _ in range(8)]
    for t in range(8):
        for s in range(8 if inverse else t + 1):
            e[s][t] = lanes(rows[s][:, :128], base + t)
    if inverse:
        rows = [left(rows[s], (lane == base + s).astype(F32)) for s in range(8)]
    inv = []
    for s in range(8):
        inv.append(recip(e[s][s]))
        for t in range(s + 1, 8):
            f = (e[t][s] if inverse else e[s][t]) * inv[s]
            for u in range(s + 1 if inverse else t, 8):
                e[t][u] = e[t][u] - f * e[s][u]
            rows[t] = rows[t] - times(f, rows[s])
    if not inverse:
        out[pl.ds(base, 8), :] = put([times(lax.rsqrt(e[s][s]), rows[s]) for s in range(8)])
    solved = [None] * 8
    for s in reversed(range(8)):
        acc = rows[s]
        for t in range(s + 1, 8):
            acc = acc - times(e[s][t], solved[t])
        solved[s] = times(inv[s], acc)
    own = put(solved)
    strip = pl.multiple_of(base // 32 * 32, 32)
    blocks = [aug[pl.ds(strip + 8 * k, 8), :] for k in range(4)]
    after = [left(b, 0.0) if inverse else b for b in blocks]
    for s in range(8):
        for k in range(4):
            after[k] = after[k] - times(lanes(blocks[k][:, :128], base + s), solved[s])
    for k in range(4):
        aug[pl.ds(strip + 8 * k, 8), :] = jnp.where(strip + 8 * k == base, own, after[k])


def strips(aug, out, lo, hi, inverse):
    row = lax.broadcasted_iota(jnp.int32, (128, 128), 0) // 32
    lane = lax.broadcasted_iota(jnp.int32, (128, 128), 1) // 32

    def one(k, q):
        group(aug, out, pl.multiple_of(32 * q + 8 * k, 8), inverse)
        return q

    def strip(q, carry):
        lax.fori_loop(0, 4, one, q)
        aim = (lane == q) & ((row != q) if inverse else (row > q))
        near = aug[:, :128]
        prod = dot(jnp.where(aim, near, 0.0), aug[...])
        if inverse:
            near = jnp.where(aim, 0.0, near)
        aug[:, :128] = near - prod[:, :128]
        if aug.shape[1] > 128:
            aug[:, 128:] = aug[:, 128:] - prod[:, 128:]
        return carry

    lax.fori_loop(lo, hi, strip, 0)


def remote(src, dst, send, recv, row, col):
    return pltpu.make_async_remote_copy(
        src_ref=src,
        dst_ref=dst,
        send_sem=send,
        recv_sem=recv,
        device_id=(row, col),
        device_id_type=MESH,
    )


def greet(r, c):
    barrier = pltpu.get_barrier_semaphore()
    for k in range(1, N):
        pl.semaphore_signal(barrier, inc=1, device_id=(r, lax.rem(c + k, N)), device_id_type=MESH)
        pl.semaphore_signal(barrier, inc=1, device_id=(lax.rem(r + k, N), c), device_id_type=MESH)
    pl.semaphore_wait(barrier, 2 * (N - 1))


def at(index, size):
    return pl.ds(pl.multiple_of(index * size, size), size)


def kernel(
    a_ref, out_ref,
    cur, pr, pct, pc, aer, aec, aepr, aepc, aefr, aefc, gram, gin, tsrc, tall, lt_ref, k_ref, n_ref, aug, aug2, low,
    zr, zc, wr, wc, m, mpair, mh, ybuf, yin, inr, inm, iny, half, hsum, zin, xr, xc, mring, ball,
    ux, uy,
    ss, g_r, b_r, td_r, t_r, tm_r, pa_r, p_r, qa_r, q_r, ql_r, ar_r, ac_r, af_r, ag_r, am_r,
    r_r, m_r, yt_r, ys_r, h_r, z_r, x_r, y_r, w_r, s_r, u_r, v_r, f_r,
):
    r, c = lax.axis_index("row"), lax.axis_index("col")
    z, core = r // 2, lax.rem(r, 2)
    other = 1 - core
    mate = r + 1 - 2 * core
    height = a_ref.shape[0]
    upper = lax.broadcasted_iota(jnp.int32, (128, 128), 0) <= lax.broadcasted_iota(
        jnp.int32, (128, 128), 1
    )
    plane = [lax.rem(c + k, N) for k in range(1, N)]
    line = [lax.rem(r + k, N) for k in range(1, N)]
    ring = [lax.rem(z + k, NZ) for k in range(1, NZ)]

    def got(ref, sem):
        remote(ref, ref, ss.at[0], sem, r, c).wait_recv()

    def when(cond, run):
        pl.when(cond)(run)

    cur[...] = a_ref[...]
    zown = 0

    for p in range(PANELS):
        first, lead = p * BLOCK, (p + 1) * BLOCK
        owner, off = lead // height, lead % height
        count = iter(range(1, 60))
        sends = []

        class Group:
            def __init__(self, rows):
                self.sem = ss.at[next(count)]
                self.rows = rows
                self.copies = []

            def add(self, src, dst, sem, row, col):
                self.copies.append(remote(src, dst, self.sem, sem, row, col))
                return self.copies[-1]

            def start(self):
                for copy in self.copies:
                    copy.start()

            def left(self):
                if self.rows <= 512:
                    view = wc.at[pl.ds(0, self.rows)]
                else:
                    view = pr.at[:, pl.ds(0, self.rows // 2)]
                remote(view, view, self.sem, self.sem, r, c).wait_send()

        def group_of(rows, items):
            made = Group(rows)
            for item in items:
                made.add(*item)
            return made

        def go(made):
            made.start()
            sends.append(made)

        def slot(a, i, h):
            return tall.at[p, a, i, h]

        def aer_at(i):
            return aefr.at[at(i, 32)] if p == 0 else aepr

        def aec_at(i):
            return aefc.at[at(i, 32)] if p == 0 else aepc

        spot = core * NZ + z

        if p == 0:

            @pl.when(r == 0)
            def _():
                cols = c * height + lax.broadcasted_iota(jnp.int32, (BLOCK, height), 1)
                pct[...] = jnp.where(cols >= lead, cur[first : first + BLOCK, :], 0.0)
                gram[...] = dot(pct[...], pct[...], (1, 1))
                gin[p, c] = gram[at(c, 16), :]

            @pl.when(c == 0)
            def _():
                rows = r * height + lax.broadcasted_iota(jnp.int32, (height, BLOCK), 0)
                pr[p] = jnp.where(rows >= lead, cur[:, first : first + BLOCK], 0.0)

        else:

            @pl.when(r == 0)
            def _():
                gram[...] = dot(pc[p], pc[p], (0, 0))
                gin[p, c] = gram[at(c, 16), :]

        def row8(i, h):
            return pl.ds(pl.multiple_of(off + 16 * i + 8 * h, 8), 8)

        g_out = group_of(240, [(gram.at[at(i, 16)], gin.at[p, c], g_r.at[p], r, i) for i in plane])
        top_out = group_of(
            240,
            [(pr.at[p, row8(i, h)], tsrc.at[p, 1, h], b_r.at[p, 1], r, i) for i in plane for h in (0, 1)],
        )
        ee_out = group_of(
            240,
            [(aer.at[row8(i, h)], tsrc.at[p, 2, h], b_r.at[p, 2], r, i) for i in plane for h in (0, 1)],
        )
        down = [
            group_of(
                120,
                [
                    (tsrc.at[p, a, lax.rem(i, 2)], slot(a, c, lax.rem(i, 2)), td_r.at[p, a], i, c)
                    for i in line
                ],
            )
            for a in range(3)
        ]
        share = [
            group_of(120, [(slot(a, c, core), slot(a, c, core), t_r.at[p, a], r, i) for i in plane])
            for a in range(3)
        ]
        cross = [
            group_of(128, [(tall.at[p, a, :, core], tall.at[p, a, :, core], tm_r.at[p, a], mate, c)])
            for a in range(3)
        ]
        ae_r = group_of(480, [(aer.at[at(i, 32)], aer_at(i), ar_r.at[p], r, i) for i in plane])
        ae_c = group_of(
            480,
            [
                (aec.at[at(lax.rem(i, 2) * NZ + i // 2, 32)], aec_at(lax.rem(i, 2) * NZ + i // 2), ac_r.at[p], i, c)
                for i in line
            ],
        )
        relay = (core == 0) & (z != 0)
        if p == 0:

            def pr_part(q, sem, i):
                return (pr.at[p, at(q, 32)], pr.at[p, at(q, 32)], sem.at[0], r, i)

            def pc_part(q, sem, row):
                return (pc.at[p, at(q, 64)], pc.at[p, at(q, 64)], sem.at[0], row, c)

            root_r = group_of(
                960,
                [pr_part(i, pa_r, i) for i in range(1, N)] + [pr_part(0, p_r, i) for i in range(1, N)],
            )
            root_c = group_of(
                896,
                [pc_part(q, qa_r, 2 * q) for q in range(1, NZ)]
                + [pc_part(0, q_r, 2 * q) for q in range(1, NZ)],
            )
            ahead_r = group_of(448, [pr_part(c, p_r, i) for i in plane])
            ahead_c = group_of(384, [pc_part(z, q_r, 2 * q) for q in ring])
            low_c = group_of(512, [(pc.at[p], pc.at[p], ql_r.at[0], r + 1, c)])

        @pl.when(c == owner)
        def _():
            aer[...] = cur[:, off : off + BLOCK]
            mine = aer[at(c, 32), :]
            if p == 0:
                aefr[at(c, 32), :] = mine
            else:
                aepr[...] = mine

        @pl.when(r == owner)
        def _():
            aec[...] = cur[off : off + BLOCK, :].T
            mine = aec[at(spot, 32), :]
            if p == 0:
                aefc[at(spot, 32), :] = mine
            else:
                aepc[...] = mine

        if p == 0:
            greet(r, c)

        when(r == 0, g_out.start)

        @pl.when((r == owner) & (c == 0))
        def _():
            for h in (0, 1):
                tsrc[p, 1, h] = pr[p, row8(c, h), :]

        @pl.when((r == owner) & (c == owner))
        def _():
            for h in (0, 1):
                tsrc[p, 2, h] = aer[row8(c, h), :]

        if p == 0:
            when((c == 0) & (r > 1), root_r.start)

        swap = group_of(256, [(wc.at[at(other, 256)], half.at[p], h_r.at[p], mate, c)])
        mswap = group_of(128, [(m.at[:, other], mpair.at[p], s_r.at[p], mate, c)])
        yswap = group_of(128, [(ybuf.at[:, other], yin.at[p], ys_r.at[p], mate, c)])
        y_own = group_of(120, [(ybuf.at[i, core], iny.at[p, c], yt_r.at[p], r, i) for i in plane])
        y_mate = group_of(120, [(yin.at[p, i], iny.at[p, c], yt_r.at[p], r, i) for i in plane])

        def products():
            wc[...] = dot3(cur[...], pr[p], (0, 0))
            go(swap)
            wr[...] = dot3(cur[...], pc[p])

            @pl.when(r == owner)
            def _():
                ybuf[...] = wr[off : off + BLOCK, :].reshape(N, 2, 8, BLOCK)
                yswap.start()

            m[...] = dot(pr[p], wr[...], (0, 0)).reshape(N, 2, 8, BLOCK)
            go(mswap)

        def scatter():
            got(mpair.at[p], s_r.at[p])
            mh[...] = m[:, core] + mpair[p]
            go(group_of(120, [(mh.at[i], inm.at[p, c], m_r.at[p], r, i) for i in plane]))
            inm[p, c] = mh[c]

            @pl.when(r == owner)
            def _():
                y_own.start()
                iny[p, c] = ybuf[c, core]

            @pl.when(mate == owner)
            def _():
                got(yin.at[p], ys_r.at[p])
                y_mate.start()
                iny[p, c] = yin[p, c]

            go(group_of(480, [(wr.at[at(i, 32)], inr.at[p, c], r_r.at[p], r, i) for i in plane]))
            inr[p, c] = wr[at(c, 32), :]
            got(half.at[p], h_r.at[p])
            hsum[...] = (wc[at(core, 256), :] + half[p]).reshape(NZ, 32, BLOCK)
            zin[p, z] = hsum[z]
            go(group_of(224, [(hsum.at[q], zin.at[p, z], z_r.at[p], 2 * q + core, c) for q in ring]))

        if p > 0:
            products()

        @pl.when(r == 0)
        def _():
            got(gin.at[p, pl.ds(0, N - 1)], g_r.at[p])
            total = gin[p, 0]
            for i in range(1, N):
                total = total + gin[p, i]
            tsrc[p, 0] = total.reshape(2, 8, BLOCK)
            tall[p, 0, c, core] = tsrc[p, 0, core]
            down[0].start()

        when((r == owner) & (c == 0), top_out.start)
        when((r == owner) & (c == owner), ee_out.start)
        when(r != 0, lambda: got(slot(0, c, core), td_r.at[p, 0]))
        share[0].start()

        if p == 0:
            when((c == 0) & (r <= 1), root_r.start)

            @pl.when(r == 0)
            def _():
                pc[p] = pct[...].T
                root_c.start()
                low_c.start()

            @pl.when(relay)
            def _():
                got(pc.at[p, at(z, 64)], qa_r.at[0])
                for q, copy in zip(ring, ahead_c.copies):
                    when(q != 0, copy.start)

        @pl.when(r == owner)
        def _():
            for a, holder in ((1, 0), (2, owner)):
                when(c != holder, lambda a=a: got(tsrc.at[p, a], b_r.at[p, a]))
                tall[p, a, c, core] = tsrc[p, a, core]
                down[a].start()

        def slots(a):
            return tall.at[p, a, pl.ds(0, N - 1), core]

        got(slots(0), t_r.at[p, 0])
        cross[0].start()

        if p == 0:

            @pl.when(c != 0)
            def _():
                got(pr.at[p, at(c, 32)], pa_r.at[0])
                for i, copy in zip(plane, ahead_r.copies):
                    when(i != 0, copy.start)

        else:
            scatter()

        when(c == owner, ae_r.start)
        when(r == owner, ae_c.start)
        got(tall.at[p, 0, :, other], tm_r.at[p, 0])

        g = tall[p, 0].reshape(BLOCK, BLOCK)
        aug[...] = g[:128, :]
        strips(aug, lt_ref, 0, 4, False)
        lt_ref[:128, :128] = jnp.where(upper, lt_ref[:128, :128], 0.0)
        lt01 = lt_ref[:128, 128:]
        aug2[...] = g[128:, 128:] - dot(lt01, lt01, (0, 0))
        lt_ref[128:, :128] = jnp.zeros((128, 128), F32)

        for a in (1, 2):
            when(r != owner, lambda a=a: got(slot(a, c, core), td_r.at[p, a]))
            share[a].start()

        if p == 0:

            @pl.when(relay)
            def _():
                got(pc.at[p, pl.ds(0, 448)], q_r.at[0])
                low_c.start()

            @pl.when(c != 0)
            def _():
                got(pr.at[p, pl.ds(0, 480)], p_r.at[0])

            when(core == 1, lambda: got(pc.at[p], ql_r.at[0]))
            products()
            scatter()

        strips(aug2, low, 0, 4, False)
        lt_ref[128:, 128:] = jnp.where(upper, low[...], 0.0)
        lt = lt_ref[...]

        for a in (1, 2):
            got(slots(a), t_r.at[p, a])
            cross[a].start()

        def sum_m():
            got(inm.at[p, pl.ds(0, N - 1)], m_r.at[p])
            total = inm[p, 0]
            for i in range(1, N):
                total = total + inm[p, i]
            mring[p, z, 0] = total

            @pl.when(z == zown)
            def _():
                got(iny.at[p, pl.ds(0, N - 1)], yt_r.at[p])
                total = iny[p, 0]
                for i in range(1, N):
                    total = total + iny[p, i]
                mring[p, z, 1] = total

            @pl.when(z != zown)
            def _():
                mring[p, z, 1] = jnp.zeros((8, BLOCK), F32)

            go(group_of(112, [(mring.at[p, z], mring.at[p, z], u_r.at[p], 2 * q + core, c) for q in ring]))

        def sum_x():
            got(inr.at[p, pl.ds(0, N - 1)], r_r.at[p])
            total = inr[p, 0]
            for i in range(1, N):
                total = total + inr[p, i]
            mine = aer_at(c)
            when(c != owner, lambda: got(mine, ar_r.at[p]))
            xr[p, at(c, 32), :] = total + dot(mine[...], lt)
            own = xr.at[p, at(c, 32)]
            go(group_of(480, [(own, own, x_r.at[p], r, i) for i in plane]))
            got(zin.at[p, pl.ds(0, NZ - 1)], z_r.at[p])
            total = zin[p, 0]
            for q in range(1, NZ):
                total = total + zin[p, q]
            mine_c = aec_at(spot)
            when(r != owner, lambda: got(mine_c, ac_r.at[p]))
            xc[p, at(spot, 32), :] = total + dot(mine_c[...], lt)
            own_c = xc.at[p, at(spot, 32)]
            go(group_of(224, [(own_c, own_c, y_r.at[p], 2 * q + core, c) for q in ring]))
            if p == 0:
                own_c = aefc.at[at(spot, 32)]
                go(group_of(224, [(own_c, own_c, ag_r.at[0], 2 * q + core, c) for q in ring]))
                own = aefr.at[at(c, 32)]
                go(group_of(480, [(own, own, af_r.at[0], r, i) for i in plane]))

        sum_m()
        if p > 0:
            sum_x()

        got(tall.at[p, 1, :, other], tm_r.at[p, 1])
        top = tall[p, 1].reshape(BLOCK, BLOCK)
        n_ref[...] = tall[p, 0].reshape(BLOCK, BLOCK) + dot(top, lt, (0, 0))
        aug[...] = n_ref[:128, :]
        strips(aug, None, 0, 4, True)

        if p == 0:
            sum_x()

        d0 = aug[:, :128]
        n01 = aug[:, 128:]
        n10d = dot(n_ref[128:, :128], d0)
        aug2[...] = n_ref[128:, 128:] - dot(n_ref[128:, :128], n01)
        strips(aug2, None, 0, 2, True)

        got(mring.at[p, pl.ds(0, NZ - 1)], u_r.at[p])
        total = mring[p, 0]
        for q in range(1, NZ):
            total = total + mring[p, q]
        ball[p, :, c, core] = total
        own_b = ball.at[p, :, c, core]
        go(group_of(240, [(own_b, own_b, v_r.at[p], r, i) for i in plane]))

        strips(aug2, None, 2, 4, True)
        part = xc.at[p, at(core, 256)]
        got(xc.at[p, pl.ds(0, 224)], y_r.at[p])
        go(group_of(256, [(part, part, w_r.at[p], mate, c)]))
        e = aug2[...]
        k10 = -dot(e, n10d)
        k_ref[:128, :128] = d0 - dot(n01, k10)
        k_ref[:128, 128:] = -dot(n01, e)
        k_ref[128:, :128] = k10
        k_ref[128:, 128:] = e

        zr[...] = pr[p]
        zc[...] = pc[p]

        @pl.when(r == owner)
        def _():
            zr[off : off + BLOCK, :] = zr[off : off + BLOCK, :] + lt_ref[...]

        @pl.when(c == owner)
        def _():
            zc[off : off + BLOCK, :] = zc[off : off + BLOCK, :] + lt_ref[...]

        got(tall.at[p, 2, :, other], tm_r.at[p, 2])
        got(ball.at[p, :, pl.ds(0, N - 1), core], v_r.at[p])
        final = ball.at[p, :, :, core]
        go(group_of(256, [(final, final, f_r.at[p], mate, c)]))
        got(xr.at[p, pl.ds(0, 480)], x_r.at[p])
        ux[...] = dot3(xr[p], k_ref[...])
        got(xc.at[p, pl.ds(0, 256)], w_r.at[p])
        uy[...] = dot3(xc[p], k_ref[...])
        if p == 0:
            part = aefc.at[at(core, 256)]
            got(aefc.at[pl.ds(0, 224)], ag_r.at[0])
            go(group_of(256, [(part, part, am_r.at[0], mate, c)]))
        got(ball.at[p, :, :, other], f_r.at[p])

        ytop = ball[p, 1].reshape(BLOCK, BLOCK)
        xtop = ytop + dot(tall[p, 2].reshape(BLOCK, BLOCK), lt)
        inner = ball[p, 0].reshape(BLOCK, BLOCK) + dot(ytop, lt, (0, 0)) + dot(lt, xtop, (0, 0))
        coupled = 0.5 * dot(k_ref[...], dot(inner, k_ref[...]), (0, 0))
        ur = ux[...] - dot3(zr[...], coupled)
        uc = uy[...] - dot3(zc[...], coupled)
        dest = out_ref if p == PANELS - 1 else cur
        dest[...] = cur[...] - dot3(ur, zc[...], (1, 1)) - dot3(zr[...], uc, (1, 1))
        if p == 0:
            ztop = top + lt
            utop = dot(xtop, k_ref[...]) - dot(ztop, coupled)
            rows = lax.broadcasted_iota(jnp.int32, (height, BLOCK), 0)
            got(aefr.at[pl.ds(0, 480)], af_r.at[0])
            near = aefr[...] - dot3(ur, ztop, (1, 1)) - dot3(zr[...], utop, (1, 1))
            pr[1] = jnp.where(r * height + rows >= lead + BLOCK, near, 0.0)
            got(aefc.at[pl.ds(0, 256)], am_r.at[0])
            near = aefc[...] - dot3(uc, ztop, (1, 1)) - dot3(zc[...], utop, (1, 1))
            pc[1] = jnp.where(c * height + rows >= lead + BLOCK, near, 0.0)

        for made in sends + share + cross:
            made.left()
        when(r == 0, g_out.left)
        when(r == 0, down[0].left)
        for made in (down[1], down[2], ae_c, y_own, yswap):
            when(r == owner, made.left)
        when(mate == owner, y_mate.left)
        when((r == owner) & (c == 0), top_out.left)
        when((r == owner) & (c == owner), ee_out.left)
        when(c == owner, ae_r.left)
        if p == 0:
            when(r == 0, root_c.left)
            when(c == 0, root_r.left)
            when(c != 0, ahead_r.left)
            when(relay, ahead_c.left)
            when(core == 0, low_c.left)


def per_device(matrix):
    dma = pltpu.SemaphoreType.DMA

    def buf(*shape):
        return pltpu.VMEM(shape, F32)

    return pl.pallas_call(
        kernel,
        out_shape=jax.ShapeDtypeStruct(matrix.shape, F32),
        in_specs=[VMEM],
        out_specs=VMEM,
        scratch_shapes=[
            buf(512, 512),
            buf(2, 512, 256),
            buf(256, 512),
            buf(2, 512, 256),
            buf(512, 256),
            buf(512, 256),
            buf(32, 256),
            buf(32, 256),
            buf(512, 256),
            buf(512, 256),
            buf(256, 256),
            buf(2, N, 16, 256),
            buf(2, 3, 2, 8, 256),
            buf(2, 3, N, 2, 8, 256),
            buf(256, 256),
            buf(256, 256),
            buf(256, 256),
            buf(128, 256),
            buf(128, 128),
            buf(128, 128),
            buf(512, 256),
            buf(512, 256),
            buf(512, 256),
            buf(512, 256),
            buf(N, 2, 8, 256),
            buf(2, N, 8, 256),
            buf(N, 8, 256),
            buf(N, 2, 8, 256),
            buf(2, N, 8, 256),
            buf(2, N, 32, 256),
            buf(2, N, 8, 256),
            buf(2, N, 8, 256),
            buf(2, 256, 256),
            buf(NZ, 32, 256),
            buf(2, NZ, 32, 256),
            buf(2, 512, 256),
            buf(2, 512, 256),
            buf(2, NZ, 2, 8, 256),
            buf(2, 2, N, 2, 8, 256),
            buf(512, 256),
            buf(512, 256),
            dma((60,)),
            dma((2,)),
            dma((2, 3)),
            dma((2, 3)),
            dma((2, 3)),
            dma((2, 3)),
            dma((1,)),
            dma((1,)),
            dma((1,)),
            dma((1,)),
            dma((1,)),
            dma((2,)),
            dma((2,)),
            dma((1,)),
            dma((1,)),
            dma((1,)),
            dma((2,)),
            dma((2,)),
            dma((2,)),
            dma((2,)),
            dma((2,)),
            dma((2,)),
            dma((2,)),
            dma((2,)),
            dma((2,)),
            dma((2,)),
            dma((2,)),
            dma((2,)),
            dma((2,)),
        ],
        compiler_params=pltpu.CompilerParams(collective_id=0, has_side_effects=True),
        name="reduce_panels",
    )(matrix)


def solution(mesh):
    return jax.shard_map(
        per_device, mesh=mesh, in_specs=(P("row", "col"),), out_specs=P("row", "col"), check_vma=False
    )
```

```python
import jax
import jax.numpy as jnp
from jax import lax
from jax.experimental import pallas as pl
from jax.experimental.pallas import tpu as pltpu
from jax.sharding import PartitionSpec as P

BLOCK = 256
PANELS = 2
N = 16
NZ = 8
HIGH = lax.Precision.HIGHEST
F32 = jnp.float32
MESH = pl.DeviceIdType.MESH
VMEM = pl.BlockSpec(memory_space=pltpu.VMEM)


def dot(left, right, over=(1, 0)):
    return lax.dot_general(
        left,
        right,
        (((over[0],), (over[1],)), ((), ())),
        precision=HIGH,
        preferred_element_type=F32,
    )


def dot3(left, right, over=(1, 0)):
    def split(x):
        high = x.astype(jnp.bfloat16)
        return high, (x - high.astype(F32)).astype(jnp.bfloat16)

    def part(a, b):
        return lax.dot_general(
            a, b, (((over[0],), (over[1],)), ((), ())), preferred_element_type=F32
        )

    lh, ll = split(left)
    rh, rl = split(right)
    return part(lh, rh) + (part(lh, rl) + part(ll, rh))


def recip(x):
    r = pl.reciprocal(x, approx=True)
    return r * (2.0 - x * r)


def lanes(block, index):
    return jnp.take_along_axis(block, jnp.full((8, 128), index, jnp.int32), axis=1)


def times(scale, row):
    if row.shape[1] == 128:
        return scale * row
    return jnp.concatenate([scale * row[:, :128], scale * row[:, 128:]], axis=1)


def put(rows):
    sub = lax.broadcasted_iota(jnp.int32, rows[0].shape, 0)
    out = rows[0]
    for s in range(1, 8):
        out = jnp.where(sub == s, rows[s], out)
    return out


def group(aug, out, base, inverse):
    width = aug.shape[1]
    lane = lax.broadcasted_iota(jnp.int32, (8, 128), 1)
    inside = (lane >= base) & (lane < base + 8)

    def left(block, value):
        if width == 128:
            return jnp.where(inside, value, block)
        return jnp.concatenate([jnp.where(inside, value, block[:, :128]), block[:, 128:]], axis=1)

    rows = [jnp.broadcast_to(aug[pl.ds(base + s, 1), :], (8, width)) for s in range(8)]
    e = [[None] * 8 for _ in range(8)]
    for t in range(8):
        for s in range(8 if inverse else t + 1):
            e[s][t] = lanes(rows[s][:, :128], base + t)
    if inverse:
        rows = [left(rows[s], (lane == base + s).astype(F32)) for s in range(8)]
    inv = []
    for s in range(8):
        inv.append(recip(e[s][s]))
        for t in range(s + 1, 8):
            f = (e[t][s] if inverse else e[s][t]) * inv[s]
            for u in range(s + 1 if inverse else t, 8):
                e[t][u] = e[t][u] - f * e[s][u]
            rows[t] = rows[t] - times(f, rows[s])
    if not inverse:
        out[pl.ds(base, 8), :] = put([times(lax.rsqrt(e[s][s]), rows[s]) for s in range(8)])
    solved = [None] * 8
    for s in reversed(range(8)):
        acc = rows[s]
        for t in range(s + 1, 8):
            acc = acc - times(e[s][t], solved[t])
        solved[s] = times(inv[s], acc)
    own = put(solved)
    strip = pl.multiple_of(base // 32 * 32, 32)
    blocks = [aug[pl.ds(strip + 8 * k, 8), :] for k in range(4)]
    after = [left(b, 0.0) if inverse else b for b in blocks]
    for s in range(8):
        for k in range(4):
            after[k] = after[k] - times(lanes(blocks[k][:, :128], base + s), solved[s])
    for k in range(4):
        aug[pl.ds(strip + 8 * k, 8), :] = jnp.where(strip + 8 * k == base, own, after[k])


def strips(aug, out, lo, hi, inverse):
    row = lax.broadcasted_iota(jnp.int32, (128, 128), 0) // 32
    lane = lax.broadcasted_iota(jnp.int32, (128, 128), 1) // 32

    def one(k, q):
        group(aug, out, pl.multiple_of(32 * q + 8 * k, 8), inverse)
        return q

    def strip(q, carry):
        lax.fori_loop(0, 4, one, q)
        aim = (lane == q) & ((row != q) if inverse else (row > q))
        near = aug[:, :128]
        prod = dot(jnp.where(aim, near, 0.0), aug[...])
        if inverse:
            near = jnp.where(aim, 0.0, near)
        aug[:, :128] = near - prod[:, :128]
        if aug.shape[1] > 128:
            aug[:, 128:] = aug[:, 128:] - prod[:, 128:]
        return carry

    lax.fori_loop(lo, hi, strip, 0)


def remote(src, dst, send, recv, row, col):
    return pltpu.make_async_remote_copy(
        src_ref=src,
        dst_ref=dst,
        send_sem=send,
        recv_sem=recv,
        device_id=(row, col),
        device_id_type=MESH,
    )


def greet(r, c):
    barrier = pltpu.get_barrier_semaphore()
    for k in range(1, N):
        pl.semaphore_signal(barrier, inc=1, device_id=(r, lax.rem(c + k, N)), device_id_type=MESH)
        pl.semaphore_signal(barrier, inc=1, device_id=(lax.rem(r + k, N), c), device_id_type=MESH)
    pl.semaphore_wait(barrier, 2 * (N - 1))


def at(index, size):
    return pl.ds(pl.multiple_of(index * size, size), size)


def kernel(
    a_ref, out_ref,
    cur, pr, pct, pc, aer, aec, aepr, aepc, aefr, aefc, gram, gin, tsrc, tall, lt_ref, k_ref, n_ref, aug, aug2, low,
    zr, zc, wr, wc, m, mpair, mh, ybuf, yin, inr, inm, iny, half, hsum, zin, xr, xc, mring, ball,
    ux, uy,
    ss, g_r, b_r, td_r, t_r, tm_r, pa_r, p_r, qa_r, q_r, ql_r, ar_r, ac_r, af_r, ag_r, am_r,
    r_r, m_r, yt_r, ys_r, h_r, z_r, x_r, y_r, w_r, s_r, u_r, v_r, f_r,
):
    r, c = lax.axis_index("row"), lax.axis_index("col")
    z, core = r // 2, lax.rem(r, 2)
    other = 1 - core
    mate = r + 1 - 2 * core
    height = a_ref.shape[0]
    upper = lax.broadcasted_iota(jnp.int32, (128, 128), 0) <= lax.broadcasted_iota(
        jnp.int32, (128, 128), 1
    )
    plane = [lax.rem(c + k, N) for k in range(1, N)]
    line = [lax.rem(r + k, N) for k in range(1, N)]
    ring = [lax.rem(z + k, NZ) for k in range(1, NZ)]

    def got(ref, sem):
        remote(ref, ref, ss.at[0], sem, r, c).wait_recv()

    def when(cond, run):
        pl.when(cond)(run)

    cur[...] = a_ref[...]
    zown = 0

    for p in range(PANELS):
        first, lead = p * BLOCK, (p + 1) * BLOCK
        owner, off = lead // height, lead % height
        count = iter(range(1, 60))
        sends = []

        class Group:
            def __init__(self, rows):
                self.sem = ss.at[next(count)]
                self.rows = rows
                self.copies = []

            def add(self, src, dst, sem, row, col):
                self.copies.append(remote(src, dst, self.sem, sem, row, col))
                return self.copies[-1]

            def start(self):
                for copy in self.copies:
                    copy.start()

            def left(self):
                if self.rows <= 512:
                    view = wc.at[pl.ds(0, self.rows)]
                else:
                    view = pr.at[:, pl.ds(0, self.rows // 2)]
                remote(view, view, self.sem, self.sem, r, c).wait_send()

        def group_of(rows, items):
            made = Group(rows)
            for item in items:
                made.add(*item)
            return made

        def go(made):
            made.start()
            sends.append(made)

        def slot(a, i, h):
            return tall.at[p, a, i, h]

        def aer_at(i):
            return aefr.at[at(i, 32)] if p == 0 else aepr

        def aec_at(i):
            return aefc.at[at(i, 32)] if p == 0 else aepc

        spot = core * NZ + z

        if p == 0:

            @pl.when(r == 0)
            def _():
                cols = c * height + lax.broadcasted_iota(jnp.int32, (BLOCK, height), 1)
                pct[...] = jnp.where(cols >= lead, cur[first : first + BLOCK, :], 0.0)
                gram[...] = dot(pct[...], pct[...], (1, 1))
                gin[p, c] = gram[at(c, 16), :]

            @pl.when(c == 0)
            def _():
                rows = r * height + lax.broadcasted_iota(jnp.int32, (height, BLOCK), 0)
                pr[p] = jnp.where(rows >= lead, cur[:, first : first + BLOCK], 0.0)

        else:

            @pl.when(r == 0)
            def _():
                gram[...] = dot(pc[p], pc[p], (0, 0))
                gin[p, c] = gram[at(c, 16), :]

        def row8(i, h):
            return pl.ds(pl.multiple_of(off + 16 * i + 8 * h, 8), 8)

        g_out = group_of(240, [(gram.at[at(i, 16)], gin.at[p, c], g_r.at[p], r, i) for i in plane])
        top_out = group_of(
            240,
            [(pr.at[p, row8(i, h)], tsrc.at[p, 1, h], b_r.at[p, 1], r, i) for i in plane for h in (0, 1)],
        )
        ee_out = group_of(
            240,
            [(aer.at[row8(i, h)], tsrc.at[p, 2, h], b_r.at[p, 2], r, i) for i in plane for h in (0, 1)],
        )
        down = [
            group_of(
                120,
                [
                    (tsrc.at[p, a, lax.rem(i, 2)], slot(a, c, lax.rem(i, 2)), td_r.at[p, a], i, c)
                    for i in line
                ],
            )
            for a in range(3)
        ]
        share = [
            group_of(120, [(slot(a, c, core), slot(a, c, core), t_r.at[p, a], r, i) for i in plane])
            for a in range(3)
        ]
        cross = [
            group_of(128, [(tall.at[p, a, :, core], tall.at[p, a, :, core], tm_r.at[p, a], mate, c)])
            for a in range(3)
        ]
        ae_r = group_of(480, [(aer.at[at(i, 32)], aer_at(i), ar_r.at[p], r, i) for i in plane])
        ae_c = group_of(
            480,
            [
                (aec.at[at(lax.rem(i, 2) * NZ + i // 2, 32)], aec_at(lax.rem(i, 2) * NZ + i // 2), ac_r.at[p], i, c)
                for i in line
            ],
        )
        relay = (core == 0) & (z != 0)
        if p == 0:

            def pr_part(q, sem, i):
                return (pr.at[p, at(q, 32)], pr.at[p, at(q, 32)], sem.at[0], r, i)

            def pc_part(q, sem, row):
                return (pc.at[p, at(q, 64)], pc.at[p, at(q, 64)], sem.at[0], row, c)

            root_r = group_of(
                960,
                [pr_part(i, pa_r, i) for i in range(1, N)] + [pr_part(0, p_r, i) for i in range(1, N)],
            )
            root_c = group_of(
                896,
                [pc_part(q, qa_r, 2 * q) for q in range(1, NZ)]
                + [pc_part(0, q_r, 2 * q) for q in range(1, NZ)],
            )
            ahead_r = group_of(448, [pr_part(c, p_r, i) for i in plane])
            ahead_c = group_of(384, [pc_part(z, q_r, 2 * q) for q in ring])
            low_c = group_of(512, [(pc.at[p], pc.at[p], ql_r.at[0], r + 1, c)])

        @pl.when(c == owner)
        def _():
            aer[...] = cur[:, off : off + BLOCK]
            mine = aer[at(c, 32), :]
            if p == 0:
                aefr[at(c, 32), :] = mine
            else:
                aepr[...] = mine

        @pl.when(r == owner)
        def _():
            aec[...] = cur[off : off + BLOCK, :].T
            mine = aec[at(spot, 32), :]
            if p == 0:
                aefc[at(spot, 32), :] = mine
            else:
                aepc[...] = mine

        if p == 0:
            greet(r, c)

        when(r == 0, g_out.start)

        @pl.when((r == owner) & (c == 0))
        def _():
            for h in (0, 1):
                tsrc[p, 1, h] = pr[p, row8(c, h), :]

        @pl.when((r == owner) & (c == owner))
        def _():
            for h in (0, 1):
                tsrc[p, 2, h] = aer[row8(c, h), :]

        when((r == owner) & (c == 0), top_out.start)
        when((r == owner) & (c == owner), ee_out.start)
        if p == 0:
            when(c == 0, root_r.start)

        swap = group_of(256, [(wc.at[at(other, 256)], half.at[p], h_r.at[p], mate, c)])
        mswap = group_of(128, [(m.at[:, other], mpair.at[p], s_r.at[p], mate, c)])
        yswap = group_of(128, [(ybuf.at[:, other], yin.at[p], ys_r.at[p], mate, c)])
        y_own = group_of(120, [(ybuf.at[i, core], iny.at[p, c], yt_r.at[p], r, i) for i in plane])
        y_mate = group_of(120, [(yin.at[p, i], iny.at[p, c], yt_r.at[p], r, i) for i in plane])

        def products():
            wc[...] = dot3(cur[...], pr[p], (0, 0))
            go(swap)
            if p == 0:
                when(core == 1, lambda: got(pc.at[p], ql_r.at[0]))
            wr[...] = dot3(cur[...], pc[p])

            @pl.when(r == owner)
            def _():
                ybuf[...] = wr[off : off + BLOCK, :].reshape(N, 2, 8, BLOCK)
                yswap.start()

            m[...] = dot(pr[p], wr[...], (0, 0)).reshape(N, 2, 8, BLOCK)
            go(mswap)

        def scatter():
            got(mpair.at[p], s_r.at[p])
            mh[...] = m[:, core] + mpair[p]
            go(group_of(120, [(mh.at[i], inm.at[p, c], m_r.at[p], r, i) for i in plane]))
            inm[p, c] = mh[c]

            @pl.when(r == owner)
            def _():
                y_own.start()
                iny[p, c] = ybuf[c, core]

            @pl.when(mate == owner)
            def _():
                got(yin.at[p], ys_r.at[p])
                y_mate.start()
                iny[p, c] = yin[p, c]

            go(group_of(480, [(wr.at[at(i, 32)], inr.at[p, c], r_r.at[p], r, i) for i in plane]))
            inr[p, c] = wr[at(c, 32), :]
            got(half.at[p], h_r.at[p])
            hsum[...] = (wc[at(core, 256), :] + half[p]).reshape(NZ, 32, BLOCK)
            zin[p, z] = hsum[z]
            go(group_of(224, [(hsum.at[q], zin.at[p, z], z_r.at[p], 2 * q + core, c) for q in ring]))

        if p > 0:
            products()

        @pl.when(r == 0)
        def _():
            got(gin.at[p, pl.ds(0, N - 1)], g_r.at[p])
            total = gin[p, 0]
            for i in range(1, N):
                total = total + gin[p, i]
            tsrc[p, 0] = total.reshape(2, 8, BLOCK)
            tall[p, 0, c, core] = tsrc[p, 0, core]
            down[0].start()

        @pl.when(r == owner)
        def _():
            for a, holder in ((1, 0), (2, owner)):
                when(c != holder, lambda a=a: got(tsrc.at[p, a], b_r.at[p, a]))
                tall[p, a, c, core] = tsrc[p, a, core]
                down[a].start()

        when(r != 0, lambda: got(slot(0, c, core), td_r.at[p, 0]))
        share[0].start()

        if p == 0:
            @pl.when(r == 0)
            def _():
                pc[p] = pct[...].T
                root_c.start()
                low_c.start()

            @pl.when(relay)
            def _():
                got(pc.at[p, at(z, 64)], qa_r.at[0])
                for q, copy in zip(ring, ahead_c.copies):
                    when(q != 0, copy.start)

        def share_rest():
            for a in (1, 2):
                when(r != owner, lambda a=a: got(slot(a, c, core), td_r.at[p, a]))
                share[a].start()

        if p > 0:
            share_rest()

        def slots(a):
            return tall.at[p, a, pl.ds(0, N - 1), core]

        got(slots(0), t_r.at[p, 0])
        cross[0].start()

        if p == 0:

            @pl.when(c != 0)
            def _():
                got(pr.at[p, at(c, 32)], pa_r.at[0])
                for i, copy in zip(plane, ahead_r.copies):
                    when(i != 0, copy.start)

            share_rest()

        else:
            scatter()
            when(c == owner, ae_r.start)
            when(r == owner, ae_c.start)

        got(tall.at[p, 0, :, other], tm_r.at[p, 0])

        g = tall[p, 0].reshape(BLOCK, BLOCK)
        aug[...] = g[:128, :]
        strips(aug, lt_ref, 0, 4, False)
        lt_ref[:128, :128] = jnp.where(upper, lt_ref[:128, :128], 0.0)
        lt01 = lt_ref[:128, 128:]
        aug2[...] = g[128:, 128:] - dot(lt01, lt01, (0, 0))
        lt_ref[128:, :128] = jnp.zeros((128, 128), F32)

        def cross_rest():
            for a in (1, 2):
                got(slots(a), t_r.at[p, a])
                cross[a].start()

        if p > 0:
            cross_rest()

        if p == 0:

            @pl.when(relay)
            def _():
                got(pc.at[p, pl.ds(0, 448)], q_r.at[0])
                low_c.start()

            @pl.when(c != 0)
            def _():
                got(pr.at[p, pl.ds(0, 480)], p_r.at[0])

            products()
            scatter()
            when(c == owner, ae_r.start)
            when(r == owner, ae_c.start)

        strips(aug2, low, 0, 4, False)
        lt_ref[128:, 128:] = jnp.where(upper, low[...], 0.0)
        lt = lt_ref[...]

        def sum_m():
            got(inm.at[p, pl.ds(0, N - 1)], m_r.at[p])
            total = inm[p, 0]
            for i in range(1, N):
                total = total + inm[p, i]
            mring[p, z, 0] = total

            @pl.when(z == zown)
            def _():
                got(iny.at[p, pl.ds(0, N - 1)], yt_r.at[p])
                total = iny[p, 0]
                for i in range(1, N):
                    total = total + iny[p, i]
                mring[p, z, 1] = total

            @pl.when(z != zown)
            def _():
                mring[p, z, 1] = jnp.zeros((8, BLOCK), F32)

            go(group_of(112, [(mring.at[p, z], mring.at[p, z], u_r.at[p], 2 * q + core, c) for q in ring]))

        def sum_x():
            got(inr.at[p, pl.ds(0, N - 1)], r_r.at[p])
            total = inr[p, 0]
            for i in range(1, N):
                total = total + inr[p, i]
            mine = aer_at(c)
            when(c != owner, lambda: got(mine, ar_r.at[p]))
            xr[p, at(c, 32), :] = total + dot(mine[...], lt)
            own = xr.at[p, at(c, 32)]
            go(group_of(480, [(own, own, x_r.at[p], r, i) for i in plane]))
            got(zin.at[p, pl.ds(0, NZ - 1)], z_r.at[p])
            total = zin[p, 0]
            for q in range(1, NZ):
                total = total + zin[p, q]
            mine_c = aec_at(spot)
            when(r != owner, lambda: got(mine_c, ac_r.at[p]))
            xc[p, at(spot, 32), :] = total + dot(mine_c[...], lt)
            own_c = xc.at[p, at(spot, 32)]
            go(group_of(224, [(own_c, own_c, y_r.at[p], 2 * q + core, c) for q in ring]))
            if p == 0:
                own_c = aefc.at[at(spot, 32)]
                go(group_of(224, [(own_c, own_c, ag_r.at[0], 2 * q + core, c) for q in ring]))
                own = aefr.at[at(c, 32)]
                go(group_of(480, [(own, own, af_r.at[0], r, i) for i in plane]))

        if p == 0:
            cross_rest()
        else:
            sum_m()

        got(tall.at[p, 1, :, other], tm_r.at[p, 1])
        top = tall[p, 1].reshape(BLOCK, BLOCK)
        n_ref[...] = tall[p, 0].reshape(BLOCK, BLOCK) + dot(top, lt, (0, 0))
        aug[...] = n_ref[:128, :]
        strips(aug, None, 0, 2, True)
        if p == 0:
            sum_m()
        else:
            sum_x()
        strips(aug, None, 2, 4, True)
        if p == 0:
            sum_x()

        d0 = aug[:, :128]
        n01 = aug[:, 128:]
        n10d = dot(n_ref[128:, :128], d0)
        aug2[...] = n_ref[128:, 128:] - dot(n_ref[128:, :128], n01)
        strips(aug2, None, 0, 2, True)

        got(mring.at[p, pl.ds(0, NZ - 1)], u_r.at[p])
        total = mring[p, 0]
        for q in range(1, NZ):
            total = total + mring[p, q]
        ball[p, :, c, core] = total
        own_b = ball.at[p, :, c, core]
        go(group_of(240, [(own_b, own_b, v_r.at[p], r, i) for i in plane]))

        strips(aug2, None, 2, 4, True)
        part = xc.at[p, at(core, 256)]
        got(xc.at[p, pl.ds(0, 224)], y_r.at[p])
        go(group_of(256, [(part, part, w_r.at[p], mate, c)]))
        e = aug2[...]
        k10 = -dot(e, n10d)
        k_ref[:128, :128] = d0 - dot(n01, k10)
        k_ref[:128, 128:] = -dot(n01, e)
        k_ref[128:, :128] = k10
        k_ref[128:, 128:] = e

        zr[...] = pr[p]
        zc[...] = pc[p]

        @pl.when(r == owner)
        def _():
            zr[off : off + BLOCK, :] = zr[off : off + BLOCK, :] + lt_ref[...]

        @pl.when(c == owner)
        def _():
            zc[off : off + BLOCK, :] = zc[off : off + BLOCK, :] + lt_ref[...]

        got(tall.at[p, 2, :, other], tm_r.at[p, 2])
        got(ball.at[p, :, pl.ds(0, N - 1), core], v_r.at[p])
        final = ball.at[p, :, :, core]
        go(group_of(256, [(final, final, f_r.at[p], mate, c)]))
        got(xr.at[p, pl.ds(0, 480)], x_r.at[p])
        ux[...] = dot3(xr[p], k_ref[...])
        got(xc.at[p, pl.ds(0, 256)], w_r.at[p])
        uy[...] = dot3(xc[p], k_ref[...])
        if p == 0:
            part = aefc.at[at(core, 256)]
            got(aefc.at[pl.ds(0, 224)], ag_r.at[0])
            go(group_of(256, [(part, part, am_r.at[0], mate, c)]))
        got(ball.at[p, :, :, other], f_r.at[p])

        ytop = ball[p, 1].reshape(BLOCK, BLOCK)
        xtop = ytop + dot(tall[p, 2].reshape(BLOCK, BLOCK), lt)
        inner = ball[p, 0].reshape(BLOCK, BLOCK) + dot(ytop, lt, (0, 0)) + dot(lt, xtop, (0, 0))
        coupled = 0.5 * dot(k_ref[...], dot(inner, k_ref[...]), (0, 0))
        ur = ux[...] - dot3(zr[...], coupled)
        uc = uy[...] - dot3(zc[...], coupled)
        dest = out_ref if p == PANELS - 1 else cur
        dest[...] = cur[...] - dot3(ur, zc[...], (1, 1)) - dot3(zr[...], uc, (1, 1))
        if p == 0:
            ztop = top + lt
            utop = dot(xtop, k_ref[...]) - dot(ztop, coupled)
            rows = lax.broadcasted_iota(jnp.int32, (height, BLOCK), 0)
            got(aefr.at[pl.ds(0, 480)], af_r.at[0])
            near = aefr[...] - dot3(ur, ztop, (1, 1)) - dot3(zr[...], utop, (1, 1))
            pr[1] = jnp.where(r * height + rows >= lead + BLOCK, near, 0.0)
            got(aefc.at[pl.ds(0, 256)], am_r.at[0])
            near = aefc[...] - dot3(uc, ztop, (1, 1)) - dot3(zc[...], utop, (1, 1))
            pc[1] = jnp.where(c * height + rows >= lead + BLOCK, near, 0.0)

        for made in sends + share + cross:
            made.left()
        when(r == 0, g_out.left)
        when(r == 0, down[0].left)
        for made in (down[1], down[2], ae_c, y_own, yswap):
            when(r == owner, made.left)
        when(mate == owner, y_mate.left)
        when((r == owner) & (c == 0), top_out.left)
        when((r == owner) & (c == owner), ee_out.left)
        when(c == owner, ae_r.left)
        if p == 0:
            when(r == 0, root_c.left)
            when(c == 0, root_r.left)
            when(c != 0, ahead_r.left)
            when(relay, ahead_c.left)
            when(core == 0, low_c.left)


def per_device(matrix):
    dma = pltpu.SemaphoreType.DMA

    def buf(*shape):
        return pltpu.VMEM(shape, F32)

    return pl.pallas_call(
        kernel,
        out_shape=jax.ShapeDtypeStruct(matrix.shape, F32),
        in_specs=[VMEM],
        out_specs=VMEM,
        scratch_shapes=[
            buf(512, 512),
            buf(2, 512, 256),
            buf(256, 512),
            buf(2, 512, 256),
            buf(512, 256),
            buf(512, 256),
            buf(32, 256),
            buf(32, 256),
            buf(512, 256),
            buf(512, 256),
            buf(256, 256),
            buf(2, N, 16, 256),
            buf(2, 3, 2, 8, 256),
            buf(2, 3, N, 2, 8, 256),
            buf(256, 256),
            buf(256, 256),
            buf(256, 256),
            buf(128, 256),
            buf(128, 128),
            buf(128, 128),
            buf(512, 256),
            buf(512, 256),
            buf(512, 256),
            buf(512, 256),
            buf(N, 2, 8, 256),
            buf(2, N, 8, 256),
            buf(N, 8, 256),
            buf(N, 2, 8, 256),
            buf(2, N, 8, 256),
            buf(2, N, 32, 256),
            buf(2, N, 8, 256),
            buf(2, N, 8, 256),
            buf(2, 256, 256),
            buf(NZ, 32, 256),
            buf(2, NZ, 32, 256),
            buf(2, 512, 256),
            buf(2, 512, 256),
            buf(2, NZ, 2, 8, 256),
            buf(2, 2, N, 2, 8, 256),
            buf(512, 256),
            buf(512, 256),
            dma((60,)),
            dma((2,)),
            dma((2, 3)),
            dma((2, 3)),
            dma((2, 3)),
            dma((2, 3)),
            dma((1,)),
            dma((1,)),
            dma((1,)),
            dma((1,)),
            dma((1,)),
            dma((2,)),
            dma((2,)),
            dma((1,)),
            dma((1,)),
            dma((1,)),
            dma((2,)),
            dma((2,)),
            dma((2,)),
            dma((2,)),
            dma((2,)),
            dma((2,)),
            dma((2,)),
            dma((2,)),
            dma((2,)),
            dma((2,)),
            dma((2,)),
            dma((2,)),
            dma((2,)),
        ],
        compiler_params=pltpu.CompilerParams(collective_id=0, has_side_effects=True),
        name="reduce_panels",
    )(matrix)


def solution(mesh):
    return jax.shard_map(
        per_device, mesh=mesh, in_specs=(P("row", "col"),), out_specs=P("row", "col"), check_vma=False
    )
```

```python
import jax
import jax.numpy as jnp
from jax import lax
from jax.experimental import pallas as pl
from jax.experimental.pallas import tpu as pltpu
from jax.sharding import PartitionSpec as P

BLOCK = 256
PANELS = 2
N = 16
NZ = 8
HIGH = lax.Precision.HIGHEST
F32 = jnp.float32
MESH = pl.DeviceIdType.MESH
VMEM = pl.BlockSpec(memory_space=pltpu.VMEM)


def dot(left, right, over=(1, 0)):
    return lax.dot_general(
        left,
        right,
        (((over[0],), (over[1],)), ((), ())),
        precision=HIGH,
        preferred_element_type=F32,
    )


def dot3(left, right, over=(1, 0)):
    def split(x):
        high = x.astype(jnp.bfloat16)
        return high, (x - high.astype(F32)).astype(jnp.bfloat16)

    def part(a, b):
        return lax.dot_general(
            a, b, (((over[0],), (over[1],)), ((), ())), preferred_element_type=F32
        )

    lh, ll = split(left)
    rh, rl = split(right)
    return part(lh, rh) + (part(lh, rl) + part(ll, rh))


def recip(x):
    r = pl.reciprocal(x, approx=True)
    return r * (2.0 - x * r)


def lanes(block, index):
    return jnp.take_along_axis(block, jnp.full((8, 128), index, jnp.int32), axis=1)


def times(scale, row):
    if row.shape[1] == 128:
        return scale * row
    return jnp.concatenate([scale * row[:, :128], scale * row[:, 128:]], axis=1)


def put(rows):
    sub = lax.broadcasted_iota(jnp.int32, rows[0].shape, 0)
    out = rows[0]
    for s in range(1, 8):
        out = jnp.where(sub == s, rows[s], out)
    return out


def group(aug, out, base, inverse):
    width = aug.shape[1]
    lane = lax.broadcasted_iota(jnp.int32, (8, 128), 1)
    inside = (lane >= base) & (lane < base + 8)

    def left(block, value):
        if width == 128:
            return jnp.where(inside, value, block)
        return jnp.concatenate([jnp.where(inside, value, block[:, :128]), block[:, 128:]], axis=1)

    rows = [jnp.broadcast_to(aug[pl.ds(base + s, 1), :], (8, width)) for s in range(8)]
    e = [[None] * 8 for _ in range(8)]
    for t in range(8):
        for s in range(8 if inverse else t + 1):
            e[s][t] = lanes(rows[s][:, :128], base + t)
    if inverse:
        rows = [left(rows[s], (lane == base + s).astype(F32)) for s in range(8)]
    inv = []
    for s in range(8):
        inv.append(recip(e[s][s]))
        for t in range(s + 1, 8):
            f = (e[t][s] if inverse else e[s][t]) * inv[s]
            for u in range(s + 1 if inverse else t, 8):
                e[t][u] = e[t][u] - f * e[s][u]
            rows[t] = rows[t] - times(f, rows[s])
    if not inverse:
        out[pl.ds(base, 8), :] = put([times(lax.rsqrt(e[s][s]), rows[s]) for s in range(8)])
    solved = [None] * 8
    for s in reversed(range(8)):
        acc = rows[s]
        for t in range(s + 1, 8):
            acc = acc - times(e[s][t], solved[t])
        solved[s] = times(inv[s], acc)
    own = put(solved)
    strip = pl.multiple_of(base // 32 * 32, 32)
    blocks = [aug[pl.ds(strip + 8 * k, 8), :] for k in range(4)]
    after = [left(b, 0.0) if inverse else b for b in blocks]
    for s in range(8):
        for k in range(4):
            after[k] = after[k] - times(lanes(blocks[k][:, :128], base + s), solved[s])
    for k in range(4):
        aug[pl.ds(strip + 8 * k, 8), :] = jnp.where(strip + 8 * k == base, own, after[k])


def strips(aug, out, lo, hi, inverse):
    row = lax.broadcasted_iota(jnp.int32, (128, 128), 0) // 32
    lane = lax.broadcasted_iota(jnp.int32, (128, 128), 1) // 32

    def one(k, q):
        group(aug, out, pl.multiple_of(32 * q + 8 * k, 8), inverse)
        return q

    def strip(q, carry):
        lax.fori_loop(0, 4, one, q)
        aim = (lane == q) & ((row != q) if inverse else (row > q))
        near = aug[:, :128]
        prod = dot(jnp.where(aim, near, 0.0), aug[...])
        if inverse:
            near = jnp.where(aim, 0.0, near)
        aug[:, :128] = near - prod[:, :128]
        if aug.shape[1] > 128:
            aug[:, 128:] = aug[:, 128:] - prod[:, 128:]
        return carry

    lax.fori_loop(lo, hi, strip, 0)


def remote(src, dst, send, recv, row, col):
    return pltpu.make_async_remote_copy(
        src_ref=src,
        dst_ref=dst,
        send_sem=send,
        recv_sem=recv,
        device_id=(row, col),
        device_id_type=MESH,
    )


def greet(r, c):
    barrier = pltpu.get_barrier_semaphore()
    for k in range(1, N):
        pl.semaphore_signal(barrier, inc=1, device_id=(r, lax.rem(c + k, N)), device_id_type=MESH)
        pl.semaphore_signal(barrier, inc=1, device_id=(lax.rem(r + k, N), c), device_id_type=MESH)
    pl.semaphore_wait(barrier, 2 * (N - 1))


def at(index, size):
    return pl.ds(pl.multiple_of(index * size, size), size)


def kernel(
    a_ref, out_ref,
    cur, pr, pct, pc, aer, aec, aepr, aepc, aefr, aefc, gram, gin, tsrc, tall, lt_ref, k_ref, n_ref, aug, aug2, low,
    zr, zc, wr, wc, m, mpair, mh, ybuf, yin, inr, inm, iny, half, hsum, zin, xr, xc, mring, ball,
    ux, uy,
    ss, g_r, b_r, td_r, t_r, tm_r, pa_r, p_r, qa_r, q_r, ql_r, ar_r, ac_r, af_r, ag_r, am_r,
    r_r, m_r, yt_r, ys_r, h_r, z_r, x_r, y_r, w_r, s_r, u_r, v_r, f_r,
):
    r, c = lax.axis_index("row"), lax.axis_index("col")
    z, core = r // 2, lax.rem(r, 2)
    other = 1 - core
    mate = r + 1 - 2 * core
    height = a_ref.shape[0]
    upper = lax.broadcasted_iota(jnp.int32, (128, 128), 0) <= lax.broadcasted_iota(
        jnp.int32, (128, 128), 1
    )
    plane = [lax.rem(c + k, N) for k in range(1, N)]
    line = [lax.rem(r + k, N) for k in range(1, N)]
    ring = [lax.rem(z + k, NZ) for k in range(1, NZ)]

    def got(ref, sem):
        remote(ref, ref, ss.at[0], sem, r, c).wait_recv()

    def when(cond, run):
        pl.when(cond)(run)

    cur[...] = a_ref[...]
    zown = 0

    for p in range(PANELS):
        first, lead = p * BLOCK, (p + 1) * BLOCK
        owner, off = lead // height, lead % height
        count = iter(range(1, 60))
        sends = []

        class Group:
            def __init__(self, rows):
                self.sem = ss.at[next(count)]
                self.rows = rows
                self.copies = []

            def add(self, src, dst, sem, row, col):
                self.copies.append(remote(src, dst, self.sem, sem, row, col))
                return self.copies[-1]

            def start(self):
                for copy in self.copies:
                    copy.start()

            def left(self):
                if self.rows <= 512:
                    view = wc.at[pl.ds(0, self.rows)]
                else:
                    view = pr.at[:, pl.ds(0, self.rows // 2)]
                remote(view, view, self.sem, self.sem, r, c).wait_send()

        def group_of(rows, items):
            made = Group(rows)
            for item in items:
                made.add(*item)
            return made

        def go(made):
            made.start()
            sends.append(made)

        def slot(a, i, h):
            return tall.at[p, a, i, h]

        def aer_at(i):
            return aefr.at[at(i, 32)] if p == 0 else aepr

        def aec_at(i):
            return aefc.at[at(i, 32)] if p == 0 else aepc

        spot = core * NZ + z

        if p == 0:

            @pl.when(r == 0)
            def _():
                cols = c * height + lax.broadcasted_iota(jnp.int32, (BLOCK, height), 1)
                pct[...] = jnp.where(cols >= lead, cur[first : first + BLOCK, :], 0.0)
                gram[...] = dot(pct[...], pct[...], (1, 1))
                gin[p, c] = gram[at(c, 16), :]

            @pl.when(c == 0)
            def _():
                rows = r * height + lax.broadcasted_iota(jnp.int32, (height, BLOCK), 0)
                pr[p] = jnp.where(rows >= lead, cur[:, first : first + BLOCK], 0.0)

        else:

            @pl.when(r == 0)
            def _():
                gram[...] = dot(pc[p], pc[p], (0, 0))
                gin[p, c] = gram[at(c, 16), :]

        def row8(i, h):
            return pl.ds(pl.multiple_of(off + 16 * i + 8 * h, 8), 8)

        g_out = group_of(240, [(gram.at[at(i, 16)], gin.at[p, c], g_r.at[p], r, i) for i in plane])
        top_out = group_of(
            240,
            [(pr.at[p, row8(i, h)], tsrc.at[p, 1, h], b_r.at[p, 1], r, i) for i in plane for h in (0, 1)],
        )
        ee_out = group_of(
            240,
            [(aer.at[row8(i, h)], tsrc.at[p, 2, h], b_r.at[p, 2], r, i) for i in plane for h in (0, 1)],
        )
        down = [
            group_of(
                120,
                [
                    (tsrc.at[p, a, lax.rem(i, 2)], slot(a, c, lax.rem(i, 2)), td_r.at[p, a], i, c)
                    for i in line
                ],
            )
            for a in range(3)
        ]
        share = [
            group_of(120, [(slot(a, c, core), slot(a, c, core), t_r.at[p, a], r, i) for i in plane])
            for a in range(3)
        ]
        cross = [
            group_of(128, [(tall.at[p, a, :, core], tall.at[p, a, :, core], tm_r.at[p, a], mate, c)])
            for a in range(3)
        ]
        ae_r = group_of(480, [(aer.at[at(i, 32)], aer_at(i), ar_r.at[p], r, i) for i in plane])
        ae_c = group_of(
            480,
            [
                (aec.at[at(lax.rem(i, 2) * NZ + i // 2, 32)], aec_at(lax.rem(i, 2) * NZ + i // 2), ac_r.at[p], i, c)
                for i in line
            ],
        )
        relay = (core == 0) & (z != 0)
        if p == 0:

            def pr_part(q, sem, i):
                return (pr.at[p, at(q, 32)], pr.at[p, at(q, 32)], sem.at[0], r, i)

            def pc_part(q, sem, row):
                return (pc.at[p, at(q, 64)], pc.at[p, at(q, 64)], sem.at[0], row, c)

            root_r = group_of(480, [pr_part(i, pa_r, i) for i in range(1, N)])
            root_own = group_of(480, [pr_part(0, p_r, i) for i in range(1, N)])
            root_c = group_of(
                896,
                [pc_part(q, qa_r, 2 * q) for q in range(1, NZ)]
                + [pc_part(0, q_r, 2 * q) for q in range(1, NZ)],
            )
            ahead_r = group_of(448, [pr_part(c, p_r, i) for i in plane])
            ahead_c = group_of(384, [pc_part(z, q_r, 2 * q) for q in ring])
            low_c = group_of(512, [(pc.at[p], pc.at[p], ql_r.at[0], r + 1, c)])

        @pl.when(c == owner)
        def _():
            aer[...] = cur[:, off : off + BLOCK]
            mine = aer[at(c, 32), :]
            if p == 0:
                aefr[at(c, 32), :] = mine
            else:
                aepr[...] = mine

        @pl.when(r == owner)
        def _():
            aec[...] = cur[off : off + BLOCK, :].T
            mine = aec[at(spot, 32), :]
            if p == 0:
                aefc[at(spot, 32), :] = mine
            else:
                aepc[...] = mine

        if p == 0:
            greet(r, c)

        when(r == 0, g_out.start)

        @pl.when((r == owner) & (c == 0))
        def _():
            for h in (0, 1):
                tsrc[p, 1, h] = pr[p, row8(c, h), :]

        @pl.when((r == owner) & (c == owner))
        def _():
            for h in (0, 1):
                tsrc[p, 2, h] = aer[row8(c, h), :]

        when((r == owner) & (c == 0), top_out.start)
        when((r == owner) & (c == owner), ee_out.start)
        if p == 0:
            when(c == 0, root_r.start)

        swap = group_of(256, [(wc.at[at(other, 256)], half.at[p], h_r.at[p], mate, c)])
        mswap = group_of(128, [(m.at[:, other], mpair.at[p], s_r.at[p], mate, c)])
        yswap = group_of(128, [(ybuf.at[:, other], yin.at[p], ys_r.at[p], mate, c)])
        y_own = group_of(120, [(ybuf.at[i, core], iny.at[p, c], yt_r.at[p], r, i) for i in plane])
        y_mate = group_of(120, [(yin.at[p, i], iny.at[p, c], yt_r.at[p], r, i) for i in plane])

        def products():
            wc[...] = dot3(cur[...], pr[p], (0, 0))
            go(swap)
            if p == 0:
                when(core == 1, lambda: got(pc.at[p], ql_r.at[0]))
            wr[...] = dot3(cur[...], pc[p])

            @pl.when(r == owner)
            def _():
                ybuf[...] = wr[off : off + BLOCK, :].reshape(N, 2, 8, BLOCK)
                yswap.start()

            m[...] = dot(pr[p], wr[...], (0, 0)).reshape(N, 2, 8, BLOCK)
            go(mswap)

        def scatter():
            got(mpair.at[p], s_r.at[p])
            mh[...] = m[:, core] + mpair[p]
            go(group_of(120, [(mh.at[i], inm.at[p, c], m_r.at[p], r, i) for i in plane]))
            inm[p, c] = mh[c]

            @pl.when(r == owner)
            def _():
                y_own.start()
                iny[p, c] = ybuf[c, core]

            @pl.when(mate == owner)
            def _():
                got(yin.at[p], ys_r.at[p])
                y_mate.start()
                iny[p, c] = yin[p, c]

            go(group_of(480, [(wr.at[at(i, 32)], inr.at[p, c], r_r.at[p], r, i) for i in plane]))
            inr[p, c] = wr[at(c, 32), :]
            got(half.at[p], h_r.at[p])
            hsum[...] = (wc[at(core, 256), :] + half[p]).reshape(NZ, 32, BLOCK)
            zin[p, z] = hsum[z]
            go(group_of(224, [(hsum.at[q], zin.at[p, z], z_r.at[p], 2 * q + core, c) for q in ring]))

        if p > 0:
            products()

        @pl.when(r == 0)
        def _():
            got(gin.at[p, pl.ds(0, N - 1)], g_r.at[p])
            total = gin[p, 0]
            for i in range(1, N):
                total = total + gin[p, i]
            tsrc[p, 0] = total.reshape(2, 8, BLOCK)
            tall[p, 0, c, core] = tsrc[p, 0, core]
            down[0].start()

        def own_rest():
            @pl.when(r == owner)
            def _():
                for a, holder in ((1, 0), (2, owner)):
                    when(c != holder, lambda a=a: got(tsrc.at[p, a], b_r.at[p, a]))
                    tall[p, a, c, core] = tsrc[p, a, core]
                    down[a].start()

        if p > 0:
            own_rest()
        when(r != 0, lambda: got(slot(0, c, core), td_r.at[p, 0]))
        share[0].start()
        if p == 0:
            own_rest()

        if p == 0:
            @pl.when(r == 0)
            def _():
                pc[p] = pct[...].T
                root_c.start()
                low_c.start()

            @pl.when(relay)
            def _():
                got(pc.at[p, at(z, 64)], qa_r.at[0])
                for q, copy in zip(ring, ahead_c.copies):
                    when(q != 0, copy.start)

        def share_rest():
            for a in (1, 2):
                when(r != owner, lambda a=a: got(slot(a, c, core), td_r.at[p, a]))
                share[a].start()

        if p > 0:
            share_rest()

        def slots(a):
            return tall.at[p, a, pl.ds(0, N - 1), core]

        got(slots(0), t_r.at[p, 0])
        cross[0].start()

        if p == 0:

            when(c == 0, root_own.start)

            @pl.when(c != 0)
            def _():
                got(pr.at[p, at(c, 32)], pa_r.at[0])
                for i, copy in zip(plane, ahead_r.copies):
                    when(i != 0, copy.start)

            share_rest()

        else:
            scatter()
            when(c == owner, ae_r.start)
            when(r == owner, ae_c.start)

        got(tall.at[p, 0, :, other], tm_r.at[p, 0])

        g = tall[p, 0].reshape(BLOCK, BLOCK)
        aug[...] = g[:128, :]
        strips(aug, lt_ref, 0, 4, False)
        lt_ref[:128, :128] = jnp.where(upper, lt_ref[:128, :128], 0.0)
        lt01 = lt_ref[:128, 128:]
        aug2[...] = g[128:, 128:] - dot(lt01, lt01, (0, 0))
        lt_ref[128:, :128] = jnp.zeros((128, 128), F32)

        def cross_rest():
            for a in (1, 2):
                got(slots(a), t_r.at[p, a])
                cross[a].start()

        if p > 0:
            cross_rest()

        if p == 0:

            @pl.when(relay)
            def _():
                got(pc.at[p, pl.ds(0, 448)], q_r.at[0])
                low_c.start()

            @pl.when(c != 0)
            def _():
                got(pr.at[p, pl.ds(0, 480)], p_r.at[0])

            products()
            scatter()
            when(c == owner, ae_r.start)
            when(r == owner, ae_c.start)

        strips(aug2, low, 0, 4, False)
        lt_ref[128:, 128:] = jnp.where(upper, low[...], 0.0)
        lt = lt_ref[...]

        def sum_m():
            got(inm.at[p, pl.ds(0, N - 1)], m_r.at[p])
            total = inm[p, 0]
            for i in range(1, N):
                total = total + inm[p, i]
            mring[p, z, 0] = total

            @pl.when(z == zown)
            def _():
                got(iny.at[p, pl.ds(0, N - 1)], yt_r.at[p])
                total = iny[p, 0]
                for i in range(1, N):
                    total = total + iny[p, i]
                mring[p, z, 1] = total

            @pl.when(z != zown)
            def _():
                mring[p, z, 1] = jnp.zeros((8, BLOCK), F32)

            go(group_of(112, [(mring.at[p, z], mring.at[p, z], u_r.at[p], 2 * q + core, c) for q in ring]))

        def sum_x():
            got(inr.at[p, pl.ds(0, N - 1)], r_r.at[p])
            total = inr[p, 0]
            for i in range(1, N):
                total = total + inr[p, i]
            mine = aer_at(c)
            when(c != owner, lambda: got(mine, ar_r.at[p]))
            xr[p, at(c, 32), :] = total + dot(mine[...], lt)
            own = xr.at[p, at(c, 32)]
            go(group_of(480, [(own, own, x_r.at[p], r, i) for i in plane]))
            got(zin.at[p, pl.ds(0, NZ - 1)], z_r.at[p])
            total = zin[p, 0]
            for q in range(1, NZ):
                total = total + zin[p, q]
            mine_c = aec_at(spot)
            when(r != owner, lambda: got(mine_c, ac_r.at[p]))
            xc[p, at(spot, 32), :] = total + dot(mine_c[...], lt)
            own_c = xc.at[p, at(spot, 32)]
            go(group_of(224, [(own_c, own_c, y_r.at[p], 2 * q + core, c) for q in ring]))

        if p == 0:
            cross_rest()
        else:
            sum_m()

        got(tall.at[p, 1, :, other], tm_r.at[p, 1])
        top = tall[p, 1].reshape(BLOCK, BLOCK)
        n_ref[...] = tall[p, 0].reshape(BLOCK, BLOCK) + dot(top, lt, (0, 0))
        aug[...] = n_ref[:128, :]
        strips(aug, None, 0, 2, True)
        if p == 0:
            sum_m()
        else:
            sum_x()
        strips(aug, None, 2, 4, True)
        if p == 0:
            sum_x()

        d0 = aug[:, :128]
        n01 = aug[:, 128:]
        n10d = dot(n_ref[128:, :128], d0)
        aug2[...] = n_ref[128:, 128:] - dot(n_ref[128:, :128], n01)
        def hand_out():
            got(mring.at[p, pl.ds(0, NZ - 1)], u_r.at[p])
            total = mring[p, 0]
            for q in range(1, NZ):
                total = total + mring[p, q]
            ball[p, :, c, core] = total
            own_b = ball.at[p, :, c, core]
            go(group_of(240, [(own_b, own_b, v_r.at[p], r, i) for i in plane]))

        strips(aug2, None, 0, 2, True)
        hand_out()
        if p == 0:
            own_c = aefc.at[at(spot, 32)]
            go(group_of(224, [(own_c, own_c, ag_r.at[0], 2 * q + core, c) for q in ring]))
            own = aefr.at[at(c, 32)]
            go(group_of(480, [(own, own, af_r.at[0], r, i) for i in plane]))
        strips(aug2, None, 2, 4, True)
        part = xc.at[p, at(core, 256)]
        got(xc.at[p, pl.ds(0, 224)], y_r.at[p])
        go(group_of(256, [(part, part, w_r.at[p], mate, c)]))
        e = aug2[...]
        k10 = -dot(e, n10d)
        k_ref[:128, :128] = d0 - dot(n01, k10)
        k_ref[:128, 128:] = -dot(n01, e)
        k_ref[128:, :128] = k10
        k_ref[128:, 128:] = e

        zr[...] = pr[p]
        zc[...] = pc[p]

        @pl.when(r == owner)
        def _():
            zr[off : off + BLOCK, :] = zr[off : off + BLOCK, :] + lt_ref[...]

        @pl.when(c == owner)
        def _():
            zc[off : off + BLOCK, :] = zc[off : off + BLOCK, :] + lt_ref[...]

        got(tall.at[p, 2, :, other], tm_r.at[p, 2])
        got(ball.at[p, :, pl.ds(0, N - 1), core], v_r.at[p])
        final = ball.at[p, :, :, core]
        go(group_of(256, [(final, final, f_r.at[p], mate, c)]))
        got(xr.at[p, pl.ds(0, 480)], x_r.at[p])
        ux[...] = dot3(xr[p], k_ref[...])
        got(xc.at[p, pl.ds(0, 256)], w_r.at[p])
        uy[...] = dot3(xc[p], k_ref[...])
        got(ball.at[p, :, :, other], f_r.at[p])

        ytop = ball[p, 1].reshape(BLOCK, BLOCK)
        xtop = ytop + dot(tall[p, 2].reshape(BLOCK, BLOCK), lt)
        inner = ball[p, 0].reshape(BLOCK, BLOCK) + dot(ytop, lt, (0, 0)) + dot(lt, xtop, (0, 0))
        if p == 0:
            part = aefc.at[at(core, 256)]
            got(aefc.at[pl.ds(0, 224)], ag_r.at[0])
            go(group_of(256, [(part, part, am_r.at[0], mate, c)]))
        coupled = 0.5 * dot(k_ref[...], dot(inner, k_ref[...]), (0, 0))
        ur = ux[...] - dot3(zr[...], coupled)
        uc = uy[...] - dot3(zc[...], coupled)
        dest = out_ref if p == PANELS - 1 else cur
        dest[...] = cur[...] - dot3(ur, zc[...], (1, 1)) - dot3(zr[...], uc, (1, 1))
        if p == 0:
            ztop = top + lt
            utop = dot(xtop, k_ref[...]) - dot(ztop, coupled)
            rows = lax.broadcasted_iota(jnp.int32, (height, BLOCK), 0)
            got(aefr.at[pl.ds(0, 480)], af_r.at[0])
            near = aefr[...] - dot3(ur, ztop, (1, 1)) - dot3(zr[...], utop, (1, 1))
            pr[1] = jnp.where(r * height + rows >= lead + BLOCK, near, 0.0)
            got(aefc.at[pl.ds(0, 256)], am_r.at[0])
            near = aefc[...] - dot3(uc, ztop, (1, 1)) - dot3(zc[...], utop, (1, 1))
            pc[1] = jnp.where(c * height + rows >= lead + BLOCK, near, 0.0)

        for made in sends + share + cross:
            made.left()
        when(r == 0, g_out.left)
        when(r == 0, down[0].left)
        for made in (down[1], down[2], ae_c, y_own, yswap):
            when(r == owner, made.left)
        when(mate == owner, y_mate.left)
        when((r == owner) & (c == 0), top_out.left)
        when((r == owner) & (c == owner), ee_out.left)
        when(c == owner, ae_r.left)
        if p == 0:
            when(r == 0, root_c.left)
            when(c == 0, root_r.left)
            when(c == 0, root_own.left)
            when(c != 0, ahead_r.left)
            when(relay, ahead_c.left)
            when(core == 0, low_c.left)


def per_device(matrix):
    dma = pltpu.SemaphoreType.DMA

    def buf(*shape):
        return pltpu.VMEM(shape, F32)

    return pl.pallas_call(
        kernel,
        out_shape=jax.ShapeDtypeStruct(matrix.shape, F32),
        in_specs=[VMEM],
        out_specs=VMEM,
        scratch_shapes=[
            buf(512, 512),
            buf(2, 512, 256),
            buf(256, 512),
            buf(2, 512, 256),
            buf(512, 256),
            buf(512, 256),
            buf(32, 256),
            buf(32, 256),
            buf(512, 256),
            buf(512, 256),
            buf(256, 256),
            buf(2, N, 16, 256),
            buf(2, 3, 2, 8, 256),
            buf(2, 3, N, 2, 8, 256),
            buf(256, 256),
            buf(256, 256),
            buf(256, 256),
            buf(128, 256),
            buf(128, 128),
            buf(128, 128),
            buf(512, 256),
            buf(512, 256),
            buf(512, 256),
            buf(512, 256),
            buf(N, 2, 8, 256),
            buf(2, N, 8, 256),
            buf(N, 8, 256),
            buf(N, 2, 8, 256),
            buf(2, N, 8, 256),
            buf(2, N, 32, 256),
            buf(2, N, 8, 256),
            buf(2, N, 8, 256),
            buf(2, 256, 256),
            buf(NZ, 32, 256),
            buf(2, NZ, 32, 256),
            buf(2, 512, 256),
            buf(2, 512, 256),
            buf(2, NZ, 2, 8, 256),
            buf(2, 2, N, 2, 8, 256),
            buf(512, 256),
            buf(512, 256),
            dma((60,)),
            dma((2,)),
            dma((2, 3)),
            dma((2, 3)),
            dma((2, 3)),
            dma((2, 3)),
            dma((1,)),
            dma((1,)),
            dma((1,)),
            dma((1,)),
            dma((1,)),
            dma((2,)),
            dma((2,)),
            dma((1,)),
            dma((1,)),
            dma((1,)),
            dma((2,)),
            dma((2,)),
            dma((2,)),
            dma((2,)),
            dma((2,)),
            dma((2,)),
            dma((2,)),
            dma((2,)),
            dma((2,)),
            dma((2,)),
            dma((2,)),
            dma((2,)),
            dma((2,)),
        ],
        compiler_params=pltpu.CompilerParams(collective_id=0, has_side_effects=True),
        name="reduce_panels",
    )(matrix)


def solution(mesh):
    return jax.shard_map(
        per_device, mesh=mesh, in_specs=(P("row", "col"),), out_specs=P("row", "col"), check_vma=False
    )
```

```python
import jax
import jax.numpy as jnp
from jax import lax
from jax.experimental import pallas as pl
from jax.experimental.pallas import tpu as pltpu
from jax.sharding import PartitionSpec as P

BLOCK = 256
PANELS = 2
N = 16
NZ = 8
HIGH = lax.Precision.HIGHEST
F32 = jnp.float32
MESH = pl.DeviceIdType.MESH
VMEM = pl.BlockSpec(memory_space=pltpu.VMEM)


def dot(left, right, over=(1, 0)):
    return lax.dot_general(
        left,
        right,
        (((over[0],), (over[1],)), ((), ())),
        precision=HIGH,
        preferred_element_type=F32,
    )


def dot3(left, right, over=(1, 0)):
    def split(x):
        high = x.astype(jnp.bfloat16)
        return high, (x - high.astype(F32)).astype(jnp.bfloat16)

    def part(a, b):
        return lax.dot_general(
            a, b, (((over[0],), (over[1],)), ((), ())), preferred_element_type=F32
        )

    lh, ll = split(left)
    rh, rl = split(right)
    return part(lh, rh) + (part(lh, rl) + part(ll, rh))


def recip(x):
    r = pl.reciprocal(x, approx=True)
    return r * (2.0 - x * r)


def lanes(block, index):
    return jnp.take_along_axis(block, jnp.full((8, 128), index, jnp.int32), axis=1)


def times(scale, row):
    if row.shape[1] == 128:
        return scale * row
    return jnp.concatenate([scale * row[:, :128], scale * row[:, 128:]], axis=1)


def put(rows):
    sub = lax.broadcasted_iota(jnp.int32, rows[0].shape, 0)
    out = rows[0]
    for s in range(1, 8):
        out = jnp.where(sub == s, rows[s], out)
    return out


def group(aug, out, base, inverse):
    width = aug.shape[1]
    lane = lax.broadcasted_iota(jnp.int32, (8, 128), 1)
    inside = (lane >= base) & (lane < base + 8)

    def left(block, value):
        if width == 128:
            return jnp.where(inside, value, block)
        return jnp.concatenate([jnp.where(inside, value, block[:, :128]), block[:, 128:]], axis=1)

    rows = [jnp.broadcast_to(aug[pl.ds(base + s, 1), :], (8, width)) for s in range(8)]
    e = [[None] * 8 for _ in range(8)]
    for t in range(8):
        for s in range(8 if inverse else t + 1):
            e[s][t] = lanes(rows[s][:, :128], base + t)
    if inverse:
        rows = [left(rows[s], (lane == base + s).astype(F32)) for s in range(8)]
    inv = []
    for s in range(8):
        inv.append(recip(e[s][s]))
        for t in range(s + 1, 8):
            f = (e[t][s] if inverse else e[s][t]) * inv[s]
            for u in range(s + 1 if inverse else t, 8):
                e[t][u] = e[t][u] - f * e[s][u]
            rows[t] = rows[t] - times(f, rows[s])
    if not inverse:
        out[pl.ds(base, 8), :] = put([times(lax.rsqrt(e[s][s]), rows[s]) for s in range(8)])
    solved = [None] * 8
    for s in reversed(range(8)):
        acc = rows[s]
        for t in range(s + 1, 8):
            acc = acc - times(e[s][t], solved[t])
        solved[s] = times(inv[s], acc)
    own = put(solved)
    strip = pl.multiple_of(base // 32 * 32, 32)
    blocks = [aug[pl.ds(strip + 8 * k, 8), :] for k in range(4)]
    after = [left(b, 0.0) if inverse else b for b in blocks]
    for s in range(8):
        for k in range(4):
            after[k] = after[k] - times(lanes(blocks[k][:, :128], base + s), solved[s])
    for k in range(4):
        aug[pl.ds(strip + 8 * k, 8), :] = jnp.where(strip + 8 * k == base, own, after[k])


def strips(aug, out, lo, hi, inverse):
    row = lax.broadcasted_iota(jnp.int32, (128, 128), 0) // 32
    lane = lax.broadcasted_iota(jnp.int32, (128, 128), 1) // 32

    def one(k, q):
        group(aug, out, pl.multiple_of(32 * q + 8 * k, 8), inverse)
        return q

    def strip(q, carry):
        lax.fori_loop(0, 4, one, q)
        aim = (lane == q) & ((row != q) if inverse else (row > q))
        near = aug[:, :128]
        prod = dot(jnp.where(aim, near, 0.0), aug[...])
        if inverse:
            near = jnp.where(aim, 0.0, near)
        aug[:, :128] = near - prod[:, :128]
        if aug.shape[1] > 128:
            aug[:, 128:] = aug[:, 128:] - prod[:, 128:]
        return carry

    lax.fori_loop(lo, hi, strip, 0)


def remote(src, dst, send, recv, row, col):
    return pltpu.make_async_remote_copy(
        src_ref=src,
        dst_ref=dst,
        send_sem=send,
        recv_sem=recv,
        device_id=(row, col),
        device_id_type=MESH,
    )


def greet(r, c):
    barrier = pltpu.get_barrier_semaphore()
    for k in range(1, N):
        pl.semaphore_signal(barrier, inc=1, device_id=(r, lax.rem(c + k, N)), device_id_type=MESH)
        pl.semaphore_signal(barrier, inc=1, device_id=(lax.rem(r + k, N), c), device_id_type=MESH)
    pl.semaphore_wait(barrier, 2 * (N - 1))


def at(index, size):
    return pl.ds(pl.multiple_of(index * size, size), size)


def kernel(
    a_ref, out_ref,
    cur, pr, pct, pc, aer, aec, aepr, aepc, aefr, aefc, gram, gin, tsrc, tall, lt_ref, k_ref, n_ref, aug, aug2, low,
    zr, zc, wr, wc, m, mpair, mh, ybuf, yin, inr, inm, iny, half, hsum, zin, xr, xc, mring, ball,
    ux, uy,
    ss, g_r, b_r, td_r, t_r, tm_r, pa_r, p_r, qa_r, q_r, ql_r, ar_r, ac_r, af_r, ag_r, am_r,
    r_r, m_r, yt_r, ys_r, h_r, z_r, x_r, y_r, w_r, s_r, u_r, v_r, f_r,
):
    r, c = lax.axis_index("row"), lax.axis_index("col")
    z, core = r // 2, lax.rem(r, 2)
    other = 1 - core
    mate = r + 1 - 2 * core
    height = a_ref.shape[0]
    upper = lax.broadcasted_iota(jnp.int32, (128, 128), 0) <= lax.broadcasted_iota(
        jnp.int32, (128, 128), 1
    )
    plane = [lax.rem(c + k, N) for k in range(1, N)]
    line = [lax.rem(r + k, N) for k in range(1, N)]
    ring = [lax.rem(z + k, NZ) for k in range(1, NZ)]

    def got(ref, sem):
        remote(ref, ref, ss.at[0], sem, r, c).wait_recv()

    def when(cond, run):
        pl.when(cond)(run)

    cur[...] = a_ref[...]
    zown = 0

    for p in range(PANELS):
        first, lead = p * BLOCK, (p + 1) * BLOCK
        owner, off = lead // height, lead % height
        count = iter(range(1, 60))
        sends = []

        class Group:
            def __init__(self, rows):
                self.sem = ss.at[next(count)]
                self.rows = rows
                self.copies = []

            def add(self, src, dst, sem, row, col):
                self.copies.append(remote(src, dst, self.sem, sem, row, col))
                return self.copies[-1]

            def start(self):
                for copy in self.copies:
                    copy.start()

            def left(self):
                if self.rows <= 512:
                    view = wc.at[pl.ds(0, self.rows)]
                else:
                    view = pr.at[:, pl.ds(0, self.rows // 2)]
                remote(view, view, self.sem, self.sem, r, c).wait_send()

        def group_of(rows, items):
            made = Group(rows)
            for item in items:
                made.add(*item)
            return made

        def go(made):
            made.start()
            sends.append(made)

        def slot(a, i, h):
            return tall.at[p, a, i, h]

        def aer_at(i):
            return aefr.at[at(i, 32)] if p == 0 else aepr

        def aec_at(i):
            return aefc.at[at(i, 32)] if p == 0 else aepc

        spot = core * NZ + z

        if p == 0:

            @pl.when(r == 0)
            def _():
                cols = c * height + lax.broadcasted_iota(jnp.int32, (BLOCK, height), 1)
                pct[...] = jnp.where(cols >= lead, cur[first : first + BLOCK, :], 0.0)
                gram[...] = dot(pct[...], pct[...], (1, 1))
                gin[p, c] = gram[at(c, 16), :]

            @pl.when(c == 0)
            def _():
                rows = r * height + lax.broadcasted_iota(jnp.int32, (height, BLOCK), 0)
                pr[p] = jnp.where(rows >= lead, cur[:, first : first + BLOCK], 0.0)

        else:

            @pl.when(r == 0)
            def _():
                gram[...] = dot(pc[p], pc[p], (0, 0))
                gin[p, c] = gram[at(c, 16), :]

        def row8(i, h):
            return pl.ds(pl.multiple_of(off + 16 * i + 8 * h, 8), 8)

        g_out = group_of(240, [(gram.at[at(i, 16)], gin.at[p, c], g_r.at[p], r, i) for i in plane])
        top_out = group_of(
            240,
            [(pr.at[p, row8(i, h)], tsrc.at[p, 1, h], b_r.at[p, 1], r, i) for i in plane for h in (0, 1)],
        )
        ee_out = group_of(
            240,
            [(aer.at[row8(i, h)], tsrc.at[p, 2, h], b_r.at[p, 2], r, i) for i in plane for h in (0, 1)],
        )
        down = [
            group_of(
                120,
                [
                    (tsrc.at[p, a, lax.rem(i, 2)], slot(a, c, lax.rem(i, 2)), td_r.at[p, a], i, c)
                    for i in line
                ],
            )
            for a in range(3)
        ]
        share = [
            group_of(120, [(slot(a, c, core), slot(a, c, core), t_r.at[p, a], r, i) for i in plane])
            for a in range(3)
        ]
        cross = [
            group_of(128, [(tall.at[p, a, :, core], tall.at[p, a, :, core], tm_r.at[p, a], mate, c)])
            for a in range(3)
        ]
        ae_r = group_of(480, [(aer.at[at(i, 32)], aer_at(i), ar_r.at[p], r, i) for i in plane])
        ae_c = group_of(
            480,
            [
                (aec.at[at(lax.rem(i, 2) * NZ + i // 2, 32)], aec_at(lax.rem(i, 2) * NZ + i // 2), ac_r.at[p], i, c)
                for i in line
            ],
        )
        relay = (core == 0) & (z != 0)
        if p == 0:

            def pr_part(q, sem, i):
                return (pr.at[p, at(q, 32)], pr.at[p, at(q, 32)], sem.at[0], r, i)

            def pc_part(q, sem, row):
                return (pc.at[p, at(q, 64)], pc.at[p, at(q, 64)], sem.at[0], row, c)

            root_r = group_of(480, [pr_part(i, pa_r, i) for i in range(1, N)])
            root_own = group_of(480, [pr_part(0, p_r, i) for i in range(1, N)])
            root_c = group_of(
                896,
                [pc_part(q, qa_r, 2 * q) for q in range(1, NZ)]
                + [pc_part(0, q_r, 2 * q) for q in range(1, NZ)],
            )
            ahead_r = group_of(448, [pr_part(c, p_r, i) for i in plane])
            ahead_c = group_of(384, [pc_part(z, q_r, 2 * q) for q in ring])
            low_c = group_of(512, [(pc.at[p], pc.at[p], ql_r.at[0], r + 1, c)])

        @pl.when(c == owner)
        def _():
            aer[...] = cur[:, off : off + BLOCK]
            mine = aer[at(c, 32), :]
            if p == 0:
                aefr[at(c, 32), :] = mine
            else:
                aepr[...] = mine

        @pl.when(r == owner)
        def _():
            aec[...] = cur[off : off + BLOCK, :].T
            mine = aec[at(spot, 32), :]
            if p == 0:
                aefc[at(spot, 32), :] = mine
            else:
                aepc[...] = mine

        if p == 0:
            greet(r, c)

        when(r == 0, g_out.start)

        @pl.when((r == owner) & (c == 0))
        def _():
            for h in (0, 1):
                tsrc[p, 1, h] = pr[p, row8(c, h), :]

        @pl.when((r == owner) & (c == owner))
        def _():
            for h in (0, 1):
                tsrc[p, 2, h] = aer[row8(c, h), :]

        when((r == owner) & (c == 0), top_out.start)
        when((r == owner) & (c == owner), ee_out.start)
        if p == 0:
            when(c == 0, root_r.start)

        swap = group_of(256, [(wc.at[at(other, 256)], half.at[p], h_r.at[p], mate, c)])
        mswap = group_of(128, [(m.at[:, other], mpair.at[p], s_r.at[p], mate, c)])
        yswap = group_of(128, [(ybuf.at[:, other], yin.at[p], ys_r.at[p], mate, c)])
        y_own = group_of(120, [(ybuf.at[i, core], iny.at[p, c], yt_r.at[p], r, i) for i in plane])
        y_mate = group_of(120, [(yin.at[p, i], iny.at[p, c], yt_r.at[p], r, i) for i in plane])

        def products():
            wc[...] = dot3(cur[...], pr[p], (0, 0))
            go(swap)
            if p == 0:
                when(core == 1, lambda: got(pc.at[p], ql_r.at[0]))
            wr[...] = dot3(cur[...], pc[p])

            @pl.when(r == owner)
            def _():
                ybuf[...] = wr[off : off + BLOCK, :].reshape(N, 2, 8, BLOCK)
                yswap.start()

            m[...] = dot3(pr[p], wr[...], (0, 0)).reshape(N, 2, 8, BLOCK)
            go(mswap)

        def scatter():
            got(mpair.at[p], s_r.at[p])
            mh[...] = m[:, core] + mpair[p]
            go(group_of(120, [(mh.at[i], inm.at[p, c], m_r.at[p], r, i) for i in plane]))
            inm[p, c] = mh[c]

            @pl.when(r == owner)
            def _():
                y_own.start()
                iny[p, c] = ybuf[c, core]

            @pl.when(mate == owner)
            def _():
                got(yin.at[p], ys_r.at[p])
                y_mate.start()
                iny[p, c] = yin[p, c]

            go(group_of(480, [(wr.at[at(i, 32)], inr.at[p, c], r_r.at[p], r, i) for i in plane]))
            inr[p, c] = wr[at(c, 32), :]
            got(half.at[p], h_r.at[p])
            hsum[...] = (wc[at(core, 256), :] + half[p]).reshape(NZ, 32, BLOCK)
            zin[p, z] = hsum[z]
            go(group_of(224, [(hsum.at[q], zin.at[p, z], z_r.at[p], 2 * q + core, c) for q in ring]))

        if p > 0:
            products()

        @pl.when(r == 0)
        def _():
            got(gin.at[p, pl.ds(0, N - 1)], g_r.at[p])
            total = gin[p, 0]
            for i in range(1, N):
                total = total + gin[p, i]
            tsrc[p, 0] = total.reshape(2, 8, BLOCK)
            tall[p, 0, c, core] = tsrc[p, 0, core]
            down[0].start()

        def own_rest():
            @pl.when(r == owner)
            def _():
                for a, holder in ((1, 0), (2, owner)):
                    when(c != holder, lambda a=a: got(tsrc.at[p, a], b_r.at[p, a]))
                    tall[p, a, c, core] = tsrc[p, a, core]
                    down[a].start()

        if p > 0:
            own_rest()
        when(r != 0, lambda: got(slot(0, c, core), td_r.at[p, 0]))
        share[0].start()
        if p == 0:
            own_rest()

        if p == 0:
            @pl.when(r == 0)
            def _():
                pc[p] = pct[...].T
                root_c.start()
                low_c.start()

            @pl.when(relay)
            def _():
                got(pc.at[p, at(z, 64)], qa_r.at[0])
                for q, copy in zip(ring, ahead_c.copies):
                    when(q != 0, copy.start)

        def share_rest():
            for a in (1, 2):
                when(r != owner, lambda a=a: got(slot(a, c, core), td_r.at[p, a]))
                share[a].start()

        if p > 0:
            share_rest()

        def slots(a):
            return tall.at[p, a, pl.ds(0, N - 1), core]

        got(slots(0), t_r.at[p, 0])
        cross[0].start()

        if p == 0:

            when(c == 0, root_own.start)

            @pl.when(c != 0)
            def _():
                got(pr.at[p, at(c, 32)], pa_r.at[0])
                for i, copy in zip(plane, ahead_r.copies):
                    when(i != 0, copy.start)

            share_rest()

        else:
            scatter()
            when(c == owner, ae_r.start)
            when(r == owner, ae_c.start)

        got(tall.at[p, 0, :, other], tm_r.at[p, 0])

        g = tall[p, 0].reshape(BLOCK, BLOCK)
        aug[...] = g[:128, :]
        strips(aug, lt_ref, 0, 4, False)
        lt_ref[:128, :128] = jnp.where(upper, lt_ref[:128, :128], 0.0)
        lt01 = lt_ref[:128, 128:]
        aug2[...] = g[128:, 128:] - dot(lt01, lt01, (0, 0))
        lt_ref[128:, :128] = jnp.zeros((128, 128), F32)

        def cross_rest():
            for a in (1, 2):
                got(slots(a), t_r.at[p, a])
                cross[a].start()

        if p > 0:
            cross_rest()

        if p == 0:

            @pl.when(relay)
            def _():
                got(pc.at[p, pl.ds(0, 448)], q_r.at[0])
                low_c.start()

            @pl.when(c != 0)
            def _():
                got(pr.at[p, pl.ds(0, 480)], p_r.at[0])

            products()
            scatter()
            when(c == owner, ae_r.start)
            when(r == owner, ae_c.start)

        strips(aug2, low, 0, 4, False)
        lt_ref[128:, 128:] = jnp.where(upper, low[...], 0.0)
        lt = lt_ref[...]

        def sum_m():
            got(inm.at[p, pl.ds(0, N - 1)], m_r.at[p])
            total = inm[p, 0]
            for i in range(1, N):
                total = total + inm[p, i]
            mring[p, z, 0] = total

            @pl.when(z == zown)
            def _():
                got(iny.at[p, pl.ds(0, N - 1)], yt_r.at[p])
                total = iny[p, 0]
                for i in range(1, N):
                    total = total + iny[p, i]
                mring[p, z, 1] = total

            @pl.when(z != zown)
            def _():
                mring[p, z, 1] = jnp.zeros((8, BLOCK), F32)

            go(group_of(112, [(mring.at[p, z], mring.at[p, z], u_r.at[p], 2 * q + core, c) for q in ring]))

        def sum_x():
            got(inr.at[p, pl.ds(0, N - 1)], r_r.at[p])
            total = inr[p, 0]
            for i in range(1, N):
                total = total + inr[p, i]
            mine = aer_at(c)
            when(c != owner, lambda: got(mine, ar_r.at[p]))
            xr[p, at(c, 32), :] = total + dot(mine[...], lt)
            own = xr.at[p, at(c, 32)]
            go(group_of(480, [(own, own, x_r.at[p], r, i) for i in plane]))
            got(zin.at[p, pl.ds(0, NZ - 1)], z_r.at[p])
            total = zin[p, 0]
            for q in range(1, NZ):
                total = total + zin[p, q]
            mine_c = aec_at(spot)
            when(r != owner, lambda: got(mine_c, ac_r.at[p]))
            xc[p, at(spot, 32), :] = total + dot(mine_c[...], lt)
            own_c = xc.at[p, at(spot, 32)]
            go(group_of(224, [(own_c, own_c, y_r.at[p], 2 * q + core, c) for q in ring]))

        if p == 0:
            cross_rest()
        else:
            sum_m()

        got(tall.at[p, 1, :, other], tm_r.at[p, 1])
        top = tall[p, 1].reshape(BLOCK, BLOCK)
        n_ref[...] = tall[p, 0].reshape(BLOCK, BLOCK) + dot(top, lt, (0, 0))
        aug[...] = n_ref[:128, :]
        strips(aug, None, 0, 2, True)
        if p == 0:
            sum_m()
        else:
            sum_x()
        strips(aug, None, 2, 4, True)
        if p == 0:
            sum_x()

        d0 = aug[:, :128]
        n01 = aug[:, 128:]
        n10d = dot(n_ref[128:, :128], d0)
        aug2[...] = n_ref[128:, 128:] - dot(n_ref[128:, :128], n01)
        def hand_out():
            got(mring.at[p, pl.ds(0, NZ - 1)], u_r.at[p])
            total = mring[p, 0]
            for q in range(1, NZ):
                total = total + mring[p, q]
            ball[p, :, c, core] = total
            own_b = ball.at[p, :, c, core]
            go(group_of(240, [(own_b, own_b, v_r.at[p], r, i) for i in plane]))

        if p > 0:
            hand_out()
        strips(aug2, None, 0, 2, True)
        if p == 0:
            hand_out()
            own_c = aefc.at[at(spot, 32)]
            go(group_of(224, [(own_c, own_c, ag_r.at[0], 2 * q + core, c) for q in ring]))
            own = aefr.at[at(c, 32)]
            go(group_of(480, [(own, own, af_r.at[0], r, i) for i in plane]))
        strips(aug2, None, 2, 4, True)
        part = xc.at[p, at(core, 256)]
        got(xc.at[p, pl.ds(0, 224)], y_r.at[p])
        go(group_of(256, [(part, part, w_r.at[p], mate, c)]))
        e = aug2[...]
        k10 = -dot(e, n10d)
        k_ref[:128, :128] = d0 - dot(n01, k10)
        k_ref[:128, 128:] = -dot(n01, e)
        k_ref[128:, :128] = k10
        k_ref[128:, 128:] = e

        zr[...] = pr[p]
        zc[...] = pc[p]

        @pl.when(r == owner)
        def _():
            zr[off : off + BLOCK, :] = zr[off : off + BLOCK, :] + lt_ref[...]

        @pl.when(c == owner)
        def _():
            zc[off : off + BLOCK, :] = zc[off : off + BLOCK, :] + lt_ref[...]

        got(tall.at[p, 2, :, other], tm_r.at[p, 2])
        got(ball.at[p, :, pl.ds(0, N - 1), core], v_r.at[p])
        final = ball.at[p, :, :, core]
        go(group_of(256, [(final, final, f_r.at[p], mate, c)]))
        got(xr.at[p, pl.ds(0, 480)], x_r.at[p])
        ux[...] = dot3(xr[p], k_ref[...])
        got(xc.at[p, pl.ds(0, 256)], w_r.at[p])
        uy[...] = dot3(xc[p], k_ref[...])
        got(ball.at[p, :, :, other], f_r.at[p])

        ytop = ball[p, 1].reshape(BLOCK, BLOCK)
        xtop = ytop + dot3(tall[p, 2].reshape(BLOCK, BLOCK), lt)
        inner = ball[p, 0].reshape(BLOCK, BLOCK) + dot3(ytop, lt, (0, 0)) + dot3(lt, xtop, (0, 0))
        if p == 0:
            part = aefc.at[at(core, 256)]
            got(aefc.at[pl.ds(0, 224)], ag_r.at[0])
            go(group_of(256, [(part, part, am_r.at[0], mate, c)]))
        coupled = 0.5 * dot3(k_ref[...], dot3(inner, k_ref[...]), (0, 0))
        ur = ux[...] - dot3(zr[...], coupled)
        uc = uy[...] - dot3(zc[...], coupled)
        dest = out_ref if p == PANELS - 1 else cur
        dest[...] = cur[...] - dot3(ur, zc[...], (1, 1)) - dot3(zr[...], uc, (1, 1))
        if p == 0:
            ztop = top + lt
            utop = dot3(xtop, k_ref[...]) - dot3(ztop, coupled)
            rows = lax.broadcasted_iota(jnp.int32, (height, BLOCK), 0)
            got(aefr.at[pl.ds(0, 480)], af_r.at[0])
            near = aefr[...] - dot3(ur, ztop, (1, 1)) - dot3(zr[...], utop, (1, 1))
            pr[1] = jnp.where(r * height + rows >= lead + BLOCK, near, 0.0)
            got(aefc.at[pl.ds(0, 256)], am_r.at[0])
            near = aefc[...] - dot3(uc, ztop, (1, 1)) - dot3(zc[...], utop, (1, 1))
            pc[1] = jnp.where(c * height + rows >= lead + BLOCK, near, 0.0)

        for made in sends + share + cross:
            made.left()
        when(r == 0, g_out.left)
        when(r == 0, down[0].left)
        for made in (down[1], down[2], ae_c, y_own, yswap):
            when(r == owner, made.left)
        when(mate == owner, y_mate.left)
        when((r == owner) & (c == 0), top_out.left)
        when((r == owner) & (c == owner), ee_out.left)
        when(c == owner, ae_r.left)
        if p == 0:
            when(r == 0, root_c.left)
            when(c == 0, root_r.left)
            when(c == 0, root_own.left)
            when(c != 0, ahead_r.left)
            when(relay, ahead_c.left)
            when(core == 0, low_c.left)


def per_device(matrix):
    dma = pltpu.SemaphoreType.DMA

    def buf(*shape):
        return pltpu.VMEM(shape, F32)

    return pl.pallas_call(
        kernel,
        out_shape=jax.ShapeDtypeStruct(matrix.shape, F32),
        in_specs=[VMEM],
        out_specs=VMEM,
        scratch_shapes=[
            buf(512, 512),
            buf(2, 512, 256),
            buf(256, 512),
            buf(2, 512, 256),
            buf(512, 256),
            buf(512, 256),
            buf(32, 256),
            buf(32, 256),
            buf(512, 256),
            buf(512, 256),
            buf(256, 256),
            buf(2, N, 16, 256),
            buf(2, 3, 2, 8, 256),
            buf(2, 3, N, 2, 8, 256),
            buf(256, 256),
            buf(256, 256),
            buf(256, 256),
            buf(128, 256),
            buf(128, 128),
            buf(128, 128),
            buf(512, 256),
            buf(512, 256),
            buf(512, 256),
            buf(512, 256),
            buf(N, 2, 8, 256),
            buf(2, N, 8, 256),
            buf(N, 8, 256),
            buf(N, 2, 8, 256),
            buf(2, N, 8, 256),
            buf(2, N, 32, 256),
            buf(2, N, 8, 256),
            buf(2, N, 8, 256),
            buf(2, 256, 256),
            buf(NZ, 32, 256),
            buf(2, NZ, 32, 256),
            buf(2, 512, 256),
            buf(2, 512, 256),
            buf(2, NZ, 2, 8, 256),
            buf(2, 2, N, 2, 8, 256),
            buf(512, 256),
            buf(512, 256),
            dma((60,)),
            dma((2,)),
            dma((2, 3)),
            dma((2, 3)),
            dma((2, 3)),
            dma((2, 3)),
            dma((1,)),
            dma((1,)),
            dma((1,)),
            dma((1,)),
            dma((1,)),
            dma((2,)),
            dma((2,)),
            dma((1,)),
            dma((1,)),
            dma((1,)),
            dma((2,)),
            dma((2,)),
            dma((2,)),
            dma((2,)),
            dma((2,)),
            dma((2,)),
            dma((2,)),
            dma((2,)),
            dma((2,)),
            dma((2,)),
            dma((2,)),
            dma((2,)),
            dma((2,)),
        ],
        compiler_params=pltpu.CompilerParams(collective_id=0, has_side_effects=True),
        name="reduce_panels",
    )(matrix)


def solution(mesh):
    return jax.shard_map(
        per_device, mesh=mesh, in_specs=(P("row", "col"),), out_specs=P("row", "col"), check_vma=False
    )
```

```python
import jax
import jax.numpy as jnp
from jax import lax
from jax.experimental import pallas as pl
from jax.experimental.pallas import tpu as pltpu
from jax.sharding import PartitionSpec as P

BLOCK = 256
PANELS = 2
N = 16
NZ = 8
HIGH = lax.Precision.HIGHEST
F32 = jnp.float32
MESH = pl.DeviceIdType.MESH
VMEM = pl.BlockSpec(memory_space=pltpu.VMEM)


def dot(left, right, over=(1, 0)):
    return lax.dot_general(
        left,
        right,
        (((over[0],), (over[1],)), ((), ())),
        precision=HIGH,
        preferred_element_type=F32,
    )


def dot3(left, right, over=(1, 0)):
    def split(x):
        high = x.astype(jnp.bfloat16)
        return high, (x - high.astype(F32)).astype(jnp.bfloat16)

    def part(a, b):
        return lax.dot_general(
            a, b, (((over[0],), (over[1],)), ((), ())), preferred_element_type=F32
        )

    lh, ll = split(left)
    rh, rl = split(right)
    return part(lh, rh) + (part(lh, rl) + part(ll, rh))


def recip(x):
    r = pl.reciprocal(x, approx=True)
    return r * (2.0 - x * r)


def lanes(block, index):
    return jnp.take_along_axis(block, jnp.full((8, 128), index, jnp.int32), axis=1)


def times(scale, row):
    if row.shape[1] == 128:
        return scale * row
    return jnp.concatenate([scale * row[:, :128], scale * row[:, 128:]], axis=1)


def put(rows):
    sub = lax.broadcasted_iota(jnp.int32, rows[0].shape, 0)
    out = rows[0]
    for s in range(1, 8):
        out = jnp.where(sub == s, rows[s], out)
    return out


def group(aug, out, base, inverse):
    width = aug.shape[1]
    lane = lax.broadcasted_iota(jnp.int32, (8, 128), 1)
    inside = (lane >= base) & (lane < base + 8)

    def left(block, value):
        if width == 128:
            return jnp.where(inside, value, block)
        return jnp.concatenate([jnp.where(inside, value, block[:, :128]), block[:, 128:]], axis=1)

    rows = [jnp.broadcast_to(aug[pl.ds(base + s, 1), :], (8, width)) for s in range(8)]
    e = [[None] * 8 for _ in range(8)]
    for t in range(8):
        for s in range(8 if inverse else t + 1):
            e[s][t] = lanes(rows[s][:, :128], base + t)
    if inverse:
        rows = [left(rows[s], (lane == base + s).astype(F32)) for s in range(8)]
    inv = []
    for s in range(8):
        inv.append(recip(e[s][s]))
        for t in range(s + 1, 8):
            f = (e[t][s] if inverse else e[s][t]) * inv[s]
            for u in range(s + 1 if inverse else t, 8):
                e[t][u] = e[t][u] - f * e[s][u]
            rows[t] = rows[t] - times(f, rows[s])
    if not inverse:
        out[pl.ds(base, 8), :] = put([times(lax.rsqrt(e[s][s]), rows[s]) for s in range(8)])
    solved = [None] * 8
    for s in reversed(range(8)):
        acc = rows[s]
        for t in range(s + 1, 8):
            acc = acc - times(e[s][t], solved[t])
        solved[s] = times(inv[s], acc)
    own = put(solved)
    strip = pl.multiple_of(base // 32 * 32, 32)
    blocks = [aug[pl.ds(strip + 8 * k, 8), :] for k in range(4)]
    after = [left(b, 0.0) if inverse else b for b in blocks]
    for s in range(8):
        for k in range(4):
            after[k] = after[k] - times(lanes(blocks[k][:, :128], base + s), solved[s])
    for k in range(4):
        aug[pl.ds(strip + 8 * k, 8), :] = jnp.where(strip + 8 * k == base, own, after[k])


def strips(aug, out, lo, hi, inverse):
    row = lax.broadcasted_iota(jnp.int32, (128, 128), 0) // 32
    lane = lax.broadcasted_iota(jnp.int32, (128, 128), 1) // 32

    def one(k, q):
        group(aug, out, pl.multiple_of(32 * q + 8 * k, 8), inverse)
        return q

    def strip(q, carry):
        lax.fori_loop(0, 4, one, q)
        aim = (lane == q) & ((row != q) if inverse else (row > q))
        near = aug[:, :128]
        prod = dot(jnp.where(aim, near, 0.0), aug[...])
        if inverse:
            near = jnp.where(aim, 0.0, near)
        aug[:, :128] = near - prod[:, :128]
        if aug.shape[1] > 128:
            aug[:, 128:] = aug[:, 128:] - prod[:, 128:]
        return carry

    lax.fori_loop(lo, hi, strip, 0)


def remote(src, dst, send, recv, row, col):
    return pltpu.make_async_remote_copy(
        src_ref=src,
        dst_ref=dst,
        send_sem=send,
        recv_sem=recv,
        device_id=(row, col),
        device_id_type=MESH,
    )


def greet(r, c):
    barrier = pltpu.get_barrier_semaphore()
    for k in range(1, N):
        pl.semaphore_signal(barrier, inc=1, device_id=(r, lax.rem(c + k, N)), device_id_type=MESH)
        pl.semaphore_signal(barrier, inc=1, device_id=(lax.rem(r + k, N), c), device_id_type=MESH)
    pl.semaphore_wait(barrier, 2 * (N - 1))


def at(index, size):
    return pl.ds(pl.multiple_of(index * size, size), size)


def kernel(
    a_ref, out_ref,
    cur, pr, pct, pc, aer, aec, aepr, aepc, aefr, aefc, gram, gin, tsrc, tall, lt_ref, k_ref, n_ref, aug, aug2, low,
    zr, zc, wr, wc, m, mpair, mh, ybuf, yin, inr, inm, iny, half, hsum, zin, xr, xc, mring, ball,
    ux, uy,
    ss, g_r, b_r, td_r, t_r, tm_r, pa_r, p_r, qa_r, q_r, ql_r, ar_r, ac_r, af_r, ag_r, am_r,
    r_r, m_r, yt_r, ys_r, h_r, z_r, x_r, y_r, w_r, s_r, u_r, v_r, f_r,
):
    r, c = lax.axis_index("row"), lax.axis_index("col")
    z, core = r // 2, lax.rem(r, 2)
    other = 1 - core
    mate = r + 1 - 2 * core
    height = a_ref.shape[0]
    upper = lax.broadcasted_iota(jnp.int32, (128, 128), 0) <= lax.broadcasted_iota(
        jnp.int32, (128, 128), 1
    )
    steps = [(2, 2), (2, 1), (1, 2), (2, 3), (3, 2), (1, 1), (3, 3), (1, 3), (3, 1), (2, 0), (0, 2)]
    steps += [(1, 0), (0, 1), (3, 0), (0, 3)]
    plane = [lax.rem(c // 4 + dy, 4) * 4 + lax.rem(lax.rem(c, 4) + dx, 4) for dy, dx in steps]
    line = [lax.rem(r + k, N) for k in range(1, N)]
    ring = [lax.rem(z + k, NZ) for k in range(1, NZ)]

    def got(ref, sem):
        remote(ref, ref, ss.at[0], sem, r, c).wait_recv()

    def when(cond, run):
        pl.when(cond)(run)

    cur[...] = a_ref[...]
    zown = 0

    for p in range(PANELS):
        first, lead = p * BLOCK, (p + 1) * BLOCK
        owner, off = lead // height, lead % height
        count = iter(range(1, 60))
        sends = []

        class Group:
            def __init__(self, rows):
                self.sem = ss.at[next(count)]
                self.rows = rows
                self.copies = []

            def add(self, src, dst, sem, row, col):
                self.copies.append(remote(src, dst, self.sem, sem, row, col))
                return self.copies[-1]

            def start(self):
                for copy in self.copies:
                    copy.start()

            def left(self):
                if self.rows <= 512:
                    view = wc.at[pl.ds(0, self.rows)]
                else:
                    view = pr.at[:, pl.ds(0, self.rows // 2)]
                remote(view, view, self.sem, self.sem, r, c).wait_send()

        def group_of(rows, items):
            made = Group(rows)
            for item in items:
                made.add(*item)
            return made

        def go(made):
            made.start()
            sends.append(made)

        def slot(a, i, h):
            return tall.at[p, a, i, h]

        def aer_at(i):
            return aefr.at[at(i, 32)] if p == 0 else aepr

        def aec_at(i):
            return aefc.at[at(i, 32)] if p == 0 else aepc

        spot = core * NZ + z

        if p == 0:

            @pl.when(r == 0)
            def _():
                cols = c * height + lax.broadcasted_iota(jnp.int32, (BLOCK, height), 1)
                pct[...] = jnp.where(cols >= lead, cur[first : first + BLOCK, :], 0.0)
                gram[...] = dot(pct[...], pct[...], (1, 1))
                gin[p, c] = gram[at(c, 16), :]

            @pl.when(c == 0)
            def _():
                rows = r * height + lax.broadcasted_iota(jnp.int32, (height, BLOCK), 0)
                pr[p] = jnp.where(rows >= lead, cur[:, first : first + BLOCK], 0.0)

        else:

            @pl.when(r == 0)
            def _():
                gram[...] = dot(pc[p], pc[p], (0, 0))
                gin[p, c] = gram[at(c, 16), :]

        def row8(i, h):
            return pl.ds(pl.multiple_of(off + 16 * i + 8 * h, 8), 8)

        g_out = group_of(240, [(gram.at[at(i, 16)], gin.at[p, c], g_r.at[p], r, i) for i in plane])
        top_out = group_of(
            240,
            [(pr.at[p, row8(i, h)], tsrc.at[p, 1, h], b_r.at[p, 1], r, i) for i in plane for h in (0, 1)],
        )
        ee_out = group_of(
            240,
            [(aer.at[row8(i, h)], tsrc.at[p, 2, h], b_r.at[p, 2], r, i) for i in plane for h in (0, 1)],
        )
        down = [
            group_of(
                120,
                [
                    (tsrc.at[p, a, lax.rem(i, 2)], slot(a, c, lax.rem(i, 2)), td_r.at[p, a], i, c)
                    for i in line
                ],
            )
            for a in range(3)
        ]
        share = [
            group_of(120, [(slot(a, c, core), slot(a, c, core), t_r.at[p, a], r, i) for i in plane])
            for a in range(3)
        ]
        cross = [
            group_of(128, [(tall.at[p, a, :, core], tall.at[p, a, :, core], tm_r.at[p, a], mate, c)])
            for a in range(3)
        ]
        ae_r = group_of(480, [(aer.at[at(i, 32)], aer_at(i), ar_r.at[p], r, i) for i in plane])
        ae_c = group_of(
            480,
            [
                (aec.at[at(lax.rem(i, 2) * NZ + i // 2, 32)], aec_at(lax.rem(i, 2) * NZ + i // 2), ac_r.at[p], i, c)
                for i in line
            ],
        )
        relay = (core == 0) & (z != 0)
        if p == 0:

            def pr_part(q, sem, i):
                return (pr.at[p, at(q, 32)], pr.at[p, at(q, 32)], sem.at[0], r, i)

            def pc_part(q, sem, row):
                return (pc.at[p, at(q, 64)], pc.at[p, at(q, 64)], sem.at[0], row, c)

            root_r = group_of(480, [pr_part(i, pa_r, i) for i in range(1, N)])
            root_own = group_of(480, [pr_part(0, p_r, i) for i in range(1, N)])
            root_c = group_of(
                896,
                [pc_part(q, qa_r, 2 * q) for q in range(1, NZ)]
                + [pc_part(0, q_r, 2 * q) for q in range(1, NZ)],
            )
            ahead_r = group_of(448, [pr_part(c, p_r, i) for i in plane])
            ahead_c = group_of(384, [pc_part(z, q_r, 2 * q) for q in ring])
            low_c = group_of(512, [(pc.at[p], pc.at[p], ql_r.at[0], r + 1, c)])

        @pl.when(c == owner)
        def _():
            aer[...] = cur[:, off : off + BLOCK]
            mine = aer[at(c, 32), :]
            if p == 0:
                aefr[at(c, 32), :] = mine
            else:
                aepr[...] = mine

        @pl.when(r == owner)
        def _():
            aec[...] = cur[off : off + BLOCK, :].T
            mine = aec[at(spot, 32), :]
            if p == 0:
                aefc[at(spot, 32), :] = mine
            else:
                aepc[...] = mine

        if p == 0:
            greet(r, c)

        when(r == 0, g_out.start)

        @pl.when((r == owner) & (c == 0))
        def _():
            for h in (0, 1):
                tsrc[p, 1, h] = pr[p, row8(c, h), :]

        @pl.when((r == owner) & (c == owner))
        def _():
            for h in (0, 1):
                tsrc[p, 2, h] = aer[row8(c, h), :]

        when((r == owner) & (c == 0), top_out.start)
        when((r == owner) & (c == owner), ee_out.start)
        if p == 0:
            when(c == 0, root_r.start)

        swap = group_of(256, [(wc.at[at(other, 256)], half.at[p], h_r.at[p], mate, c)])
        mswap = group_of(128, [(m.at[:, other], mpair.at[p], s_r.at[p], mate, c)])
        yswap = group_of(128, [(ybuf.at[:, other], yin.at[p], ys_r.at[p], mate, c)])
        y_own = group_of(120, [(ybuf.at[i, core], iny.at[p, c], yt_r.at[p], r, i) for i in plane])
        y_mate = group_of(120, [(yin.at[p, i], iny.at[p, c], yt_r.at[p], r, i) for i in plane])

        def products():
            wc[...] = dot3(cur[...], pr[p], (0, 0))
            go(swap)
            if p == 0:
                when(core == 1, lambda: got(pc.at[p], ql_r.at[0]))
            wr[...] = dot3(cur[...], pc[p])

            @pl.when(r == owner)
            def _():
                ybuf[...] = wr[off : off + BLOCK, :].reshape(N, 2, 8, BLOCK)
                yswap.start()

            m[...] = dot3(pr[p], wr[...], (0, 0)).reshape(N, 2, 8, BLOCK)
            go(mswap)

        def scatter():
            got(mpair.at[p], s_r.at[p])
            mh[...] = m[:, core] + mpair[p]
            go(group_of(120, [(mh.at[i], inm.at[p, c], m_r.at[p], r, i) for i in plane]))
            inm[p, c] = mh[c]

            @pl.when(r == owner)
            def _():
                y_own.start()
                iny[p, c] = ybuf[c, core]

            @pl.when(mate == owner)
            def _():
                got(yin.at[p], ys_r.at[p])
                y_mate.start()
                iny[p, c] = yin[p, c]

            go(group_of(480, [(wr.at[at(i, 32)], inr.at[p, c], r_r.at[p], r, i) for i in plane]))
            inr[p, c] = wr[at(c, 32), :]
            got(half.at[p], h_r.at[p])
            hsum[...] = (wc[at(core, 256), :] + half[p]).reshape(NZ, 32, BLOCK)
            zin[p, z] = hsum[z]
            go(group_of(224, [(hsum.at[q], zin.at[p, z], z_r.at[p], 2 * q + core, c) for q in ring]))

        if p > 0:
            products()

        @pl.when(r == 0)
        def _():
            got(gin.at[p, pl.ds(0, N - 1)], g_r.at[p])
            total = gin[p, 0]
            for i in range(1, N):
                total = total + gin[p, i]
            tsrc[p, 0] = total.reshape(2, 8, BLOCK)
            tall[p, 0, c, core] = tsrc[p, 0, core]
            down[0].start()

        def own_rest():
            @pl.when(r == owner)
            def _():
                for a, holder in ((1, 0), (2, owner)):
                    when(c != holder, lambda a=a: got(tsrc.at[p, a], b_r.at[p, a]))
                    tall[p, a, c, core] = tsrc[p, a, core]
                    down[a].start()

        if p > 0:
            own_rest()
        when(r != 0, lambda: got(slot(0, c, core), td_r.at[p, 0]))
        share[0].start()
        if p == 0:
            own_rest()

        if p == 0:
            @pl.when(r == 0)
            def _():
                pc[p] = pct[...].T
                root_c.start()
                low_c.start()

            @pl.when(relay)
            def _():
                got(pc.at[p, at(z, 64)], qa_r.at[0])
                for q, copy in zip(ring, ahead_c.copies):
                    when(q != 0, copy.start)

        def share_rest():
            for a in (1, 2):
                when(r != owner, lambda a=a: got(slot(a, c, core), td_r.at[p, a]))
                share[a].start()

        if p > 0:
            share_rest()

        def slots(a):
            return tall.at[p, a, pl.ds(0, N - 1), core]

        got(slots(0), t_r.at[p, 0])
        cross[0].start()

        if p == 0:

            when(c == 0, root_own.start)

            @pl.when(c != 0)
            def _():
                got(pr.at[p, at(c, 32)], pa_r.at[0])
                for i, copy in zip(plane, ahead_r.copies):
                    when(i != 0, copy.start)

            share_rest()

        else:
            scatter()
            when(c == owner, ae_r.start)
            when(r == owner, ae_c.start)

        got(tall.at[p, 0, :, other], tm_r.at[p, 0])

        g = tall[p, 0].reshape(BLOCK, BLOCK)
        aug[...] = g[:128, :]
        strips(aug, lt_ref, 0, 4, False)
        lt_ref[:128, :128] = jnp.where(upper, lt_ref[:128, :128], 0.0)
        lt01 = lt_ref[:128, 128:]
        aug2[...] = g[128:, 128:] - dot(lt01, lt01, (0, 0))
        lt_ref[128:, :128] = jnp.zeros((128, 128), F32)

        def cross_rest():
            for a in (1, 2):
                got(slots(a), t_r.at[p, a])
                cross[a].start()

        if p > 0:
            cross_rest()

        if p == 0:

            @pl.when(relay)
            def _():
                got(pc.at[p, pl.ds(0, 448)], q_r.at[0])
                low_c.start()

            @pl.when(c != 0)
            def _():
                got(pr.at[p, pl.ds(0, 480)], p_r.at[0])

            products()
            scatter()
            when(c == owner, ae_r.start)
            when(r == owner, ae_c.start)

        strips(aug2, low, 0, 4, False)
        lt_ref[128:, 128:] = jnp.where(upper, low[...], 0.0)
        lt = lt_ref[...]

        def sum_m():
            got(inm.at[p, pl.ds(0, N - 1)], m_r.at[p])
            total = inm[p, 0]
            for i in range(1, N):
                total = total + inm[p, i]
            mring[p, z, 0] = total

            @pl.when(z == zown)
            def _():
                got(iny.at[p, pl.ds(0, N - 1)], yt_r.at[p])
                total = iny[p, 0]
                for i in range(1, N):
                    total = total + iny[p, i]
                mring[p, z, 1] = total

            @pl.when(z != zown)
            def _():
                mring[p, z, 1] = jnp.zeros((8, BLOCK), F32)

            go(group_of(112, [(mring.at[p, z], mring.at[p, z], u_r.at[p], 2 * q + core, c) for q in ring]))

        def sum_x():
            got(inr.at[p, pl.ds(0, N - 1)], r_r.at[p])
            total = inr[p, 0]
            for i in range(1, N):
                total = total + inr[p, i]
            mine = aer_at(c)
            when(c != owner, lambda: got(mine, ar_r.at[p]))
            xr[p, at(c, 32), :] = total + dot(mine[...], lt)
            own = xr.at[p, at(c, 32)]
            go(group_of(480, [(own, own, x_r.at[p], r, i) for i in plane]))
            got(zin.at[p, pl.ds(0, NZ - 1)], z_r.at[p])
            total = zin[p, 0]
            for q in range(1, NZ):
                total = total + zin[p, q]
            mine_c = aec_at(spot)
            when(r != owner, lambda: got(mine_c, ac_r.at[p]))
            xc[p, at(spot, 32), :] = total + dot(mine_c[...], lt)
            own_c = xc.at[p, at(spot, 32)]
            go(group_of(224, [(own_c, own_c, y_r.at[p], 2 * q + core, c) for q in ring]))

        if p == 0:
            cross_rest()
        else:
            sum_m()

        got(tall.at[p, 1, :, other], tm_r.at[p, 1])
        top = tall[p, 1].reshape(BLOCK, BLOCK)
        n_ref[...] = tall[p, 0].reshape(BLOCK, BLOCK) + dot(top, lt, (0, 0))
        aug[...] = n_ref[:128, :]
        strips(aug, None, 0, 2, True)
        if p == 0:
            sum_m()
        else:
            sum_x()
        strips(aug, None, 2, 4, True)
        if p == 0:
            sum_x()

        d0 = aug[:, :128]
        n01 = aug[:, 128:]
        n10d = dot(n_ref[128:, :128], d0)
        aug2[...] = n_ref[128:, 128:] - dot(n_ref[128:, :128], n01)
        def hand_out():
            got(mring.at[p, pl.ds(0, NZ - 1)], u_r.at[p])
            total = mring[p, 0]
            for q in range(1, NZ):
                total = total + mring[p, q]
            ball[p, :, c, core] = total
            own_b = ball.at[p, :, c, core]
            go(group_of(240, [(own_b, own_b, v_r.at[p], r, i) for i in plane]))

        if p > 0:
            hand_out()
        strips(aug2, None, 0, 2, True)
        if p == 0:
            hand_out()
            own_c = aefc.at[at(spot, 32)]
            go(group_of(224, [(own_c, own_c, ag_r.at[0], 2 * q + core, c) for q in ring]))
            own = aefr.at[at(c, 32)]
            go(group_of(480, [(own, own, af_r.at[0], r, i) for i in plane]))
        strips(aug2, None, 2, 4, True)
        part = xc.at[p, at(core, 256)]
        got(xc.at[p, pl.ds(0, 224)], y_r.at[p])
        go(group_of(256, [(part, part, w_r.at[p], mate, c)]))
        e = aug2[...]
        k10 = -dot(e, n10d)
        k_ref[:128, :128] = d0 - dot(n01, k10)
        k_ref[:128, 128:] = -dot(n01, e)
        k_ref[128:, :128] = k10
        k_ref[128:, 128:] = e

        zr[...] = pr[p]
        zc[...] = pc[p]

        @pl.when(r == owner)
        def _():
            zr[off : off + BLOCK, :] = zr[off : off + BLOCK, :] + lt_ref[...]

        @pl.when(c == owner)
        def _():
            zc[off : off + BLOCK, :] = zc[off : off + BLOCK, :] + lt_ref[...]

        got(tall.at[p, 2, :, other], tm_r.at[p, 2])
        got(ball.at[p, :, pl.ds(0, N - 1), core], v_r.at[p])
        final = ball.at[p, :, :, core]
        go(group_of(256, [(final, final, f_r.at[p], mate, c)]))
        got(xr.at[p, pl.ds(0, 480)], x_r.at[p])
        ux[...] = dot3(xr[p], k_ref[...])
        got(xc.at[p, pl.ds(0, 256)], w_r.at[p])
        uy[...] = dot3(xc[p], k_ref[...])
        got(ball.at[p, :, :, other], f_r.at[p])

        ytop = ball[p, 1].reshape(BLOCK, BLOCK)
        xtop = ytop + dot3(tall[p, 2].reshape(BLOCK, BLOCK), lt)
        inner = ball[p, 0].reshape(BLOCK, BLOCK) + dot3(ytop, lt, (0, 0)) + dot3(lt, xtop, (0, 0))
        if p == 0:
            part = aefc.at[at(core, 256)]
            got(aefc.at[pl.ds(0, 224)], ag_r.at[0])
            go(group_of(256, [(part, part, am_r.at[0], mate, c)]))
        coupled = 0.5 * dot3(k_ref[...], dot3(inner, k_ref[...]), (0, 0))
        ur = ux[...] - dot3(zr[...], coupled)
        uc = uy[...] - dot3(zc[...], coupled)
        dest = out_ref if p == PANELS - 1 else cur
        dest[...] = cur[...] - dot3(ur, zc[...], (1, 1)) - dot3(zr[...], uc, (1, 1))
        if p == 0:
            ztop = top + lt
            utop = dot3(xtop, k_ref[...]) - dot3(ztop, coupled)
            rows = lax.broadcasted_iota(jnp.int32, (height, BLOCK), 0)
            got(aefr.at[pl.ds(0, 480)], af_r.at[0])
            near = aefr[...] - dot3(ur, ztop, (1, 1)) - dot3(zr[...], utop, (1, 1))
            pr[1] = jnp.where(r * height + rows >= lead + BLOCK, near, 0.0)
            got(aefc.at[pl.ds(0, 256)], am_r.at[0])
            near = aefc[...] - dot3(uc, ztop, (1, 1)) - dot3(zc[...], utop, (1, 1))
            pc[1] = jnp.where(c * height + rows >= lead + BLOCK, near, 0.0)

        for made in sends + share + cross:
            made.left()
        when(r == 0, g_out.left)
        when(r == 0, down[0].left)
        for made in (down[1], down[2], ae_c, y_own, yswap):
            when(r == owner, made.left)
        when(mate == owner, y_mate.left)
        when((r == owner) & (c == 0), top_out.left)
        when((r == owner) & (c == owner), ee_out.left)
        when(c == owner, ae_r.left)
        if p == 0:
            when(r == 0, root_c.left)
            when(c == 0, root_r.left)
            when(c == 0, root_own.left)
            when(c != 0, ahead_r.left)
            when(relay, ahead_c.left)
            when(core == 0, low_c.left)


def per_device(matrix):
    dma = pltpu.SemaphoreType.DMA

    def buf(*shape):
        return pltpu.VMEM(shape, F32)

    return pl.pallas_call(
        kernel,
        out_shape=jax.ShapeDtypeStruct(matrix.shape, F32),
        in_specs=[VMEM],
        out_specs=VMEM,
        scratch_shapes=[
            buf(512, 512),
            buf(2, 512, 256),
            buf(256, 512),
            buf(2, 512, 256),
            buf(512, 256),
            buf(512, 256),
            buf(32, 256),
            buf(32, 256),
            buf(512, 256),
            buf(512, 256),
            buf(256, 256),
            buf(2, N, 16, 256),
            buf(2, 3, 2, 8, 256),
            buf(2, 3, N, 2, 8, 256),
            buf(256, 256),
            buf(256, 256),
            buf(256, 256),
            buf(128, 256),
            buf(128, 128),
            buf(128, 128),
            buf(512, 256),
            buf(512, 256),
            buf(512, 256),
            buf(512, 256),
            buf(N, 2, 8, 256),
            buf(2, N, 8, 256),
            buf(N, 8, 256),
            buf(N, 2, 8, 256),
            buf(2, N, 8, 256),
            buf(2, N, 32, 256),
            buf(2, N, 8, 256),
            buf(2, N, 8, 256),
            buf(2, 256, 256),
            buf(NZ, 32, 256),
            buf(2, NZ, 32, 256),
            buf(2, 512, 256),
            buf(2, 512, 256),
            buf(2, NZ, 2, 8, 256),
            buf(2, 2, N, 2, 8, 256),
            buf(512, 256),
            buf(512, 256),
            dma((60,)),
            dma((2,)),
            dma((2, 3)),
            dma((2, 3)),
            dma((2, 3)),
            dma((2, 3)),
            dma((1,)),
            dma((1,)),
            dma((1,)),
            dma((1,)),
            dma((1,)),
            dma((2,)),
            dma((2,)),
            dma((1,)),
            dma((1,)),
            dma((1,)),
            dma((2,)),
            dma((2,)),
            dma((2,)),
            dma((2,)),
            dma((2,)),
            dma((2,)),
            dma((2,)),
            dma((2,)),
            dma((2,)),
            dma((2,)),
            dma((2,)),
            dma((2,)),
            dma((2,)),
        ],
        compiler_params=pltpu.CompilerParams(collective_id=0, has_side_effects=True),
        name="reduce_panels",
    )(matrix)


def solution(mesh):
    return jax.shard_map(
        per_device, mesh=mesh, in_specs=(P("row", "col"),), out_specs=P("row", "col"), check_vma=False
    )
```
